256 devices in a mesh: seq: 64 (over x, z, y_hi), dp: 4 (over y_lo, core).
Axes of the slice: x: 4, y: 4 (y_hi: 2, y_lo: 2; y = y_hi * 2 + y_lo), z: 8, core: 2. Of those that a mesh axis runs over, the one named last changes fastest.
Arguments:
- layer_input: bfloat16 [32768, 2560], P(('dp', 'seq')), may hold values from -24 to 24
- ssm_input: bfloat16 [32768, 2560], P(('dp', 'seq')), may hold values from -6 to 6
- out_grad: bfloat16 [32768, 2560], P(('dp', 'seq')), may hold values from -6 to 6
- b_weight: bfloat16 [2560, 128], replicated, may hold values from -0.125 to 0.125
- c_weight: bfloat16 [2560, 128], replicated, may hold values from -0.125 to 0.125
- dt_weight: bfloat16 [2560, 40], replicated, may hold values from -0.25 to 0.25
- dt_bias: float32 [40], replicated, may hold values from -9.7 to -8.2
- a_log: float32 [40], replicated, may hold values from -13 to 4.7
- d_skip: float32 [40], replicated, may hold values from 0.5 to 1.5
Outputs:
- grad_ssm_input: bfloat16 [32768, 2560], P(('dp', 'seq'))
- grad_layer_input: bfloat16 [32768, 2560], P(('dp', 'seq'))
- grad_b_weight: float32 [2560, 128], P('seq')
- grad_c_weight: float32 [2560, 128], P('seq')
- grad_dt_weight: float32 [2560, 40], P('seq')
- grad_dt_bias: float32 [40], replicated
- grad_a_log: float32 [40], replicated
- grad_d_skip: float32 [40], replicated
The draws below stay inside these ranges and needn't reach their ends.
All inputs are finite; a program needn't handle non-finite values.
Results may differ from the reference program's by a relative error of at most 0.0018.
Values sent between devices are 32-bit elements; how exact they have to be, the bound alone decides.
A program may use at most 256 MiB of HBM per device.

```python
import jax
import jax.numpy as jnp
from jax import lax

D_MODEL = 2560
STATE = 128
HEADS = 40
HEAD_DIM = 64
TOK_DEV = 128
SEQLEN = 8192
TOKENS = 32768
N_DP = 4


def decay_setup(key):
    folded = jax.random.fold_in(key, 7)
    streams = jax.random.split(folded, 4)
    portion = 0.5
    retains = jax.random.uniform(streams[0], (HEADS,)) < portion
    slow_rate = jnp.exp(jax.random.uniform(streams[1], (HEADS,), minval=jnp.log(0.3), maxval=jnp.log(2.0))) / SEQLEN
    fast_rate = jnp.exp(jax.random.uniform(streams[2], (HEADS,), minval=jnp.log(1.0 / 50), maxval=jnp.log(1.0 / 20)))
    wanted = jnp.where(retains, slow_rate, fast_rate)
    typical = 0.001 * jnp.exp(jax.random.uniform(streams[3], (HEADS,), minval=-0.7, maxval=0.7))
    return (jnp.log(typical) - 2.0, jnp.log(wanted / typical))


def draw_dt_bias(key, part):
    return decay_setup(key)[0].astype(jnp.float32)


def draw_a_log(key, part):
    return decay_setup(key)[1].astype(jnp.float32)


def raised(values, key, source, target, shards_of, factor):
    def block_of(axis_at):
        return (jnp.arange(values.shape[axis_at]) // (values.shape[axis_at] // shards_of)).reshape((-1,) + (1,) * (values.ndim - 1 - axis_at))

    first = jax.random.permutation(key, shards_of)[block_of(target)]
    other_side = (block_of(target) + shards_of // 2) % shards_of
    return jnp.where((block_of(source) == first) | (block_of(source) == other_side), factor * values, values)


def block_scale(rng, dims, cuts, low, largest):
    def one(dim, blocks):
        heights = jax.random.uniform(jax.random.fold_in(jax.random.fold_in(rng, 6), dim), (blocks,), jnp.float32, low / len(cuts), largest / len(cuts))
        return jnp.repeat(jnp.exp(heights), dims[dim] // blocks).reshape((-1,) + (1,) * (len(dims) - dim - 1))

    factor_of = one(*cuts[0])
    for cut in cuts[1:]:
        factor_of = factor_of * one(*cut)
    return factor_of


def centred(stream_key, dims, width, bound, cuts=(), held_as=jnp.bfloat16):
    entries = width * jax.random.normal(stream_key, dims, jnp.float32)
    if cuts:
        entries = entries * block_scale(stream_key, dims, cuts, -0.22, 0.18)
    return jnp.clip(entries, -bound, bound).astype(held_as)


def bell_draw_with(own_key, shape, scale, bound, cuts, heavy, kind=jnp.bfloat16):
    drawn = scale * jax.random.normal(own_key, shape, jnp.float32)
    if cuts:
        drawn = drawn * block_scale(own_key, shape, cuts, -0.22, 0.18)
    return jnp.clip(raised(drawn, jax.random.fold_in(own_key, 3), *heavy), -bound, bound).astype(kind)


def setup_inputs(seed: int = 0) -> dict:
    key_of = jax.random.split(jax.random.key(seed), 10)
    layer_input = bell_draw_with(key_of[0], (TOKENS, D_MODEL), 1.0, 24.0, ((0, 256),), (0, 1, 256, 6.0))
    ssm_input = centred(key_of[1], (TOKENS, HEADS * HEAD_DIM), 1.0, 6.0, ((0, 256),))
    out_grad = centred(key_of[2], (TOKENS, HEADS * HEAD_DIM), 1.0, 6.0, ((0, 256),))
    b_weight = centred(key_of[3], (D_MODEL, STATE), D_MODEL ** -0.5, 0.125)
    c_weight = centred(key_of[4], (D_MODEL, STATE), D_MODEL ** -0.5, 0.125)
    dt_weight = centred(key_of[5], (D_MODEL, HEADS), (D_MODEL // 4) ** -0.5, 0.25)
    dt_bias = draw_dt_bias(jax.random.fold_in(key_of[9], 71), 0)
    a_log = draw_a_log(jax.random.fold_in(key_of[9], 71), 0)
    d_skip = jnp.clip(jax.random.uniform(key_of[8], (HEADS,), jnp.float32, 0.5, 1.5), 0.5, 1.5)
    return {"layer_input": layer_input, "ssm_input": ssm_input, "out_grad": out_grad, "b_weight": b_weight, "c_weight": c_weight, "dt_weight": dt_weight, "dt_bias": dt_bias, "a_log": a_log, "d_skip": d_skip}


EXACT = lax.Precision.HIGHEST

def block_step(carried, pieces, decay_rate, d_skip):
    proj_b, proj_c, dt_values, inputs = pieces
    length = dt_values.shape[0]
    log_decay = dt_values * decay_rate[None, :]
    cumulative = jnp.cumsum(log_decay, axis=0)
    row_index = lax.broadcasted_iota(jnp.int32, (length, length), 0)
    col_index = lax.broadcasted_iota(jnp.int32, (length, length), 1)
    causal = row_index >= col_index
    spread = cumulative.T[:, :, None] - cumulative.T[:, None, :]
    decay_table = jnp.exp(jnp.where(causal[None], spread, -1e+30))
    scores = jnp.dot(proj_c, proj_b.T, precision=EXACT)
    inner = jnp.einsum('hts,ts,sh,shp->thp', decay_table, scores, dt_values, inputs, precision=EXACT)
    outer = jnp.exp(cumulative)[:, :, None] * jnp.einsum('hpn,tn->thp', carried, proj_c, precision=EXACT)
    block_out = inner + outer + d_skip[None, :, None] * inputs
    block_decay = cumulative[-1]
    weights = jnp.exp(block_decay[None, :] - cumulative) * dt_values
    next_state = jnp.exp(block_decay)[:, None, None] * carried + jnp.einsum('sh,shp,sn->hpn', weights, inputs, proj_b, precision=EXACT)
    return (next_state, block_out)

def replica_forward(u_wide, x_wide, b_wide, c_wide, dt_wide, dt_bias, a_log, d_skip):
    proj_b = jnp.dot(u_wide, b_wide, precision=EXACT)
    proj_c = jnp.dot(u_wide, c_wide, precision=EXACT)
    dt_values = jax.nn.softplus(jnp.dot(u_wide, dt_wide, precision=EXACT) + dt_bias[None, :])
    decay_rate = -jnp.exp(a_log)
    block_count = SEQLEN // TOK_DEV
    pieces = (proj_b.reshape(block_count, TOK_DEV, STATE), proj_c.reshape(block_count, TOK_DEV, STATE), dt_values.reshape(block_count, TOK_DEV, HEADS), x_wide.reshape(block_count, TOK_DEV, HEADS, HEAD_DIM))
    zero_state = jnp.zeros((HEADS, HEAD_DIM, STATE), jnp.float32)

    def advance(carried, block_pieces):
        return block_step(carried, block_pieces, decay_rate, d_skip)
    final_state, outputs = lax.scan(advance, zero_state, pieces)
    return outputs.reshape(SEQLEN, HEADS * HEAD_DIM)

def reference(layer_input, ssm_input, out_grad, b_weight, c_weight, dt_weight, dt_bias, a_log, d_skip):
    b_wide = b_weight.astype(jnp.float32)
    c_wide = c_weight.astype(jnp.float32)
    dt_wide = dt_weight.astype(jnp.float32)
    u_all = layer_input.reshape(N_DP, SEQLEN, D_MODEL)
    x_all = ssm_input.reshape(N_DP, SEQLEN, HEADS * HEAD_DIM)
    g_all = out_grad.reshape(N_DP, SEQLEN, HEADS * HEAD_DIM)

    def replica_grads(replica):
        u_rows, x_rows, g_rows = replica
        primal, pullback = jax.vjp(replica_forward, u_rows.astype(jnp.float32), x_rows.astype(jnp.float32), b_wide, c_wide, dt_wide, dt_bias, a_log, d_skip)
        return pullback(g_rows.astype(jnp.float32))
    results = lax.map(replica_grads, (u_all, x_all, g_all))
    grad_u = results[0].reshape(TOKENS, D_MODEL).astype(jnp.bfloat16)
    grad_x = results[1].reshape(TOKENS, HEADS * HEAD_DIM).astype(jnp.bfloat16)
    return (grad_x, grad_u, lax.optimization_barrier(jnp.sum(results[2], axis=0)), lax.optimization_barrier(jnp.sum(results[3], axis=0)), lax.optimization_barrier(jnp.sum(results[4], axis=0)), lax.optimization_barrier(jnp.sum(results[5], axis=0)), lax.optimization_barrier(jnp.sum(results[6], axis=0)), lax.optimization_barrier(jnp.sum(results[7], axis=0)))
```

```python
import jax
import jax.numpy as jnp
from jax import lax
from jax.experimental import pallas as pl
from jax.experimental.pallas import tpu as pltpu
from jax.sharding import Mesh
from jax.sharding import PartitionSpec as P

SEQ = ("x", "z", "yh")
DP_SEQ = ("yl", "core", "x", "z", "yh")
EXACT = lax.Precision.HIGHEST

AXES = ("x", "z", "yh", "yl", "core")
SIZES = {"x": 4, "z": 8, "yh": 2, "yl": 2, "core": 2}
MESH = pl.DeviceIdType.MESH
HEADS, WIDTH, STATE = 40, 64, 128
HALF = HEADS // 2
CHUNK = 4
CHUNKS = HALF // CHUNK
NX, NZ = SIZES["x"], SIZES["z"]
PIECE = WIDTH // NZ


def place():
    return {axis: lax.axis_index(axis) for axis in AXES}


def shifted(here, **steps):
    there = dict(here)
    for axis, step in steps.items():
        there[axis] = lax.rem(here[axis] + step, SIZES[axis])
    return tuple(there[axis] for axis in AXES)


def greet(peers):
    barrier = pltpu.get_barrier_semaphore()
    for peer in peers:
        pl.semaphore_signal(barrier, inc=1, device_id=peer, device_id_type=MESH)
    pl.semaphore_wait(barrier, len(peers))


def push(src, dst, send, recv, peer):
    return pltpu.make_async_remote_copy(
        src_ref=src, dst_ref=dst, send_sem=send, recv_sem=recv, device_id=peer, device_id_type=MESH
    )


def scan_kernel(
    sr, dec, out, par, pq, arec, xs, xr, bs, ps, ys, dpar, coef, pair, zd, rd,
    y1s, y1r, as_, ar_, xss, xrs, bss, brs, y2s, y2r, d1s, d1r, d2s, d2r, d3s, d3r,
):
    here = place()
    x, z, h = here["x"], here["z"], here["yh"]
    low = h == 0
    mine, other = h * HALF, (1 - h) * HALF
    partner = shifted(here, yh=1)
    zpeers = [shifted(here, z=d) for d in range(1, NZ)]
    xpeers = [shifted(here, x=d) for d in range(1, NX)]
    greet([partner] + zpeers + xpeers)

    first = push(dec.at[1 - h], dpar, d1s, d1r, partner)
    first.start()
    y1 = [
        push(
            sr.at[:, pl.ds(other + c * CHUNK, CHUNK)],
            par.at[:, pl.ds(c * CHUNK, CHUNK)],
            y1s.at[c], y1r.at[c], partner,
        )
        for c in range(CHUNKS)
    ]
    y1[0].start()
    y1[1].start()
    xr[x] = jnp.zeros((HALF, PIECE, STATE), jnp.float32)
    first.wait()
    own_decay = dec[h]
    par_decay = dpar[...]
    one = jnp.ones_like(own_decay)
    coef[0] = jnp.where(low, par_decay, one)
    coef[1] = jnp.where(low, one, own_decay)
    coef[2] = jnp.where(low, one, par_decay)
    coef[3] = jnp.where(low, own_decay, one)
    pair[...] = own_decay * par_decay
    zd[z] = own_decay * par_decay
    second = [
        push(pair, zd.at[z], d2s.at[d], d2r.at[d], peer) for d, peer in enumerate(zpeers)
    ]
    for copy in second:
        copy.start()
    for copy in second:
        copy.wait()
    row = zd[0]
    for k in range(1, NZ):
        row = row * zd[k]
    rd[x] = row
    third = [push(rd.at[x], rd.at[x], d3s.at[d], d3r.at[d], peer) for d, peer in enumerate(xpeers)]
    for copy in third:
        copy.start()

    def a_copies(c):
        heads = pl.ds(c * CHUNK, CHUNK)
        copies = []
        for d, peer in enumerate(zpeers):
            pz = pl.multiple_of(lax.rem(z + d + 1, NZ) * PIECE, PIECE)
            copies.append(
                push(pq.at[:, heads, pl.ds(pz, PIECE)], arec.at[z, :, heads], as_.at[c, d], ar_.at[c, d], peer)
            )
        return copies

    def x_copies(c):
        heads = pl.ds(c * CHUNK, CHUNK)
        copies = []
        for d, peer in enumerate(xpeers):
            px = lax.rem(x + d + 1, NX)
            back = jnp.where(px > x, 0, 1)
            copies.append(push(xs.at[back, heads], xr.at[x, heads], xss.at[c, d], xrs.at[c, d], peer))
        return copies

    def b_copies(c):
        heads = pl.ds(c * CHUNK, CHUNK)
        here_rows = pl.ds(pl.multiple_of(z * PIECE, PIECE), PIECE)
        copies = []
        for d, peer in enumerate(zpeers):
            pz = lax.rem(z + d + 1, NZ)
            copies.append(
                push(bs.at[pz, :, heads], ps.at[:, heads, here_rows], bss.at[c, d], brs.at[c, d], peer)
            )
        return copies

    def y2_copy(c):
        return push(
            ys.at[:, pl.ds(c * CHUNK, CHUNK)],
            out.at[:, pl.ds(mine + c * CHUNK, CHUNK)],
            y2s.at[c], y2r.at[c], partner,
        )

    def pairs(c):
        y1[c].wait_recv()
        if c + 2 < CHUNKS:
            y1[c + 2].start()

        def head(i, carry):
            k = c * CHUNK + i
            at = pl.ds(k, 1)
            pq[0, k] = coef[0, at, :] * sr[0, mine + k] + coef[1, at, :] * par[0, k]
            pq[1, k] = coef[2, at, :] * sr[1, mine + k] + coef[3, at, :] * par[1, k]
            return carry

        lax.fori_loop(0, CHUNK, head, 0)
        heads = pl.ds(c * CHUNK, CHUNK)
        own = pl.ds(pl.multiple_of(z * PIECE, PIECE), PIECE)
        arec[z, :, heads] = pq[:, heads, own, :]
        for copy in a_copies(c):
            copy.start()

    def totals(c):
        for copy in a_copies(c):
            copy.wait_recv()

        def head(i, carry):
            k = c * CHUNK + i
            at = pl.ds(k, 1)
            forward = arec[0, 0, k]
            backward = arec[NZ - 1, 1, k]
            for j in range(1, NZ):
                forward = zd[j, at, :] * forward + arec[j, 0, k]
                backward = zd[NZ - 1 - j, at, :] * backward + arec[NZ - 1 - j, 1, k]
            xs[0, k] = forward
            xs[1, k] = backward
            return carry

        lax.fori_loop(0, CHUNK, head, 0)
        for copy in x_copies(c):
            copy.start()

    def prefixes(c):
        if c == 0:
            for copy in third:
                copy.wait()
        for copy in x_copies(c):
            copy.wait_recv()

        def head(i, carry):
            k = c * CHUNK + i
            at = pl.ds(k, 1)
            forward = jnp.zeros((PIECE, STATE), jnp.float32)
            backward = jnp.zeros((PIECE, STATE), jnp.float32)
            for j in range(NX):
                forward = jnp.where(j < x, rd[j, at, :] * forward + xr[j, k], forward)
                m = NX - 1 - j
                backward = jnp.where(m > x, rd[m, at, :] * backward + xr[m, k], backward)
            for j in range(NZ):
                bs[j, 0, k] = forward
                forward = zd[j, at, :] * forward + arec[j, 0, k]
                m = NZ - 1 - j
                bs[m, 1, k] = backward
                backward = zd[m, at, :] * backward + arec[m, 1, k]
            return carry

        lax.fori_loop(0, CHUNK, head, 0)
        heads = pl.ds(c * CHUNK, CHUNK)
        own = pl.ds(pl.multiple_of(z * PIECE, PIECE), PIECE)
        ps[:, heads, own, :] = bs[z, :, heads]
        for copy in b_copies(c):
            copy.start()

    def finals(c):
        for copy in b_copies(c):
            copy.wait_recv()

        def head(i, carry):
            k = c * CHUNK + i
            at = pl.ds(k, 1)
            before, after = ps[0, k], ps[1, k]
            zero = jnp.zeros_like(before)
            ys[0, k] = coef[3, at, :] * before + jnp.where(low, sr[0, mine + k], zero)
            ys[1, k] = coef[1, at, :] * after + jnp.where(low, zero, sr[1, mine + k])
            out[0, mine + k] = coef[2, at, :] * before + jnp.where(low, zero, par[0, k])
            out[1, mine + k] = coef[0, at, :] * after + jnp.where(low, par[1, k], zero)
            return carry

        lax.fori_loop(0, CHUNK, head, 0)
        y2_copy(c).start()

    for step in range(CHUNKS + 3):
        if step < CHUNKS:
            pairs(step)
        if 0 <= step - 1 < CHUNKS:
            totals(step - 1)
        if 0 <= step - 2 < CHUNKS:
            prefixes(step - 2)
        if 0 <= step - 3 < CHUNKS:
            finals(step - 3)
    for c in range(CHUNKS):
        y2_copy(c).wait_recv()
    for c in range(CHUNKS):
        y1[c].wait_send()
        for copy in a_copies(c) + x_copies(c) + b_copies(c):
            copy.wait_send()
        y2_copy(c).wait_send()


def scan_states(states, decay):
    vmem = pl.BlockSpec(memory_space=pltpu.VMEM)
    f32 = jnp.float32
    dma = pltpu.SemaphoreType.DMA
    half = (2, HALF, WIDTH, STATE)
    return pl.pallas_call(
        scan_kernel,
        out_shape=jax.ShapeDtypeStruct(states.shape, f32),
        in_specs=[vmem, vmem],
        out_specs=vmem,
        scratch_shapes=[
            pltpu.VMEM(half, f32),
            pltpu.VMEM(half, f32),
            pltpu.VMEM((NZ, 2, HALF, PIECE, STATE), f32),
            pltpu.VMEM((2, HALF, PIECE, STATE), f32),
            pltpu.VMEM((NX, HALF, PIECE, STATE), f32),
            pltpu.VMEM((NZ, 2, HALF, PIECE, STATE), f32),
            pltpu.VMEM(half, f32),
            pltpu.VMEM(half, f32),
            pltpu.VMEM((24, STATE), f32),
            pltpu.VMEM((4, 24, STATE), f32),
            pltpu.VMEM((24, STATE), f32),
            pltpu.VMEM((NZ, 24, STATE), f32),
            pltpu.VMEM((NX, 24, STATE), f32),
            dma((CHUNKS,)), dma((CHUNKS,)),
            dma((CHUNKS, NZ - 1)), dma((CHUNKS, NZ - 1)),
            dma((CHUNKS, NX - 1)), dma((CHUNKS, NX - 1)),
            dma((CHUNKS, NZ - 1)), dma((CHUNKS, NZ - 1)),
            dma((CHUNKS,)), dma((CHUNKS,)),
            dma, dma,
            dma((NZ - 1,)), dma((NZ - 1,)),
            dma((NX - 1,)), dma((NX - 1,)),
        ],
        compiler_params=pltpu.CompilerParams(
            collective_id=0, has_side_effects=True, vmem_limit_bytes=48 << 20
        ),
        name="scan_states",
    )(states, decay)


ROWS = 96
OWNERS = (NX, NZ, 2)


def reduce_kernel(g, out, c_rec, h1, a0, a1, a1r, a2, a2r, b0, b1, b1r, b2, b2r, c0, c1, c1r, c2, c2r, *sems):
    here = place()
    x, z, h, yl, core = (here[a] for a in AXES)
    y = h * 2 + yl
    cpeer = shifted(here, core=1)
    lpeer = shifted(here, yl=1)
    zpeers = [shifted(here, z=d) for d in range(1, NZ)]
    xpeers = [shifted(here, x=d) for d in range(1, NX)]
    ynext = [lax.rem(y + d, 4) for d in range(1, 4)]
    ypeers = [(x, z, t // 2, lax.rem(t, 2), core) for t in ynext]
    greet([cpeer] + zpeers + xpeers + ypeers)
    cs, cr, x0s, x0r, y0s, y0r, z0s, z0r, y1s, y1r, z1s, z1r, x1s, x1r, z2s, z2r, x2s, x2r, y2s, y2r, ls, lr, ks, kr = sems
    keep = pl.multiple_of(core * 48, 8)
    give = pl.multiple_of((1 - core) * 48, 8)
    swap = push(g.at[:, :, :, pl.ds(give, 48)], c_rec, cs, cr, cpeer)
    swap.start()
    swap.wait()
    h1[...] = g[:, :, :, pl.ds(keep, 48), :] + c_rec[...]

    def rows(start, there):
        return pl.ds(pl.multiple_of(start + 8 * lax.rem(there, 2), 8), 8)

    def start(copies):
        for copy in copies:
            copy.start()
        return copies

    def arrived(copies):
        for copy in copies:
            copy.wait_recv()

    zs = [lax.rem(z + d, NZ) for d in range(1, NZ)]
    xs = [lax.rem(x + d, NX) for d in range(1, NX)]
    z_one = start([push(h1.at[:, t, :, pl.ds(32, 16)], c0.at[z], z0s.at[d], z0r.at[d], zpeers[d]) for d, t in enumerate(zs)])
    x_one = start([push(h1.at[t, :, :, pl.ds(0, 16)], a0.at[x], x0s.at[d], x0r.at[d], xpeers[d]) for d, t in enumerate(xs)])
    y_one = start([push(h1.at[:, :, t // 2, rows(16, t)], b0.at[y], y0s.at[d], y0r.at[d], ypeers[d]) for d, t in enumerate(ynext)])
    arrived(x_one)
    total = h1[x, :, :, pl.ds(0, 16), :]
    for t in xs:
        total = total + a0[t]
    a1[...] = total
    y_two = start([push(a1.at[:, t // 2, rows(0, t)], a1r.at[y], y1s.at[d], y1r.at[d], ypeers[d]) for d, t in enumerate(ynext)])
    arrived(y_one)
    total = h1[:, :, h, rows(16, yl), :]
    for t in ynext:
        total = total + b0[t]
    b1[...] = total
    z_two = start([push(b1.at[:, t], b1r.at[z], z1s.at[d], z1r.at[d], zpeers[d]) for d, t in enumerate(zs)])
    arrived(z_one)
    total = h1[:, z, :, pl.ds(32, 16), :]
    for t in zs:
        total = total + c0[t]
    c1[...] = total
    x_two = start([push(c1.at[t], c1r.at[x], x1s.at[d], x1r.at[d], xpeers[d]) for d, t in enumerate(xs)])
    arrived(y_two)
    total = a1[:, h, rows(0, yl), :]
    for t in ynext:
        total = total + a1r[t]
    a2[...] = total
    z_three = start([push(a2.at[t], a2r.at[z], z2s.at[d], z2r.at[d], zpeers[d]) for d, t in enumerate(zs)])
    arrived(z_two)
    total = b1[:, z]
    for t in zs:
        total = total + b1r[t]
    b2[...] = total
    x_three = start([push(b2.at[t], b2r.at[x], x2s.at[d], x2r.at[d], xpeers[d]) for d, t in enumerate(xs)])
    arrived(x_two)
    total = c1[x]
    for t in xs:
        total = total + c1r[t]
    c2[...] = total
    y_three = start([push(c2.at[t // 2, rows(0, t)], c2r.at[y], y2s.at[d], y2r.at[d], ypeers[d]) for d, t in enumerate(ynext)])
    arrived(z_three)
    total = a2[z]
    for t in zs:
        total = total + a2r[t]
    out[core, 0, yl] = total
    arrived(x_three)
    total = b2[x]
    for t in xs:
        total = total + b2r[t]
    out[core, 1, yl] = total
    arrived(y_three)
    total = c2[h, rows(0, yl), :]
    for t in ynext:
        total = total + c2r[t]
    out[core, 2, yl] = total
    last = push(out.at[core, :, yl], out.at[core, :, yl], ls, lr, lpeer)
    last.start()
    last.wait()
    both = push(out.at[core], out.at[core], ks, kr, cpeer)
    both.start()
    both.wait()
    for copy in x_one + y_one + z_one + x_two + y_two + z_two + x_three + y_three + z_three:
        copy.wait_send()


def reduce_grads(blocks):
    vmem = pl.BlockSpec(memory_space=pltpu.VMEM)
    dma = pltpu.SemaphoreType.DMA

    def f32(*shape):
        return pltpu.VMEM(shape + (128,), jnp.float32)

    pairs = []
    for n in (1, 3, 3, 7, 3, 7, 3, 7, 3, 3, 1, 1):
        pairs += [dma if n == 1 else dma((n,))] * 2
    return pl.pallas_call(
        reduce_kernel,
        out_shape=jax.ShapeDtypeStruct((2, 3, 2, 8, 128), jnp.float32),
        in_specs=[vmem],
        out_specs=vmem,
        scratch_shapes=[
            f32(4, 8, 2, 48), f32(4, 8, 2, 48),
            f32(4, 8, 2, 16), f32(8, 2, 16), f32(4, 8, 8), f32(8, 8), f32(8, 8),
            f32(4, 4, 8, 8), f32(4, 8, 8), f32(8, 4, 8), f32(4, 8), f32(4, 8),
            f32(8, 4, 2, 16), f32(4, 2, 16), f32(4, 2, 16), f32(2, 16), f32(4, 8),
        ] + pairs,
        compiler_params=pltpu.CompilerParams(
            collective_id=1, has_side_effects=True, vmem_limit_bytes=48 << 20
        ),
        name="reduce_grads",
    )(blocks)


def body(layer_input, ssm_input, out_grad, b_weight, c_weight, dt_weight, dt_bias, a_log, d_skip):
    length = layer_input.shape[0]
    head_count = dt_bias.shape[0]
    state_size = b_weight.shape[1]
    head_width = ssm_input.shape[1] // head_count
    proj_b = jnp.dot(layer_input, b_weight, preferred_element_type=jnp.float32)
    proj_c = jnp.dot(layer_input, c_weight, preferred_element_type=jnp.float32)
    raw_dt = jnp.dot(layer_input, dt_weight, preferred_element_type=jnp.float32) + dt_bias[None, :]
    dt_values = jax.nn.softplus(raw_dt)
    decay_rate = -jnp.exp(a_log)
    log_decay = dt_values * decay_rate[None, :]
    row_index = lax.broadcasted_iota(jnp.int32, (length, length), 0)
    col_index = lax.broadcasted_iota(jnp.int32, (length, length), 1)
    causal = row_index >= col_index
    triangle = causal.astype(jnp.float32)
    cumulative = jnp.dot(triangle, log_decay, precision=EXACT)
    block_decay = cumulative[-1]
    to_end = jnp.exp(block_decay[None, :] - cumulative)
    from_start = jnp.exp(cumulative)
    inputs = ssm_input.astype(jnp.float32).reshape(length, head_count, head_width)
    cotangent = out_grad.astype(jnp.float32).reshape(length, head_count, head_width)
    scaled_inputs = (to_end * dt_values)[:, :, None] * inputs
    scaled_cotangent = from_start[:, :, None] * cotangent
    local_state = jnp.einsum("shp,sn->hpn", scaled_inputs, proj_b, precision=EXACT)
    local_back = jnp.einsum("thp,tn->hpn", scaled_cotangent, proj_c, precision=EXACT)
    decay = jnp.pad(jnp.exp(block_decay).reshape(2, HALF), ((0, 0), (0, 4)), constant_values=1.0)
    decay = jnp.broadcast_to(decay[:, :, None], (2, 24, STATE))
    carries = scan_states(jnp.stack([local_state, local_back]), decay)
    carry_in, carry_out = carries[0], carries[1]
    spread = cumulative.T[:, :, None] - cumulative.T[:, None, :]
    decay_table = jnp.exp(jnp.where(causal[None], spread, -1e30))
    scores = jnp.dot(proj_c, proj_b.T, precision=EXACT)
    pair_dots = jnp.einsum("thp,shp->hts", cotangent, inputs, precision=EXACT)
    weight = decay_table * scores[None]
    back_in = jnp.einsum("hst,shp->thp", weight, cotangent, precision=EXACT)
    back_carry = jnp.einsum("hpn,tn->thp", carry_out, proj_b, precision=EXACT)
    back_in = back_in + to_end[:, :, None] * back_carry
    grad_x = dt_values[:, :, None] * back_in + d_skip[None, :, None] * cotangent
    mixed_pairs = decay_table * pair_dots
    pair_sum = jnp.einsum("hts,sh->ts", mixed_pairs, dt_values, precision=EXACT)
    grad_b = jnp.dot(pair_sum.T, proj_c, precision=EXACT)
    grad_b = grad_b + jnp.einsum("thp,hpn->tn", scaled_inputs, carry_out, precision=EXACT)
    grad_c = jnp.dot(pair_sum, proj_b, precision=EXACT)
    grad_c = grad_c + jnp.einsum("thp,hpn->tn", scaled_cotangent, carry_in, precision=EXACT)
    pair_terms = weight * pair_dots * dt_values.T[:, None, :]
    front_carry = jnp.einsum("hpn,tn->thp", carry_in, proj_c, precision=EXACT)
    own_in = from_start * jnp.sum(cotangent * front_carry, axis=2)
    own_out = to_end * dt_values * jnp.sum(inputs * back_carry, axis=2)
    cross_term = jnp.exp(block_decay) * jnp.sum(carry_out * carry_in, axis=(1, 2))
    last_row = (lax.broadcasted_iota(jnp.int32, (length, 1), 0) == length - 1).astype(jnp.float32)
    change = jnp.sum(pair_terms, axis=2).T - jnp.sum(pair_terms, axis=1).T + own_in - own_out
    change = change + last_row * (cross_term + jnp.sum(own_out, axis=0))[None, :]
    grad_log = jnp.dot(triangle.T, change, precision=EXACT)
    direct = jnp.sum(inputs * back_in, axis=2)
    grad_raw = (direct + grad_log * decay_rate[None, :]) * jax.nn.sigmoid(raw_dt)
    grad_bias = jnp.sum(grad_raw, axis=0)
    grad_alog = jnp.sum(grad_log * dt_values, axis=0) * decay_rate
    grad_skip = jnp.sum(cotangent * inputs, axis=(0, 2))
    extras = jnp.stack([grad_bias, grad_alog, grad_skip])
    grad_cols = jnp.concatenate([grad_b, grad_c, grad_raw], axis=1)
    weights_wide = jnp.concatenate([b_weight, c_weight, dt_weight], axis=1).astype(jnp.float32)
    grad_u = jnp.dot(grad_cols, weights_wide.T, precision=EXACT).astype(jnp.bfloat16)
    u_wide = layer_input.astype(jnp.float32)
    full_grads = jnp.einsum("td,tk->dk", u_wide, grad_cols, precision=EXACT)
    gb = full_grads[:, :128].reshape(64, 40, 128)
    gc = full_grads[:, 128:256].reshape(64, 40, 128)
    gd = jnp.pad(full_grads[:, 256:].reshape(64, 40, 40), ((0, 0), (0, 8), (0, 0))).reshape(64, 3, 16, 40)
    gd = gd.at[:, 2, 8:11].set(extras[None])
    gd = jnp.pad(jnp.swapaxes(gd, 1, 2).reshape(64, 16, 120), ((0, 0), (0, 0), (0, 8)))
    blocks = jnp.concatenate([gb, gc, gd], axis=1).reshape(OWNERS + (ROWS, 128))
    summed = reduce_grads(blocks).reshape(ROWS, 128)
    packed = summed[80:, :120].reshape(16, 3, 40).swapaxes(0, 1).reshape(48, 40)
    grad_x_out = grad_x.reshape(length, head_count * head_width).astype(jnp.bfloat16)
    return (
        grad_x_out,
        grad_u,
        summed[:40],
        summed[40:80],
        packed[:40],
        packed[40],
        packed[41],
        packed[42],
    )


def solution(mesh):
    split = Mesh(mesh.devices.reshape(4, 8, 2, 2, 2), AXES)
    placed = (P(DP_SEQ, None), P(DP_SEQ, None), P(DP_SEQ, None), P(), P(), P(), P(), P(), P())
    return jax.shard_map(
        body,
        mesh=split,
        in_specs=placed,
        out_specs=(
            P(DP_SEQ, None),
            P(DP_SEQ, None),
            P(SEQ, None),
            P(SEQ, None),
            P(SEQ, None),
            P(),
            P(),
            P(),
        ),
        check_vma=False,
    )
```

```python
import jax
import jax.numpy as jnp
from jax import lax
from jax.experimental import pallas as pl
from jax.experimental.pallas import tpu as pltpu
from jax.sharding import Mesh
from jax.sharding import PartitionSpec as P

SEQ = ("x", "z", "yh")
DP_SEQ = ("yl", "core", "x", "z", "yh")
AXES = ("x", "z", "yh", "yl", "core")
SIZES = {"x": 4, "z": 8, "yh": 2, "yl": 2, "core": 2}
MESH = pl.DeviceIdType.MESH
HEADS, WIDTH, STATE = 40, 64, 128
HALF = HEADS // 2
CHUNK = 4
CHUNKS = HALF // CHUNK
NX, NZ = SIZES["x"], SIZES["z"]
PIECE = WIDTH // NZ


def place():
    return {axis: lax.axis_index(axis) for axis in AXES}


def shifted(here, **steps):
    there = dict(here)
    for axis, step in steps.items():
        there[axis] = lax.rem(here[axis] + step, SIZES[axis])
    return tuple(there[axis] for axis in AXES)


def greet(peers):
    barrier = pltpu.get_barrier_semaphore()
    for peer in peers:
        pl.semaphore_signal(barrier, inc=1, device_id=peer, device_id_type=MESH)
    pl.semaphore_wait(barrier, len(peers))


def push(src, dst, send, recv, peer):
    return pltpu.make_async_remote_copy(
        src_ref=src, dst_ref=dst, send_sem=send, recv_sem=recv, device_id=peer, device_id_type=MESH
    )


TOK = 128
MODEL = 2560
ROWS = 96
BLOCK = CHUNK * WIDTH
F32, BF16 = jnp.float32, jnp.bfloat16


def dot(a, b):
    return jnp.dot(a, b, preferred_element_type=F32)


def dot_tn(a, b):
    return lax.dot_general(a, b, (((0,), (0,)), ((), ())), preferred_element_type=F32)


def dot_nt(a, b):
    return lax.dot_general(a, b, (((1,), (1,)), ((), ())), preferred_element_type=F32)


def split(v):
    top = v.astype(BF16)
    return top, (v - top.astype(F32)).astype(BF16)


def wide(v):
    return jnp.concatenate(split(v), axis=1)


def tall(v):
    return jnp.concatenate(split(v), axis=0)


def square(v):
    w = wide(v)
    return jnp.concatenate([w, w], axis=0)


def fold(p):
    return p[:, :128] + p[:, 128:]


def padded(v):
    return jnp.concatenate([v, jnp.zeros((TOK - v.shape[0], TOK), F32)], axis=0)


def layer_kernel(
    u_ref, x_ref, g_ref, wb_ref, wc_ref, wd_ref, bias_ref, alog_ref, skip_ref,
    gx_ref, gu_ref, gbw_ref, gcw_ref, gdw_ref, ex_ref,
    xt, gt, ut, xw, gw, b4, c4, bt4, ct4, scores, pairacc, rowacc, inner, gbacc, gcacc,
    rows_dt, rows_ws, rows_fs, rows_te, rows_cum, rows_skip, rows_col, rows_xb, rows_gf, rows_cross, rows_gx,
    flat_dt, flat_raw, gwd, sr, dec, car, par, pq, arec, xs, xr, bs, ps, ys, dpar, coef, pair, zd, rd,
    grad, c_rec, h1, a0, a1, a1r, a2, a2r, b0, b1, b1r, b2, b2r, c0, c1, c1r, c2, c2r, fin,
    *sems,
):
    here = place()
    x, z, h, yl, core = (here[a] for a in AXES)
    y = h * 2 + yl
    low = h == 0
    mine, other = h * HALF, (1 - h) * HALF
    partner = shifted(here, yh=1)
    cpeer = shifted(here, core=1)
    lpeer = shifted(here, yl=1)
    zpeers = [shifted(here, z=d) for d in range(1, NZ)]
    xpeers = [shifted(here, x=d) for d in range(1, NX)]
    ynext = [lax.rem(y + d, 4) for d in range(1, 4)]
    ypeers = [(x, z, t // 2, lax.rem(t, 2), core) for t in ynext]
    peers = [cpeer] + ypeers + zpeers + xpeers
    scan_sems, red_sems = sems[:16], sems[16:]
    y1s, y1r, as_, ar_, xss, xrs, bss, brs, y2s, y2r, d1s, d1r, d2s, d2r, d3s, d3r = scan_sems
    barrier = pltpu.get_barrier_semaphore()
    for peer in peers:
        pl.semaphore_signal(barrier, inc=1, device_id=peer, device_id_type=MESH)

    u = u_ref[...]
    raw = dot(u, wd_ref[...])
    raw = jnp.concatenate([raw, jnp.zeros((TOK, TOK - HEADS), F32)], axis=1)
    raw = raw.T[:HEADS] + bias_ref[...]
    small = jnp.exp(-jnp.abs(raw))
    above = 1.0 + small
    gap = above - 1.0
    log_part = jnp.where(gap == 0.0, small, jnp.log(above) * (small / jnp.where(gap == 0.0, 1.0, gap)))
    dt = jnp.maximum(raw, 0.0) + log_part
    rate = -jnp.exp(alog_ref[...])
    row_i = lax.broadcasted_iota(jnp.int32, (TOK, TOK), 0)
    col_i = lax.broadcasted_iota(jnp.int32, (TOK, TOK), 1)
    upto = (row_i <= col_i).astype(F32)
    since = (row_i >= col_i).astype(F32)
    cum = jnp.dot(dt * rate, upto, precision=lax.Precision.HIGHEST, preferred_element_type=F32)
    last = cum[:, TOK - 1 :]
    to_end = jnp.exp(last - cum)
    from_start = jnp.exp(cum)
    flat_dt[...] = dt
    flat_raw[...] = raw

    def rows(v):
        return v.reshape(HEADS, 1, TOK)

    rows_dt[...] = rows(dt)
    rows_ws[...] = rows(to_end * dt)
    rows_fs[...] = rows(from_start)
    rows_te[...] = rows(to_end)
    rows_cum[...] = rows(cum)
    rows_skip[...] = rows(jnp.broadcast_to(skip_ref[...], (HEADS, TOK)))
    decay = jnp.broadcast_to(jnp.exp(last), (HEADS, STATE))
    fill = jnp.ones((4, STATE), F32)
    dec[0] = jnp.concatenate([decay[:HALF], fill], axis=0)
    dec[1] = jnp.concatenate([decay[HALF:], fill], axis=0)
    proj_b = dot(u, wb_ref[...])
    proj_c = dot(u, wc_ref[...])
    b4[...] = square(proj_b)
    c4[...] = square(proj_c)

    def states(first):
        at = pl.multiple_of(first * WIDTH, BLOCK)
        heads = pl.ds(first, CHUNK)
        rows_at = pl.ds(at, BLOCK)
        xc = x_ref[:, pl.ds(at, BLOCK)].T
        gc = g_ref[:, pl.ds(at, BLOCK)].T
        xt[rows_at, :] = xc
        gt[rows_at, :] = gc
        xsc = xc.astype(F32).reshape(CHUNK, WIDTH, TOK) * rows_ws[heads]
        gsc = gc.astype(F32).reshape(CHUNK, WIDTH, TOK) * rows_fs[heads]
        xwc = wide(xsc.reshape(BLOCK, TOK))
        gwc = wide(gsc.reshape(BLOCK, TOK))
        xw[rows_at, :] = xwc
        gw[rows_at, :] = gwc
        sr[0, heads] = fold(dot(xwc, b4[...])).reshape(CHUNK, WIDTH, STATE)
        sr[1, heads] = fold(dot(gwc, c4[...])).reshape(CHUNK, WIDTH, STATE)

    states(other)
    pl.semaphore_wait(barrier, len(peers))
    first = push(dec.at[1 - h], dpar, d1s, d1r, partner)
    first.start()
    y1 = [
        push(
            sr.at[:, pl.ds(other + c * CHUNK, CHUNK)],
            par.at[:, pl.ds(c * CHUNK, CHUNK)],
            y1s.at[c], y1r.at[c], partner,
        )
        for c in range(CHUNKS)
    ]
    y1[0].start()
    states(other + CHUNK)
    y1[1].start()
    xr[x] = jnp.zeros((HALF, PIECE, STATE), F32)
    first.wait()
    own_decay = dec[h]
    par_decay = dpar[...]
    one = jnp.ones_like(own_decay)
    coef[0] = jnp.where(low, par_decay, one)
    coef[1] = jnp.where(low, one, own_decay)
    coef[2] = jnp.where(low, one, par_decay)
    coef[3] = jnp.where(low, own_decay, one)
    pair[...] = own_decay * par_decay
    zd[z] = own_decay * par_decay
    second = [push(pair, zd.at[z], d2s.at[d], d2r.at[d], peer) for d, peer in enumerate(zpeers)]
    for copy in second:
        copy.start()
    states(mine)
    for c in range(2, CHUNKS):
        states(other + c * CHUNK)
    bt4[...] = square(proj_b.T)
    ct4[...] = square(proj_c.T)
    scores[...] = jnp.where(row_i >= col_i, fold(dot(wide(proj_c), bt4[...])), 0.0)
    pairacc[...] = jnp.zeros((TOK, TOK), F32)
    rowacc[...] = jnp.zeros((TOK, TOK), F32)
    for copy in second:
        copy.wait()
    row = zd[0]
    for k in range(1, NZ):
        row = row * zd[k]
    rd[x] = row
    third = [push(rd.at[x], rd.at[x], d3s.at[d], d3r.at[d], peer) for d, peer in enumerate(xpeers)]
    for copy in third:
        copy.start()

    def a_copies(c):
        heads = pl.ds(c * CHUNK, CHUNK)
        copies = []
        for d, peer in enumerate(zpeers):
            pz = pl.multiple_of(lax.rem(z + d + 1, NZ) * PIECE, PIECE)
            copies.append(
                push(pq.at[:, heads, pl.ds(pz, PIECE)], arec.at[z, :, heads], as_.at[c, d], ar_.at[c, d], peer)
            )
        return copies

    def x_copies(c):
        heads = pl.ds(c * CHUNK, CHUNK)
        copies = []
        for d, peer in enumerate(xpeers):
            px = lax.rem(x + d + 1, NX)
            back = jnp.where(px > x, 0, 1)
            copies.append(push(xs.at[back, heads], xr.at[x, heads], xss.at[c, d], xrs.at[c, d], peer))
        return copies

    def b_copies(c):
        heads = pl.ds(c * CHUNK, CHUNK)
        here_rows = pl.ds(pl.multiple_of(z * PIECE, PIECE), PIECE)
        copies = []
        for d, peer in enumerate(zpeers):
            pz = lax.rem(z + d + 1, NZ)
            copies.append(
                push(bs.at[pz, :, heads], ps.at[:, heads, here_rows], bss.at[c, d], brs.at[c, d], peer)
            )
        return copies

    def y2_copy(c):
        return push(
            ys.at[:, pl.ds(c * CHUNK, CHUNK)],
            car.at[:, pl.ds(mine + c * CHUNK, CHUNK)],
            y2s.at[c], y2r.at[c], partner,
        )

    def pairs(c):
        y1[c].wait_recv()
        if c + 2 < CHUNKS:
            y1[c + 2].start()

        def head(i, carry):
            k = c * CHUNK + i
            at = pl.ds(k, 1)
            pq[0, k] = coef[0, at, :] * sr[0, mine + k] + coef[1, at, :] * par[0, k]
            pq[1, k] = coef[2, at, :] * sr[1, mine + k] + coef[3, at, :] * par[1, k]
            return carry

        lax.fori_loop(0, CHUNK, head, 0)
        heads = pl.ds(c * CHUNK, CHUNK)
        own = pl.ds(pl.multiple_of(z * PIECE, PIECE), PIECE)
        arec[z, :, heads] = pq[:, heads, own, :]
        for copy in a_copies(c):
            copy.start()

    def totals(c):
        for copy in a_copies(c):
            copy.wait_recv()

        def head(i, carry):
            k = c * CHUNK + i
            at = pl.ds(k, 1)
            forward = arec[0, 0, k]
            backward = arec[NZ - 1, 1, k]
            for j in range(1, NZ):
                forward = zd[j, at, :] * forward + arec[j, 0, k]
                backward = zd[NZ - 1 - j, at, :] * backward + arec[NZ - 1 - j, 1, k]
            xs[0, k] = forward
            xs[1, k] = backward
            return carry

        lax.fori_loop(0, CHUNK, head, 0)
        for copy in x_copies(c):
            copy.start()

    def prefixes(c):
        if c == 0:
            for copy in third:
                copy.wait()
        for copy in x_copies(c):
            copy.wait_recv()

        def head(i, carry):
            k = c * CHUNK + i
            at = pl.ds(k, 1)
            forward = jnp.zeros((PIECE, STATE), jnp.float32)
            backward = jnp.zeros((PIECE, STATE), jnp.float32)
            for j in range(NX):
                forward = jnp.where(j < x, rd[j, at, :] * forward + xr[j, k], forward)
                m = NX - 1 - j
                backward = jnp.where(m > x, rd[m, at, :] * backward + xr[m, k], backward)
            for j in range(NZ):
                bs[j, 0, k] = forward
                forward = zd[j, at, :] * forward + arec[j, 0, k]
                m = NZ - 1 - j
                bs[m, 1, k] = backward
                backward = zd[m, at, :] * backward + arec[m, 1, k]
            return carry

        lax.fori_loop(0, CHUNK, head, 0)
        heads = pl.ds(c * CHUNK, CHUNK)
        own = pl.ds(pl.multiple_of(z * PIECE, PIECE), PIECE)
        ps[:, heads, own, :] = bs[z, :, heads]
        for copy in b_copies(c):
            copy.start()

    def finals(c):
        for copy in b_copies(c):
            copy.wait_recv()

        def head(i, carry):
            k = c * CHUNK + i
            at = pl.ds(k, 1)
            before, after = ps[0, k], ps[1, k]
            zero = jnp.zeros_like(before)
            ys[0, k] = coef[3, at, :] * before + jnp.where(low, sr[0, mine + k], zero)
            ys[1, k] = coef[1, at, :] * after + jnp.where(low, zero, sr[1, mine + k])
            car[0, mine + k] = coef[2, at, :] * before + jnp.where(low, zero, par[0, k])
            car[1, mine + k] = coef[0, at, :] * after + jnp.where(low, par[1, k], zero)
            return carry

        lax.fori_loop(0, CHUNK, head, 0)
        y2_copy(c).start()


    def within(start, count):
        def two(i, carry):
            for j in range(2):
                k = start + 2 * i + j
                at = pl.ds(pl.multiple_of(k * WIDTH, WIDTH), WIDTH)
                gk = gt[at, :]
                dots = dot_tn(gk, xt[at, :])
                across = jnp.broadcast_to(rows_cum[k], (TOK, TOK))
                table = jnp.exp(jnp.minimum(across.T - across, 0.0))
                weight = table * scores[...]
                inner[at, :] = fold(dot(gk, wide(weight)))
                terms = weight * dots
                rows_col[k] = jnp.sum(terms, axis=0, keepdims=True)
                pairacc[...] += table * dots * rows_dt[k]
                sums = jnp.sum(terms * rows_dt[k], axis=1, keepdims=True)
                rowacc[...] = jnp.where(col_i == k, sums, rowacc[...])
            return carry

        lax.fori_loop(0, count // 2, two, 0)

    gbacc[...] = jnp.zeros((2 * TOK, 2 * TOK), F32)
    gcacc[...] = jnp.zeros((2 * TOK, 2 * TOK), F32)

    def outputs(first):
        at = pl.multiple_of(first * WIDTH, BLOCK)
        heads = pl.ds(first, CHUNK)
        rows_at = pl.ds(at, BLOCK)
        ci = car[0, heads]
        co = car[1, heads]
        rows_cross[heads] = jnp.sum(ci * co, axis=1, keepdims=True)
        ciw = wide(ci.reshape(BLOCK, STATE))
        cow = wide(co.reshape(BLOCK, STATE))
        back = fold(dot(cow, bt4[...])).reshape(CHUNK, WIDTH, TOK)
        front = fold(dot(ciw, ct4[...])).reshape(CHUNK, WIDTH, TOK)
        gbacc[...] += dot_tn(xw[rows_at, :], cow)
        gcacc[...] += dot_tn(gw[rows_at, :], ciw)
        xf = xt[rows_at, :].astype(F32).reshape(CHUNK, WIDTH, TOK)
        gf = gt[rows_at, :].astype(F32).reshape(CHUNK, WIDTH, TOK)
        rows_xb[heads] = jnp.sum(xf * back, axis=1, keepdims=True)
        rows_gf[heads] = jnp.sum(gf * front, axis=1, keepdims=True)
        rows_gx[heads] = jnp.sum(gf * xf, axis=1, keepdims=True)
        total = inner[rows_at, :].reshape(CHUNK, WIDTH, TOK) + rows_te[heads] * back
        gx = rows_dt[heads] * total + rows_skip[heads] * gf
        gx_ref[:, pl.ds(at, BLOCK)] = gx.reshape(BLOCK, TOK).T.astype(BF16)

    within(other, 4)
    for c in range(1, CHUNKS):
        states(mine + c * CHUNK)
    within(other + 4, 4)
    for step in range(CHUNKS + 3):
        if step < CHUNKS:
            pairs(step)
        if 0 <= step - 1 < CHUNKS:
            totals(step - 1)
        if 0 <= step - 2 < CHUNKS:
            prefixes(step - 2)
        if 0 <= step - 3 < CHUNKS:
            finals(step - 3)
        if step < 3:
            within(other + 8 + 4 * step, 4)
        else:
            within(mine + 4 * (step - 3), 4)
            outputs(mine + 4 * (step - 3))
        if step == 5:
            for j in range(0, MODEL, 512):
                ut[j : j + 512, :] = u_ref[:, j : j + 512].T
    for c in range(CHUNKS):
        y2_copy(c).wait_recv()
        outputs(other + c * CHUNK)

    sums = pairacc[...]
    sums = jnp.where(row_i >= col_i, sums, 0.0)
    sumw = wide(sums)
    acc = gbacc[...] + dot_tn(sumw, wide(dot(u_ref[...], wc_ref[...])))
    acc = acc[:TOK] + acc[TOK:]
    grad_b = fold(acc)
    acc = gcacc[...]
    acc = acc[:TOK] + acc[TOK:]
    grad_c = fold(acc) + fold(dot(sumw, b4[...]))

    def flat(ref):
        return ref[...].reshape(HEADS, TOK)

    dt = flat_dt[...]
    raw = flat_raw[...]
    end = flat(rows_te)
    rate = -jnp.exp(alog_ref[...])
    col = flat(rows_col)
    xb = end * flat(rows_xb)
    direct = col + xb
    own_out = dt * xb
    own_in = flat(rows_fs) * flat(rows_gf)
    cross = flat(rows_fs)[:, TOK - 1 :] * jnp.sum(flat(rows_cross), axis=1, keepdims=True)
    change = rowacc[...].T[:HEADS] - dt * col + own_in - own_out
    lanes = lax.broadcasted_iota(jnp.int32, (HEADS, TOK), 1)
    edge = cross + jnp.sum(own_out, axis=1, keepdims=True)
    change = change + jnp.where(lanes == TOK - 1, edge, 0.0)
    grad_log = jnp.dot(change, since, precision=lax.Precision.HIGHEST, preferred_element_type=F32)
    grad_raw = (direct + grad_log * rate) * (1.0 / (1.0 + jnp.exp(-raw)))
    grad_bias = jnp.sum(grad_raw, axis=1, keepdims=True)
    grad_alog = jnp.sum(grad_log * dt, axis=1, keepdims=True) * rate
    grad_skip = jnp.sum(flat(rows_gx), axis=1, keepdims=True)
    extra = jnp.where(lanes == 0, grad_bias, jnp.where(lanes == 1, grad_alog, jnp.where(lanes == 2, grad_skip, 0.0)))
    extra = padded(extra).T[:8]
    grad_d = padded(grad_raw).T
    bw, cw, dw = wide(grad_b), wide(grad_c), wide(grad_d)

    def weights(i, carry):
        at = pl.ds(pl.multiple_of(i * 640, 640), 640)
        cols = ut[at, :]
        grad[i, :, :, 0:40, :] = fold(dot(cols, bw)).reshape(NZ, 2, 40, 128)
        grad[i, :, :, 40:80, :] = fold(dot(cols, cw)).reshape(NZ, 2, 40, 128)
        gwd[...] = fold(dot(cols, dw))
        for s in range(16):
            third_part = jnp.concatenate([gwd[s * 40 + 32 : s * 40 + 40, :], extra], axis=0)
            packed = gwd[s * 40 : s * 40 + 16, :]
            packed = packed + pltpu.roll(gwd[s * 40 + 16 : s * 40 + 32, :], 40, 1)
            grad[i, s // 2, s % 2, 80:96, :] = packed + pltpu.roll(third_part, 80, 1)
        return carry

    lax.fori_loop(0, NX, weights, 0)
    out = fin
    cs, cr, x0s, x0r, y0s, y0r, z0s, z0r, y3s, y3r, z1s, z1r, x1s, x1r, z2s, z2r, x2s, x2r, y4s, y4r, ls, lr, ks, kr = red_sems
    keep = pl.multiple_of(core * 48, 8)
    give = pl.multiple_of((1 - core) * 48, 8)
    swap = push(grad.at[:, :, :, pl.ds(give, 48)], c_rec, cs, cr, cpeer)
    swap.start()

    bt, ctall, dtall = tall(grad_b), tall(grad_c), tall(grad_d)[:, :HEADS]
    both_t = jnp.concatenate([bt, ctall], axis=1)

    def model_grads(i, carry):
        at = pl.ds(pl.multiple_of(i * 512, 512), 512)
        both_w = jnp.concatenate([wb_ref[at, :], wc_ref[at, :]], axis=1)
        p = dot_nt(both_t, both_w) + dot_nt(dtall, wd_ref[at, :])
        gu_ref[:, at] = (p[:TOK] + p[TOK:]).astype(BF16)
        return carry

    lax.fori_loop(0, 1, model_grads, 0)
    swap.wait()
    for i in range(NX):
        h1[i] = grad[i, :, :, pl.ds(keep, 48), :] + c_rec[i]

    def part(start, there):
        return pl.ds(pl.multiple_of(start + 8 * lax.rem(there, 2), 8), 8)

    def begin(copies):
        for copy in copies:
            copy.start()
        return copies

    def arrived(copies):
        for copy in copies:
            copy.wait_recv()

    znext = [lax.rem(z + d, NZ) for d in range(1, NZ)]
    xnext = [lax.rem(x + d, NX) for d in range(1, NX)]
    z_one = begin([push(h1.at[:, t, :, pl.ds(32, 16)], c0.at[z], z0s.at[d], z0r.at[d], zpeers[d]) for d, t in enumerate(znext)])
    x_one = begin([push(h1.at[t, :, :, pl.ds(0, 16)], a0.at[x], x0s.at[d], x0r.at[d], xpeers[d]) for d, t in enumerate(xnext)])
    y_one = begin([push(h1.at[:, :, t // 2, part(16, t)], b0.at[y], y0s.at[d], y0r.at[d], ypeers[d]) for d, t in enumerate(ynext)])
    lax.fori_loop(1, 5, model_grads, 0)
    arrived(x_one)
    total = h1[x, :, :, pl.ds(0, 16), :]
    for t in xnext:
        total = total + a0[t]
    a1[...] = total
    y_two = begin([push(a1.at[:, t // 2, part(0, t)], a1r.at[y], y3s.at[d], y3r.at[d], ypeers[d]) for d, t in enumerate(ynext)])
    arrived(y_one)
    total = h1[:, :, h, part(16, yl), :]
    for t in ynext:
        total = total + b0[t]
    b1[...] = total
    z_two = begin([push(b1.at[:, t], b1r.at[z], z1s.at[d], z1r.at[d], zpeers[d]) for d, t in enumerate(znext)])
    arrived(z_one)
    total = h1[:, z, :, pl.ds(32, 16), :]
    for t in znext:
        total = total + c0[t]
    c1[...] = total
    x_two = begin([push(c1.at[t], c1r.at[x], x1s.at[d], x1r.at[d], xpeers[d]) for d, t in enumerate(xnext)])
    arrived(y_two)
    total = a1[:, h, part(0, yl), :]
    for t in ynext:
        total = total + a1r[t]
    a2[...] = total
    z_three = begin([push(a2.at[t], a2r.at[z], z2s.at[d], z2r.at[d], zpeers[d]) for d, t in enumerate(znext)])
    arrived(z_two)
    total = b1[:, z]
    for t in znext:
        total = total + b1r[t]
    b2[...] = total
    x_three = begin([push(b2.at[t], b2r.at[x], x2s.at[d], x2r.at[d], xpeers[d]) for d, t in enumerate(xnext)])
    arrived(x_two)
    total = c1[x]
    for t in xnext:
        total = total + c1r[t]
    c2[...] = total
    y_three = begin([push(c2.at[t // 2, part(0, t)], c2r.at[y], y4s.at[d], y4r.at[d], ypeers[d]) for d, t in enumerate(ynext)])
    arrived(z_three)
    total = a2[z]
    for t in znext:
        total = total + a2r[t]
    out[core, 0, yl] = total
    arrived(x_three)
    total = b2[x]
    for t in xnext:
        total = total + b2r[t]
    out[core, 1, yl] = total
    arrived(y_three)
    total = c2[h, part(0, yl), :]
    for t in ynext:
        total = total + c2r[t]
    out[core, 2, yl] = total
    last = push(out.at[core, :, yl], out.at[core, :, yl], ls, lr, lpeer)
    last.start()
    last.wait()
    both = push(out.at[core], out.at[core], ks, kr, cpeer)
    both.start()
    both.wait()

    whole = fin[...].reshape(ROWS, 128)
    gbw_ref[...] = whole[:40]
    gcw_ref[...] = whole[40:80]
    tail = whole[80:]
    gdw_ref[0:16, :] = tail[:, :HEADS]
    gdw_ref[16:32, :] = tail[:, 40:80]
    tail = tail[:, 80:120]
    gdw_ref[32:40, :] = tail[:8]
    ex_ref[...] = tail[8:]
    for c in range(CHUNKS):
        y1[c].wait_send()
        for copy in a_copies(c) + x_copies(c) + b_copies(c):
            copy.wait_send()
        y2_copy(c).wait_send()
    for copy in x_one + y_one + z_one + x_two + y_two + z_two + x_three + y_three + z_three:
        copy.wait_send()


def layer(u, x, g, wb, wc, wd, bias, alog, skip):
    vmem = pl.BlockSpec(memory_space=pltpu.VMEM)
    dma = pltpu.SemaphoreType.DMA
    half = (2, HALF, WIDTH, STATE)

    def f32(*shape):
        return pltpu.VMEM(shape + (128,), F32)

    def b16(*shape):
        return pltpu.VMEM(shape, BF16)

    def sems(counts):
        pairs = []
        for n in counts:
            pairs += [dma if n == () else dma(n)] * 2
        return pairs

    shape = jax.ShapeDtypeStruct
    return pl.pallas_call(
        layer_kernel,
        out_shape=(
            shape((TOK, MODEL), BF16), shape((TOK, MODEL), BF16), shape((40, STATE), F32),
            shape((40, STATE), F32), shape((40, HEADS), F32), shape((8, HEADS), F32),
        ),
        in_specs=[vmem] * 9,
        out_specs=(vmem,) * 6,
        scratch_shapes=[
            b16(MODEL, TOK), b16(MODEL, TOK), b16(MODEL, TOK), b16(MODEL, 256), b16(MODEL, 256),
            b16(256, 256), b16(256, 256), b16(256, 256), b16(256, 256),
            f32(TOK), f32(TOK), f32(TOK), f32(MODEL), pltpu.VMEM((256, 256), F32), pltpu.VMEM((256, 256), F32),
        ] + [f32(HEADS, 1)] * 11 + [
            f32(HEADS), f32(HEADS), f32(640),
            f32(2, HEADS, WIDTH), f32(2, 24), f32(2, HEADS, WIDTH),
            f32(*half[:3]), f32(*half[:3]),
            f32(NZ, 2, HALF, PIECE), f32(2, HALF, PIECE), f32(NX, HALF, PIECE), f32(NZ, 2, HALF, PIECE),
            f32(*half[:3]), f32(*half[:3]),
            f32(24), f32(4, 24), f32(24), f32(NZ, 24), f32(NX, 24),
            f32(NX, NZ, 2, ROWS), f32(4, 8, 2, 48), f32(4, 8, 2, 48),
            f32(4, 8, 2, 16), f32(8, 2, 16), f32(4, 8, 8), f32(8, 8), f32(8, 8),
            f32(4, 4, 8, 8), f32(4, 8, 8), f32(8, 4, 8), f32(4, 8), f32(4, 8),
            f32(8, 4, 2, 16), f32(4, 2, 16), f32(4, 2, 16), f32(2, 16), f32(4, 8),
            f32(2, 3, 2, 8),
        ] + sems(
            [(CHUNKS,), (CHUNKS, NZ - 1), (CHUNKS, NX - 1), (CHUNKS, NZ - 1), (CHUNKS,), (), (NZ - 1,), (NX - 1,)]
        ) + sems([(), (3,), (3,), (7,), (3,), (7,), (3,), (7,), (3,), (3,), (), ()]),
        compiler_params=pltpu.CompilerParams(
            collective_id=0, has_side_effects=True, vmem_limit_bytes=60 << 20
        ),
        name="layer",
    )(u, x, g, wb, wc, wd, bias, alog, skip)


def body(layer_input, ssm_input, out_grad, b_weight, c_weight, dt_weight, dt_bias, a_log, d_skip):
    gx, gu, gb, gc, gd, extra = layer(
        layer_input, ssm_input, out_grad, b_weight, c_weight, dt_weight,
        dt_bias[:, None], a_log[:, None], d_skip[:, None],
    )
    return gx, gu, gb, gc, gd, extra[0], extra[1], extra[2]


def solution(mesh):
    split_mesh = Mesh(mesh.devices.reshape(4, 8, 2, 2, 2), AXES)
    cut, whole = P(DP_SEQ, None), P()
    return jax.shard_map(
        body,
        mesh=split_mesh,
        in_specs=(cut, cut, cut) + (whole,) * 6,
        out_specs=(cut, cut) + (P(SEQ, None),) * 3 + (whole,) * 3,
        check_vma=False,
    )
```

```python
import jax
import jax.numpy as jnp
from jax import lax
from jax.experimental import pallas as pl
from jax.experimental.pallas import tpu as pltpu
from jax.sharding import Mesh
from jax.sharding import PartitionSpec as P

SEQ = ("x", "z", "yh")
DP_SEQ = ("yl", "core", "x", "z", "yh")
AXES = ("x", "z", "yh", "yl", "core")
SIZES = {"x": 4, "z": 8, "yh": 2, "yl": 2, "core": 2}
MESH = pl.DeviceIdType.MESH
HEADS, WIDTH, STATE = 40, 64, 128
HALF = HEADS // 2
SIZES_OF = (2, 4, 4, 4, 4, 2)
STARTS = tuple(sum(SIZES_OF[:c]) for c in range(len(SIZES_OF)))
CHUNKS = len(SIZES_OF)
NX, NZ = SIZES["x"], SIZES["z"]
PIECE = WIDTH // NZ
FAR_FIRST = (4, 3, 5, 2, 6, 1, 7)


def place():
    return {axis: lax.axis_index(axis) for axis in AXES}


def shifted(here, **steps):
    there = dict(here)
    for axis, step in steps.items():
        there[axis] = lax.rem(here[axis] + step, SIZES[axis])
    return tuple(there[axis] for axis in AXES)


def greet(peers):
    barrier = pltpu.get_barrier_semaphore()
    for peer in peers:
        pl.semaphore_signal(barrier, inc=1, device_id=peer, device_id_type=MESH)
    pl.semaphore_wait(barrier, len(peers))


def push(src, dst, send, recv, peer):
    return pltpu.make_async_remote_copy(
        src_ref=src, dst_ref=dst, send_sem=send, recv_sem=recv, device_id=peer, device_id_type=MESH
    )


TOK = 128
MODEL = 2560
ROWS = 96
F32, BF16 = jnp.float32, jnp.bfloat16


def dot(a, b):
    return jnp.dot(a, b, preferred_element_type=F32)


def dot_tn(a, b):
    return lax.dot_general(a, b, (((0,), (0,)), ((), ())), preferred_element_type=F32)


def dot_nt(a, b):
    return lax.dot_general(a, b, (((1,), (1,)), ((), ())), preferred_element_type=F32)


def split(v):
    top = v.astype(BF16)
    return top, (v - top.astype(F32)).astype(BF16)


def wide(v):
    return jnp.concatenate(split(v), axis=1)


def tall(v):
    return jnp.concatenate(split(v), axis=0)


def square(v):
    w = wide(v)
    return jnp.concatenate([w, w], axis=0)


def fold(p):
    return p[:, :128] + p[:, 128:]


def padded(v):
    return jnp.concatenate([v, jnp.zeros((TOK - v.shape[0], TOK), F32)], axis=0)


def layer_kernel(
    u_ref, x_ref, g_ref, wb_ref, wc_ref, wd_ref, bias_ref, alog_ref, skip_ref,
    gx_ref, gu_ref, gbw_ref, gcw_ref, gdw_ref, ex_ref,
    xt, gt, ut, xw, gw, b4, c4, bt4, ct4, scores, pairacc, rowacc, inner, gbacc, gcacc,
    rows_dt, rows_ws, rows_fs, rows_te, rows_cum, rows_skip, rows_col, rows_xb, rows_gf, rows_cross, rows_gx,
    flat_dt, flat_raw, gwd, sr, dec, car, par, pq, arec, xs, xr, bs, ps, ys, dpar, coef, pair, zd, rd,
    grad, c_rec, h1, a0, a1, a1r, a2, a2r, b0, b1, b1r, b2, b2r, c0, c1, c1r, c2, c2r, fin,
    *sems,
):
    here = place()
    x, z, h, yl, core = (here[a] for a in AXES)
    y = h * 2 + yl
    low = h == 0
    mine, other = h * HALF, (1 - h) * HALF
    partner = shifted(here, yh=1)
    cpeer = shifted(here, core=1)
    dpeers = [cpeer, shifted(here, yl=1), shifted(here, yl=1, core=1)]
    zpeers = [shifted(here, z=d) for d in range(1, NZ)]
    xpeers = [shifted(here, x=d) for d in range(1, NX)]
    ynext = [lax.rem(y + d, 4) for d in range(1, 4)]
    ypeers = [(x, z, t // 2, lax.rem(t, 2), core) for t in ynext]
    peers = [cpeer, dpeers[2]] + ypeers + zpeers + xpeers
    scan_sems, red_sems = sems[:16], sems[16:]
    y1s, y1r, as_, ar_, xss, xrs, bss, brs, y2s, y2r, d1s, d1r, d2s, d2r, d3s, d3r = scan_sems
    barrier = pltpu.get_barrier_semaphore()
    for peer in peers:
        pl.semaphore_signal(barrier, inc=1, device_id=peer, device_id_type=MESH)

    u = u_ref[...]
    columns = jnp.concatenate([bias_ref[...], alog_ref[...], skip_ref[...], jnp.zeros((5, HEADS), F32)], axis=0)
    columns = jnp.concatenate([columns, jnp.zeros((8, TOK - HEADS), F32)], axis=1)
    columns = padded(columns).T[:HEADS]
    alog = columns[:, 1:2]
    raw = dot_nt(wd_ref[...], u) + columns[:, 0:1]
    small = jnp.exp(-jnp.abs(raw))
    above = 1.0 + small
    gap = above - 1.0
    log_part = jnp.where(gap == 0.0, small, jnp.log(above) * (small / jnp.where(gap == 0.0, 1.0, gap)))
    dt = jnp.maximum(raw, 0.0) + log_part
    rate = -jnp.exp(alog)
    row_i = lax.broadcasted_iota(jnp.int32, (TOK, TOK), 0)
    col_i = lax.broadcasted_iota(jnp.int32, (TOK, TOK), 1)
    upto = (row_i <= col_i).astype(F32)
    since = (row_i >= col_i).astype(F32)
    cum = jnp.dot(dt * rate, upto, precision=lax.Precision.HIGHEST, preferred_element_type=F32)
    last = cum[:, TOK - 1 :]
    to_end = jnp.exp(last - cum)
    from_start = jnp.exp(cum)
    flat_dt[...] = dt
    flat_raw[...] = raw

    def rows(v):
        return v.reshape(HEADS, 1, TOK)

    rows_dt[...] = rows(dt)
    rows_ws[...] = rows(to_end * dt)
    rows_fs[...] = rows(from_start)
    rows_te[...] = rows(to_end)
    rows_cum[...] = rows(cum)
    rows_skip[...] = rows(jnp.broadcast_to(columns[:, 2:3], (HEADS, TOK)))
    decay = jnp.broadcast_to(jnp.exp(last), (HEADS, STATE))
    fill = jnp.ones((4, STATE), F32)
    dec[0] = jnp.concatenate([decay[:HALF], fill], axis=0)
    dec[1] = jnp.concatenate([decay[HALF:], fill], axis=0)
    proj_b = dot(u, wb_ref[...])
    proj_c = dot(u, wc_ref[...])
    b4[...] = square(proj_b)
    c4[...] = square(proj_c)

    def states(start, c):
        count, block = SIZES_OF[c], SIZES_OF[c] * WIDTH
        at = pl.multiple_of((start + STARTS[c]) * WIDTH, 2 * WIDTH)
        heads = pl.ds(start + STARTS[c], count)
        rows_at = pl.ds(at, block)
        xc = x_ref[:, pl.ds(at, block)].T
        gc = g_ref[:, pl.ds(at, block)].T
        xt[rows_at, :] = xc
        gt[rows_at, :] = gc
        xsc = xc.astype(F32).reshape(count, WIDTH, TOK) * rows_ws[heads]
        gsc = gc.astype(F32).reshape(count, WIDTH, TOK) * rows_fs[heads]
        xwc = wide(xsc.reshape(block, TOK))
        gwc = wide(gsc.reshape(block, TOK))
        xw[rows_at, :] = xwc
        gw[rows_at, :] = gwc
        sr[0, heads] = fold(dot(xwc, b4[...])).reshape(count, WIDTH, STATE)
        sr[1, heads] = fold(dot(gwc, c4[...])).reshape(count, WIDTH, STATE)

    states(other, 0)
    pl.semaphore_wait(barrier, len(peers))
    first = push(dec.at[1 - h], dpar, d1s, d1r, partner)
    first.start()
    y1 = [
        push(
            sr.at[:, pl.ds(other + STARTS[c], SIZES_OF[c])],
            par.at[:, pl.ds(STARTS[c], SIZES_OF[c])],
            y1s.at[c], y1r.at[c], partner,
        )
        for c in range(CHUNKS)
    ]
    y1[0].start()
    states(other, 1)
    y1[1].start()
    xr[x] = jnp.zeros((HALF, PIECE, STATE), F32)
    first.wait()
    own_decay = dec[h]
    par_decay = dpar[...]
    one = jnp.ones_like(own_decay)
    coef[0] = jnp.where(low, par_decay, one)
    coef[1] = jnp.where(low, one, own_decay)
    coef[2] = jnp.where(low, one, par_decay)
    coef[3] = jnp.where(low, own_decay, one)
    pair[...] = own_decay * par_decay
    zd[z] = own_decay * par_decay
    second = [push(pair, zd.at[z], d2s.at[d], d2r.at[d], peer) for d, peer in enumerate(zpeers)]
    for copy in second:
        copy.start()
    states(mine, 0)
    for c in range(2, CHUNKS):
        states(other, c)
    bt4[...] = square(proj_b.T)
    ct4[...] = square(proj_c.T)
    scores[...] = jnp.where(row_i >= col_i, fold(dot(wide(proj_c), bt4[...])), 0.0)
    pairacc[...] = jnp.zeros((TOK, TOK), F32)
    rowacc[...] = jnp.zeros((TOK, TOK), F32)
    for copy in second:
        copy.wait()
    row = zd[0]
    for k in range(1, NZ):
        row = row * zd[k]
    rd[x] = row
    third = [push(rd.at[x], rd.at[x], d3s.at[d], d3r.at[d], peer) for d, peer in enumerate(xpeers)]
    for copy in third:
        copy.start()

    def a_copies(c):
        heads = pl.ds(STARTS[c], SIZES_OF[c])
        copies = []
        for d, peer in enumerate(zpeers):
            pz = pl.multiple_of(lax.rem(z + d + 1, NZ) * PIECE, PIECE)
            copies.append(
                push(pq.at[:, heads, pl.ds(pz, PIECE)], arec.at[z, :, heads], as_.at[c, d], ar_.at[c, d], peer)
            )
        return copies

    def x_copies(c):
        heads = pl.ds(STARTS[c], SIZES_OF[c])
        copies = []
        for d, peer in enumerate(xpeers):
            px = lax.rem(x + d + 1, NX)
            back = jnp.where(px > x, 0, 1)
            copies.append(push(xs.at[back, heads], xr.at[x, heads], xss.at[c, d], xrs.at[c, d], peer))
        return copies

    def b_copies(c):
        heads = pl.ds(STARTS[c], SIZES_OF[c])
        here_rows = pl.ds(pl.multiple_of(z * PIECE, PIECE), PIECE)
        copies = []
        for d, peer in enumerate(zpeers):
            pz = lax.rem(z + d + 1, NZ)
            copies.append(
                push(bs.at[pz, :, heads], ps.at[:, heads, here_rows], bss.at[c, d], brs.at[c, d], peer)
            )
        return copies

    def y2_copy(c):
        return push(
            ys.at[:, pl.ds(STARTS[c], SIZES_OF[c])],
            car.at[:, pl.ds(mine + STARTS[c], SIZES_OF[c])],
            y2s.at[c], y2r.at[c], partner,
        )

    def pairs(c):
        y1[c].wait_recv()
        if c + 2 < CHUNKS:
            y1[c + 2].start()

        def head(i, carry):
            k = STARTS[c] + i
            at = pl.ds(k, 1)
            pq[0, k] = coef[0, at, :] * sr[0, mine + k] + coef[1, at, :] * par[0, k]
            pq[1, k] = coef[2, at, :] * sr[1, mine + k] + coef[3, at, :] * par[1, k]
            return carry

        lax.fori_loop(0, SIZES_OF[c], head, 0)
        heads = pl.ds(STARTS[c], SIZES_OF[c])
        own = pl.ds(pl.multiple_of(z * PIECE, PIECE), PIECE)
        arec[z, :, heads] = pq[:, heads, own, :]
        copies = a_copies(c)
        for d in FAR_FIRST:
            copies[d - 1].start()

    def totals(c):
        for copy in a_copies(c):
            copy.wait_recv()

        def head(i, carry):
            k = STARTS[c] + i
            at = pl.ds(k, 1)
            forward = arec[0, 0, k]
            backward = arec[NZ - 1, 1, k]
            for j in range(1, NZ):
                forward = zd[j, at, :] * forward + arec[j, 0, k]
                backward = zd[NZ - 1 - j, at, :] * backward + arec[NZ - 1 - j, 1, k]
            xs[0, k] = forward
            xs[1, k] = backward
            return carry

        lax.fori_loop(0, SIZES_OF[c], head, 0)
        for copy in x_copies(c):
            copy.start()

    def prefixes(c):
        if c == 0:
            for copy in third:
                copy.wait()
        for copy in x_copies(c):
            copy.wait_recv()

        def head(i, carry):
            k = STARTS[c] + i
            at = pl.ds(k, 1)
            forward = jnp.zeros((PIECE, STATE), jnp.float32)
            backward = jnp.zeros((PIECE, STATE), jnp.float32)
            for j in range(NX):
                forward = jnp.where(j < x, rd[j, at, :] * forward + xr[j, k], forward)
                m = NX - 1 - j
                backward = jnp.where(m > x, rd[m, at, :] * backward + xr[m, k], backward)
            for j in range(NZ):
                bs[j, 0, k] = forward
                forward = zd[j, at, :] * forward + arec[j, 0, k]
                m = NZ - 1 - j
                bs[m, 1, k] = backward
                backward = zd[m, at, :] * backward + arec[m, 1, k]
            return carry

        lax.fori_loop(0, SIZES_OF[c], head, 0)
        heads = pl.ds(STARTS[c], SIZES_OF[c])
        own = pl.ds(pl.multiple_of(z * PIECE, PIECE), PIECE)
        ps[:, heads, own, :] = bs[z, :, heads]
        copies = b_copies(c)
        for d in FAR_FIRST:
            copies[d - 1].start()

    def finals(c):
        for copy in b_copies(c):
            copy.wait_recv()

        def head(i, carry):
            k = STARTS[c] + i
            at = pl.ds(k, 1)
            before, after = ps[0, k], ps[1, k]
            zero = jnp.zeros_like(before)
            ys[0, k] = coef[3, at, :] * before + jnp.where(low, sr[0, mine + k], zero)
            ys[1, k] = coef[1, at, :] * after + jnp.where(low, zero, sr[1, mine + k])
            car[0, mine + k] = coef[2, at, :] * before + jnp.where(low, zero, par[0, k])
            car[1, mine + k] = coef[0, at, :] * after + jnp.where(low, par[1, k], zero)
            return carry

        lax.fori_loop(0, SIZES_OF[c], head, 0)
        y2_copy(c).start()


    def within(start, count):
        def two(i, carry):
            for j in range(2):
                k = start + 2 * i + j
                at = pl.ds(pl.multiple_of(k * WIDTH, WIDTH), WIDTH)
                gk = gt[at, :]
                dots = dot_tn(gk, xt[at, :])
                across = jnp.broadcast_to(rows_cum[k], (TOK, TOK))
                table = jnp.exp(jnp.minimum(across.T - across, 0.0))
                weight = table * scores[...]
                inner[at, :] = fold(dot(gk, wide(weight)))
                terms = weight * dots
                rows_col[k] = jnp.sum(terms, axis=0, keepdims=True)
                pairacc[...] += table * dots * rows_dt[k]
                sums = jnp.sum(terms * rows_dt[k], axis=1, keepdims=True)
                rowacc[...] = jnp.where(col_i == k, sums, rowacc[...])
            return carry

        lax.fori_loop(0, count // 2, two, 0)

    gbacc[...] = jnp.zeros((2 * TOK, 2 * TOK), F32)
    gcacc[...] = jnp.zeros((2 * TOK, 2 * TOK), F32)

    def outputs(start, c):
        count, block = SIZES_OF[c], SIZES_OF[c] * WIDTH
        at = pl.multiple_of((start + STARTS[c]) * WIDTH, 2 * WIDTH)
        heads = pl.ds(start + STARTS[c], count)
        rows_at = pl.ds(at, block)
        ci = car[0, heads]
        co = car[1, heads]
        rows_cross[heads] = jnp.sum(ci * co, axis=1, keepdims=True)
        ciw = wide(ci.reshape(block, STATE))
        cow = wide(co.reshape(block, STATE))
        back = fold(dot(cow, bt4[...])).reshape(count, WIDTH, TOK)
        front = fold(dot(ciw, ct4[...])).reshape(count, WIDTH, TOK)
        gbacc[...] += dot_tn(xw[rows_at, :], cow)
        gcacc[...] += dot_tn(gw[rows_at, :], ciw)
        xf = xt[rows_at, :].astype(F32).reshape(count, WIDTH, TOK)
        gf = gt[rows_at, :].astype(F32).reshape(count, WIDTH, TOK)
        rows_xb[heads] = jnp.sum(xf * back, axis=1, keepdims=True)
        rows_gf[heads] = jnp.sum(gf * front, axis=1, keepdims=True)
        rows_gx[heads] = jnp.sum(gf * xf, axis=1, keepdims=True)
        total = inner[rows_at, :].reshape(count, WIDTH, TOK) + rows_te[heads] * back
        gx = rows_dt[heads] * total + rows_skip[heads] * gf
        gx_ref[:, pl.ds(at, block)] = gx.reshape(block, TOK).T.astype(BF16)

    work = [(half + n, 4) for half in (other, mine) for n in range(0, HALF, 4)]

    def fill(n):
        for _ in range(min(n, len(work))):
            within(*work.pop(0))

    fill(1)
    for c in range(1, CHUNKS):
        states(mine, c)
    fill(1)
    for step in range(CHUNKS + 3):
        if step < CHUNKS:
            pairs(step)
        if 0 <= step - 1 < CHUNKS:
            totals(step - 1)
        if 0 <= step - 2 < CHUNKS:
            prefixes(step - 2)
        if 0 <= step - 3 < CHUNKS:
            finals(step - 3)
        if step < 3:
            fill(1)
        elif step == 3:
            fill(10)
            outputs(mine, 0)
        else:
            outputs(mine, step - 3)
        if step == 5:
            for j in range(0, MODEL, 512):
                ut[j : j + 512, :] = u_ref[:, j : j + 512].T
    for c in range(CHUNKS):
        y2_copy(c).wait_recv()
        outputs(other, c)

    sums = pairacc[...]
    sums = jnp.where(row_i >= col_i, sums, 0.0)
    sumw = wide(sums)
    acc = gbacc[...] + dot_tn(sumw, wide(dot(u_ref[...], wc_ref[...])))
    acc = acc[:TOK] + acc[TOK:]
    grad_b = fold(acc)
    acc = gcacc[...]
    acc = acc[:TOK] + acc[TOK:]
    grad_c = fold(acc) + fold(dot(sumw, b4[...]))

    def flat(ref):
        return ref[...].reshape(HEADS, TOK)

    dt = flat_dt[...]
    raw = flat_raw[...]
    end = flat(rows_te)
    rate = -jnp.exp(alog)
    col = flat(rows_col)
    xb = end * flat(rows_xb)
    direct = col + xb
    own_out = dt * xb
    own_in = flat(rows_fs) * flat(rows_gf)
    cross = flat(rows_fs)[:, TOK - 1 :] * jnp.sum(flat(rows_cross), axis=1, keepdims=True)
    change = rowacc[...].T[:HEADS] - dt * col + own_in - own_out
    lanes = lax.broadcasted_iota(jnp.int32, (HEADS, TOK), 1)
    edge = cross + jnp.sum(own_out, axis=1, keepdims=True)
    change = change + jnp.where(lanes == TOK - 1, edge, 0.0)
    grad_log = jnp.dot(change, since, precision=lax.Precision.HIGHEST, preferred_element_type=F32)
    grad_raw = (direct + grad_log * rate) * (1.0 / (1.0 + jnp.exp(-raw)))
    grad_bias = jnp.sum(grad_raw, axis=1, keepdims=True)
    grad_alog = jnp.sum(grad_log * dt, axis=1, keepdims=True) * rate
    grad_skip = jnp.sum(flat(rows_gx), axis=1, keepdims=True)
    extra = jnp.where(lanes == 0, grad_bias, jnp.where(lanes == 1, grad_alog, jnp.where(lanes == 2, grad_skip, 0.0)))
    extra = padded(extra).T[:8]
    grad_d = padded(grad_raw).T
    bw, cw, dw = wide(grad_b), wide(grad_c), wide(grad_d)

    cs, cr, x0s, x0r, y0s, y0r, z0s, z0r, y3s, y3r, z1s, z1r, x1s, x1r, z2s, z2r, x2s, x2r, y4s, y4r, ls, lr = red_sems
    keep = pl.multiple_of(core * 48, 8)
    give = pl.multiple_of((1 - core) * 48, 8)

    def swap(i):
        return push(grad.at[i, :, :, pl.ds(give, 48)], c_rec.at[i], cs.at[i], cr.at[i], cpeer)

    def weights(i, carry):
        at = pl.ds(pl.multiple_of(i * 640, 640), 640)
        cols = ut[at, :]
        grad[i, :, :, 0:40, :] = fold(dot(cols, bw)).reshape(NZ, 2, 40, 128)
        grad[i, :, :, 40:80, :] = fold(dot(cols, cw)).reshape(NZ, 2, 40, 128)
        gwd[...] = fold(dot(cols, dw))
        for s in range(16):
            third_part = jnp.concatenate([gwd[s * 40 + 32 : s * 40 + 40, :], extra], axis=0)
            packed = gwd[s * 40 : s * 40 + 16, :]
            packed = packed + pltpu.roll(gwd[s * 40 + 16 : s * 40 + 32, :], 40, 1)
            grad[i, s // 2, s % 2, 80:96, :] = packed + pltpu.roll(third_part, 80, 1)
        swap(i).start()
        return carry

    lax.fori_loop(0, NX, weights, 0)
    out = fin
    bt, ctall, dtall = tall(grad_b), tall(grad_c), tall(grad_d)[:, :HEADS]
    both_t = jnp.concatenate([bt, ctall], axis=1)

    def model_grads(i, carry):
        at = pl.ds(pl.multiple_of(i * 512, 512), 512)
        both_w = jnp.concatenate([wb_ref[at, :], wc_ref[at, :]], axis=1)
        p = dot_nt(both_t, both_w) + dot(dtall, wd_ref[:, at])
        gu_ref[:, at] = (p[:TOK] + p[TOK:]).astype(BF16)
        return carry

    lax.fori_loop(0, 1, model_grads, 0)
    for i in range(NX):
        swap(i).wait()
        h1[i] = grad[i, :, :, pl.ds(keep, 48), :] + c_rec[i]

    def part(start, there):
        return pl.ds(pl.multiple_of(start + 8 * lax.rem(there, 2), 8), 8)

    def begin(copies):
        for copy in copies:
            copy.start()
        return copies

    def arrived(copies):
        for copy in copies:
            copy.wait_recv()

    znext = [lax.rem(z + d, NZ) for d in range(1, NZ)]
    xnext = [lax.rem(x + d, NX) for d in range(1, NX)]
    z_one = begin([push(h1.at[:, t, :, pl.ds(32, 16)], c0.at[z], z0s.at[d], z0r.at[d], zpeers[d]) for d, t in enumerate(znext)])
    x_one = begin([push(h1.at[t, :, :, pl.ds(0, 16)], a0.at[x], x0s.at[d], x0r.at[d], xpeers[d]) for d, t in enumerate(xnext)])
    y_one = begin([push(h1.at[:, :, t // 2, part(16, t)], b0.at[y], y0s.at[d], y0r.at[d], ypeers[d]) for d, t in enumerate(ynext)])
    lax.fori_loop(1, 5, model_grads, 0)
    arrived(x_one)
    total = h1[x, :, :, pl.ds(0, 16), :]
    for t in xnext:
        total = total + a0[t]
    a1[...] = total
    y_two = begin([push(a1.at[:, t // 2, part(0, t)], a1r.at[y], y3s.at[d], y3r.at[d], ypeers[d]) for d, t in enumerate(ynext)])
    arrived(y_one)
    total = h1[:, :, h, part(16, yl), :]
    for t in ynext:
        total = total + b0[t]
    b1[...] = total
    z_two = begin([push(b1.at[:, t], b1r.at[z], z1s.at[d], z1r.at[d], zpeers[d]) for d, t in enumerate(znext)])
    arrived(z_one)
    total = h1[:, z, :, pl.ds(32, 16), :]
    for t in znext:
        total = total + c0[t]
    c1[...] = total
    x_two = begin([push(c1.at[t], c1r.at[x], x1s.at[d], x1r.at[d], xpeers[d]) for d, t in enumerate(xnext)])
    arrived(y_two)
    total = a1[:, h, part(0, yl), :]
    for t in ynext:
        total = total + a1r[t]
    a2[...] = total
    z_three = begin([push(a2.at[t], a2r.at[z], z2s.at[d], z2r.at[d], zpeers[d]) for d, t in enumerate(znext)])
    arrived(z_two)
    total = b1[:, z]
    for t in znext:
        total = total + b1r[t]
    b2[...] = total
    x_three = begin([push(b2.at[t], b2r.at[x], x2s.at[d], x2r.at[d], xpeers[d]) for d, t in enumerate(xnext)])
    arrived(x_two)
    total = c1[x]
    for t in xnext:
        total = total + c1r[t]
    c2[...] = total
    y_three = begin([push(c2.at[t // 2, part(0, t)], c2r.at[y], y4s.at[d], y4r.at[d], ypeers[d]) for d, t in enumerate(ynext)])
    arrived(z_three)
    total = a2[z]
    for t in znext:
        total = total + a2r[t]
    out[core, 0, yl] = total
    arrived(x_three)
    total = b2[x]
    for t in xnext:
        total = total + b2r[t]
    out[core, 1, yl] = total
    arrived(y_three)
    total = c2[h, part(0, yl), :]
    for t in ynext:
        total = total + c2r[t]
    out[core, 2, yl] = total
    last = begin([push(out.at[core, :, yl], out.at[core, :, yl], ls.at[d], lr.at[d], peer) for d, peer in enumerate(dpeers)])
    for copy in last:
        copy.wait()

    whole = fin[...].reshape(ROWS, 128)
    gbw_ref[...] = whole[:40]
    gcw_ref[...] = whole[40:80]
    tail = whole[80:]
    gdw_ref[0:16, :] = tail[:, :HEADS]
    gdw_ref[16:32, :] = tail[:, 40:80]
    tail = tail[:, 80:120]
    gdw_ref[32:40, :] = tail[:8]
    ex_ref[...] = tail[8:]
    for c in range(CHUNKS):
        y1[c].wait_send()
        for copy in a_copies(c) + x_copies(c) + b_copies(c):
            copy.wait_send()
        y2_copy(c).wait_send()
    for copy in x_one + y_one + z_one + x_two + y_two + z_two + x_three + y_three + z_three:
        copy.wait_send()


def layer(u, x, g, wb, wc, wd, bias, alog, skip):
    vmem = pl.BlockSpec(memory_space=pltpu.VMEM)
    dma = pltpu.SemaphoreType.DMA
    half = (2, HALF, WIDTH, STATE)

    def f32(*shape):
        return pltpu.VMEM(shape + (128,), F32)

    def b16(*shape):
        return pltpu.VMEM(shape, BF16)

    def sems(counts):
        pairs = []
        for n in counts:
            pairs += [dma if n == () else dma(n)] * 2
        return pairs

    shape = jax.ShapeDtypeStruct
    return pl.pallas_call(
        layer_kernel,
        out_shape=(
            shape((TOK, MODEL), BF16), shape((TOK, MODEL), BF16), shape((40, STATE), F32),
            shape((40, STATE), F32), shape((40, HEADS), F32), shape((8, HEADS), F32),
        ),
        in_specs=[vmem] * 9,
        out_specs=(vmem,) * 6,
        scratch_shapes=[
            b16(MODEL, TOK), b16(MODEL, TOK), b16(MODEL, TOK), b16(MODEL, 256), b16(MODEL, 256),
            b16(256, 256), b16(256, 256), b16(256, 256), b16(256, 256),
            f32(TOK), f32(TOK), f32(TOK), f32(MODEL), pltpu.VMEM((256, 256), F32), pltpu.VMEM((256, 256), F32),
        ] + [f32(HEADS, 1)] * 11 + [
            f32(HEADS), f32(HEADS), f32(640),
            f32(2, HEADS, WIDTH), f32(2, 24), f32(2, HEADS, WIDTH),
            f32(*half[:3]), f32(*half[:3]),
            f32(NZ, 2, HALF, PIECE), f32(2, HALF, PIECE), f32(NX, HALF, PIECE), f32(NZ, 2, HALF, PIECE),
            f32(*half[:3]), f32(*half[:3]),
            f32(24), f32(4, 24), f32(24), f32(NZ, 24), f32(NX, 24),
            f32(NX, NZ, 2, ROWS), f32(4, 8, 2, 48), f32(4, 8, 2, 48),
            f32(4, 8, 2, 16), f32(8, 2, 16), f32(4, 8, 8), f32(8, 8), f32(8, 8),
            f32(4, 4, 8, 8), f32(4, 8, 8), f32(8, 4, 8), f32(4, 8), f32(4, 8),
            f32(8, 4, 2, 16), f32(4, 2, 16), f32(4, 2, 16), f32(2, 16), f32(4, 8),
            f32(2, 3, 2, 8),
        ] + sems(
            [(CHUNKS,), (CHUNKS, NZ - 1), (CHUNKS, NX - 1), (CHUNKS, NZ - 1), (CHUNKS,), (), (NZ - 1,), (NX - 1,)]
        ) + sems([(4,), (3,), (3,), (7,), (3,), (7,), (3,), (7,), (3,), (3,), (3,)]),
        compiler_params=pltpu.CompilerParams(
            collective_id=0, has_side_effects=True, vmem_limit_bytes=60 << 20
        ),
        name="layer",
    )(u, x, g, wb, wc, wd, bias, alog, skip)


def body(layer_input, ssm_input, out_grad, b_weight, c_weight, dt_weight, dt_bias, a_log, d_skip):
    gx, gu, gb, gc, gd, extra = layer(
        layer_input, ssm_input, out_grad, b_weight, c_weight, dt_weight.T,
        dt_bias[None], a_log[None], d_skip[None],
    )
    return gx, gu, gb, gc, gd, extra[0], extra[1], extra[2]


def solution(mesh):
    split_mesh = Mesh(mesh.devices.reshape(4, 8, 2, 2, 2), AXES)
    cut, whole = P(DP_SEQ, None), P()
    return jax.shard_map(
        body,
        mesh=split_mesh,
        in_specs=(cut, cut, cut) + (whole,) * 6,
        out_specs=(cut, cut) + (P(SEQ, None),) * 3 + (whole,) * 3,
        check_vma=False,
    )
```

```python
import jax
import jax.numpy as jnp
from jax import lax
from jax.experimental import pallas as pl
from jax.experimental.pallas import tpu as pltpu
from jax.sharding import Mesh
from jax.sharding import PartitionSpec as P

SEQ = ("x", "z", "yh")
DP_SEQ = ("yl", "core", "x", "z", "yh")
AXES = ("x", "z", "yh", "yl", "core")
SIZES = {"x": 4, "z": 8, "yh": 2, "yl": 2, "core": 2}
MESH = pl.DeviceIdType.MESH
HEADS, WIDTH, STATE = 40, 64, 128
HALF = HEADS // 2
SIZES_OF = (2, 4, 4, 4, 4, 2)
STARTS = tuple(sum(SIZES_OF[:c]) for c in range(len(SIZES_OF)))
CHUNKS = len(SIZES_OF)
NX, NZ = SIZES["x"], SIZES["z"]
PIECE = WIDTH // NZ
FAR_FIRST = (4, 3, 5, 2, 6, 1, 7)


def place():
    return {axis: lax.axis_index(axis) for axis in AXES}


def shifted(here, **steps):
    there = dict(here)
    for axis, step in steps.items():
        there[axis] = lax.rem(here[axis] + step, SIZES[axis])
    return tuple(there[axis] for axis in AXES)


def greet(peers):
    barrier = pltpu.get_barrier_semaphore()
    for peer in peers:
        pl.semaphore_signal(barrier, inc=1, device_id=peer, device_id_type=MESH)
    pl.semaphore_wait(barrier, len(peers))


def push(src, dst, send, recv, peer):
    return pltpu.make_async_remote_copy(
        src_ref=src, dst_ref=dst, send_sem=send, recv_sem=recv, device_id=peer, device_id_type=MESH
    )


TOK = 128
MODEL = 2560
F32, BF16 = jnp.float32, jnp.bfloat16


def dot(a, b):
    return jnp.dot(a, b, preferred_element_type=F32)


def dot_tn(a, b):
    return lax.dot_general(a, b, (((0,), (0,)), ((), ())), preferred_element_type=F32)


def dot_nt(a, b):
    return lax.dot_general(a, b, (((1,), (1,)), ((), ())), preferred_element_type=F32)


def split(v):
    top = v.astype(BF16)
    return top, (v - top.astype(F32)).astype(BF16)


def wide(v):
    return jnp.concatenate(split(v), axis=1)


def tall(v):
    return jnp.concatenate(split(v), axis=0)


def square(v):
    w = wide(v)
    return jnp.concatenate([w, w], axis=0)


def fold(p):
    return p[:, :128] + p[:, 128:]


def padded(v):
    return jnp.concatenate([v, jnp.zeros((TOK - v.shape[0], TOK), F32)], axis=0)


def layer_kernel(
    u_ref, x_ref, g_ref, wb_ref, wc_ref, wd_ref, bias_ref, alog_ref, skip_ref,
    gx_ref, gu_ref, gbw_ref, gcw_ref, gdw_ref, ex_ref,
    xt, gt, ut, xw, gw, b4, c4, bt4, ct4, scores, pairacc, rowacc, inner, gbacc, gcacc,
    rows_dt, rows_ws, rows_fs, rows_te, rows_cum, rows_skip, rows_col, rows_xb, rows_gf, rows_cross, rows_gx,
    flat_dt, flat_raw, gwd, sr, dec, car, par, pq, arec, xs, xr, bs, ps, ys, dpar, coef, pair, zd, rd,
    us, ur, gs, gr, h1, a0, a1, a1r, a2, a2r, b0, b1, b1r, b2, b2r, c0, c1, c1r, c2, c2r, fin,
    *sems,
):
    here = place()
    x, z, h, yl, core = (here[a] for a in AXES)
    y = h * 2 + yl
    low = h == 0
    mine, other = h * HALF, (1 - h) * HALF
    partner = shifted(here, yh=1)
    cpeer = shifted(here, core=1)
    dpeers = [cpeer, shifted(here, yl=1), shifted(here, yl=1, core=1)]
    zpeers = [shifted(here, z=d) for d in range(1, NZ)]
    xpeers = [shifted(here, x=d) for d in range(1, NX)]
    ynext = [lax.rem(y + d, 4) for d in range(1, 4)]
    ypeers = [(x, z, t // 2, lax.rem(t, 2), core) for t in ynext]
    peers = [cpeer, dpeers[2]] + ypeers + zpeers + xpeers
    scan_sems, red_sems = sems[:16], sems[16:]
    y1s, y1r, as_, ar_, xss, xrs, bss, brs, y2s, y2r, d1s, d1r, d2s, d2r, d3s, d3r = scan_sems
    cs, cr, x0s, x0r, y0s, y0r, z0s, z0r, y3s, y3r, z1s, z1r, x1s, x1r, z2s, z2r, x2s, x2r, y4s, y4r, ls, lr, us_sem, ur_sem = red_sems
    barrier = pltpu.get_barrier_semaphore()
    for peer in peers:
        pl.semaphore_signal(barrier, inc=1, device_id=peer, device_id_type=MESH)

    u = u_ref[...]
    columns = jnp.concatenate([bias_ref[...], alog_ref[...], skip_ref[...], jnp.zeros((5, HEADS), F32)], axis=0)
    columns = jnp.concatenate([columns, jnp.zeros((8, TOK - HEADS), F32)], axis=1)
    columns = padded(columns).T[:HEADS]
    alog = columns[:, 1:2]
    raw = dot_nt(wd_ref[...], u) + columns[:, 0:1]
    small = jnp.exp(-jnp.abs(raw))
    above = 1.0 + small
    gap = above - 1.0
    log_part = jnp.where(gap == 0.0, small, jnp.log(above) * (small / jnp.where(gap == 0.0, 1.0, gap)))
    dt = jnp.maximum(raw, 0.0) + log_part
    rate = -jnp.exp(alog)
    row_i = lax.broadcasted_iota(jnp.int32, (TOK, TOK), 0)
    col_i = lax.broadcasted_iota(jnp.int32, (TOK, TOK), 1)
    upto = (row_i <= col_i).astype(F32)
    since = (row_i >= col_i).astype(F32)
    cum = jnp.dot(dt * rate, upto, precision=lax.Precision.HIGHEST, preferred_element_type=F32)
    last = cum[:, TOK - 1 :]
    to_end = jnp.exp(last - cum)
    from_start = jnp.exp(cum)
    flat_dt[...] = dt
    flat_raw[...] = raw

    def rows(v):
        return v.reshape(HEADS, 1, TOK)

    rows_dt[...] = rows(dt)
    rows_ws[...] = rows(to_end * dt)
    rows_fs[...] = rows(from_start)
    rows_te[...] = rows(to_end)
    rows_cum[...] = rows(cum)
    rows_skip[...] = rows(jnp.broadcast_to(columns[:, 2:3], (HEADS, TOK)))
    decay = jnp.broadcast_to(jnp.exp(last), (HEADS, STATE))
    fill = jnp.ones((4, STATE), F32)
    dec[0] = jnp.concatenate([decay[:HALF], fill], axis=0)
    dec[1] = jnp.concatenate([decay[HALF:], fill], axis=0)
    proj_b = dot(u, wb_ref[...])
    proj_c = dot(u, wc_ref[...])
    b4[...] = square(proj_b)
    c4[...] = square(proj_c)

    def states(start, c):
        count, block = SIZES_OF[c], SIZES_OF[c] * WIDTH
        at = pl.multiple_of((start + STARTS[c]) * WIDTH, 2 * WIDTH)
        heads = pl.ds(start + STARTS[c], count)
        rows_at = pl.ds(at, block)
        xc = x_ref[:, pl.ds(at, block)].T
        gc = g_ref[:, pl.ds(at, block)].T
        xt[rows_at, :] = xc
        gt[rows_at, :] = gc
        xsc = xc.astype(F32).reshape(count, WIDTH, TOK) * rows_ws[heads]
        gsc = gc.astype(F32).reshape(count, WIDTH, TOK) * rows_fs[heads]
        xwc = wide(xsc.reshape(block, TOK))
        gwc = wide(gsc.reshape(block, TOK))
        xw[rows_at, :] = xwc
        gw[rows_at, :] = gwc
        sr[0, heads] = fold(dot(xwc, b4[...])).reshape(count, WIDTH, STATE)
        sr[1, heads] = fold(dot(gwc, c4[...])).reshape(count, WIDTH, STATE)

    states(other, 0)
    pl.semaphore_wait(barrier, len(peers))
    first = push(dec.at[1 - h], dpar, d1s, d1r, partner)
    first.start()
    y1 = [
        push(
            sr.at[:, pl.ds(other + STARTS[c], SIZES_OF[c])],
            par.at[:, pl.ds(STARTS[c], SIZES_OF[c])],
            y1s.at[c], y1r.at[c], partner,
        )
        for c in range(CHUNKS)
    ]
    y1[0].start()
    us[...] = u.astype(F32)
    u_swap = push(us, ur, us_sem, ur_sem, cpeer)
    u_swap.start()
    states(other, 1)
    y1[1].start()
    xr[x] = jnp.zeros((HALF, PIECE, STATE), F32)
    first.wait()
    own_decay = dec[h]
    par_decay = dpar[...]
    one = jnp.ones_like(own_decay)
    coef[0] = jnp.where(low, par_decay, one)
    coef[1] = jnp.where(low, one, own_decay)
    coef[2] = jnp.where(low, one, par_decay)
    coef[3] = jnp.where(low, own_decay, one)
    pair[...] = own_decay * par_decay
    zd[z] = own_decay * par_decay
    second = [push(pair, zd.at[z], d2s.at[d], d2r.at[d], peer) for d, peer in enumerate(zpeers)]
    for copy in second:
        copy.start()
    states(mine, 0)
    for c in range(2, CHUNKS):
        states(other, c)
    bt4[...] = square(proj_b.T)
    ct4[...] = square(proj_c.T)
    scores[...] = jnp.where(row_i >= col_i, fold(dot(wide(proj_c), bt4[...])), 0.0)
    pairacc[...] = jnp.zeros((TOK, TOK), F32)
    rowacc[...] = jnp.zeros((TOK, TOK), F32)
    for copy in second:
        copy.wait()
    row = zd[0]
    for k in range(1, NZ):
        row = row * zd[k]
    rd[x] = row
    third = [push(rd.at[x], rd.at[x], d3s.at[d], d3r.at[d], peer) for d, peer in enumerate(xpeers)]
    for copy in third:
        copy.start()

    def a_copies(c):
        heads = pl.ds(STARTS[c], SIZES_OF[c])
        copies = []
        for d, peer in enumerate(zpeers):
            pz = pl.multiple_of(lax.rem(z + d + 1, NZ) * PIECE, PIECE)
            copies.append(
                push(pq.at[:, heads, pl.ds(pz, PIECE)], arec.at[z, :, heads], as_.at[c, d], ar_.at[c, d], peer)
            )
        return copies

    def x_copies(c):
        heads = pl.ds(STARTS[c], SIZES_OF[c])
        copies = []
        for d, peer in enumerate(xpeers):
            px = lax.rem(x + d + 1, NX)
            back = jnp.where(px > x, 0, 1)
            copies.append(push(xs.at[back, heads], xr.at[x, heads], xss.at[c, d], xrs.at[c, d], peer))
        return copies

    def b_copies(c):
        heads = pl.ds(STARTS[c], SIZES_OF[c])
        here_rows = pl.ds(pl.multiple_of(z * PIECE, PIECE), PIECE)
        copies = []
        for d, peer in enumerate(zpeers):
            pz = lax.rem(z + d + 1, NZ)
            copies.append(
                push(bs.at[pz, :, heads], ps.at[:, heads, here_rows], bss.at[c, d], brs.at[c, d], peer)
            )
        return copies

    def y2_copy(c):
        return push(
            ys.at[:, pl.ds(STARTS[c], SIZES_OF[c])],
            car.at[:, pl.ds(mine + STARTS[c], SIZES_OF[c])],
            y2s.at[c], y2r.at[c], partner,
        )

    def pairs(c):
        y1[c].wait_recv()
        if c + 2 < CHUNKS:
            y1[c + 2].start()

        def head(i, carry):
            k = STARTS[c] + i
            at = pl.ds(k, 1)
            pq[0, k] = coef[0, at, :] * sr[0, mine + k] + coef[1, at, :] * par[0, k]
            pq[1, k] = coef[2, at, :] * sr[1, mine + k] + coef[3, at, :] * par[1, k]
            return carry

        lax.fori_loop(0, SIZES_OF[c], head, 0)
        heads = pl.ds(STARTS[c], SIZES_OF[c])
        own = pl.ds(pl.multiple_of(z * PIECE, PIECE), PIECE)
        arec[z, :, heads] = pq[:, heads, own, :]
        copies = a_copies(c)
        for d in FAR_FIRST:
            copies[d - 1].start()

    def totals(c):
        for copy in a_copies(c):
            copy.wait_recv()

        def head(i, carry):
            k = STARTS[c] + i
            at = pl.ds(k, 1)
            forward = arec[0, 0, k]
            backward = arec[NZ - 1, 1, k]
            for j in range(1, NZ):
                forward = zd[j, at, :] * forward + arec[j, 0, k]
                backward = zd[NZ - 1 - j, at, :] * backward + arec[NZ - 1 - j, 1, k]
            xs[0, k] = forward
            xs[1, k] = backward
            return carry

        lax.fori_loop(0, SIZES_OF[c], head, 0)
        for copy in x_copies(c):
            copy.start()

    def prefixes(c):
        if c == 0:
            for copy in third:
                copy.wait()
        for copy in x_copies(c):
            copy.wait_recv()

        def head(i, carry):
            k = STARTS[c] + i
            at = pl.ds(k, 1)
            forward = jnp.zeros((PIECE, STATE), jnp.float32)
            backward = jnp.zeros((PIECE, STATE), jnp.float32)
            for j in range(NX):
                forward = jnp.where(j < x, rd[j, at, :] * forward + xr[j, k], forward)
                m = NX - 1 - j
                backward = jnp.where(m > x, rd[m, at, :] * backward + xr[m, k], backward)
            for j in range(NZ):
                bs[j, 0, k] = forward
                forward = zd[j, at, :] * forward + arec[j, 0, k]
                m = NZ - 1 - j
                bs[m, 1, k] = backward
                backward = zd[m, at, :] * backward + arec[m, 1, k]
            return carry

        lax.fori_loop(0, SIZES_OF[c], head, 0)
        heads = pl.ds(STARTS[c], SIZES_OF[c])
        own = pl.ds(pl.multiple_of(z * PIECE, PIECE), PIECE)
        ps[:, heads, own, :] = bs[z, :, heads]
        copies = b_copies(c)
        for d in FAR_FIRST:
            copies[d - 1].start()

    def finals(c):
        for copy in b_copies(c):
            copy.wait_recv()

        def head(i, carry):
            k = STARTS[c] + i
            at = pl.ds(k, 1)
            before, after = ps[0, k], ps[1, k]
            zero = jnp.zeros_like(before)
            ys[0, k] = coef[3, at, :] * before + jnp.where(low, sr[0, mine + k], zero)
            ys[1, k] = coef[1, at, :] * after + jnp.where(low, zero, sr[1, mine + k])
            car[0, mine + k] = coef[2, at, :] * before + jnp.where(low, zero, par[0, k])
            car[1, mine + k] = coef[0, at, :] * after + jnp.where(low, par[1, k], zero)
            return carry

        lax.fori_loop(0, SIZES_OF[c], head, 0)
        y2_copy(c).start()


    def within(start, count):
        def two(i, carry):
            for j in range(2):
                k = start + 2 * i + j
                at = pl.ds(pl.multiple_of(k * WIDTH, WIDTH), WIDTH)
                gk = gt[at, :]
                dots = dot_tn(gk, xt[at, :])
                across = jnp.broadcast_to(rows_cum[k], (TOK, TOK))
                table = jnp.exp(jnp.minimum(across.T - across, 0.0))
                weight = table * scores[...]
                inner[at, :] = fold(dot(gk, wide(weight)))
                terms = weight * dots
                rows_col[k] = jnp.sum(terms, axis=0, keepdims=True)
                pairacc[...] += table * dots * rows_dt[k]
                sums = jnp.sum(terms * rows_dt[k], axis=1, keepdims=True)
                rowacc[...] = jnp.where(col_i == k, sums, rowacc[...])
            return carry

        lax.fori_loop(0, count // 2, two, 0)

    gbacc[...] = jnp.zeros((2 * TOK, 2 * TOK), F32)
    gcacc[...] = jnp.zeros((2 * TOK, 2 * TOK), F32)

    def outputs(start, c):
        count, block = SIZES_OF[c], SIZES_OF[c] * WIDTH
        at = pl.multiple_of((start + STARTS[c]) * WIDTH, 2 * WIDTH)
        heads = pl.ds(start + STARTS[c], count)
        rows_at = pl.ds(at, block)
        ci = car[0, heads]
        co = car[1, heads]
        rows_cross[heads] = jnp.sum(ci * co, axis=1, keepdims=True)
        ciw = wide(ci.reshape(block, STATE))
        cow = wide(co.reshape(block, STATE))
        back = fold(dot(cow, bt4[...])).reshape(count, WIDTH, TOK)
        front = fold(dot(ciw, ct4[...])).reshape(count, WIDTH, TOK)
        gbacc[...] += dot_tn(xw[rows_at, :], cow)
        gcacc[...] += dot_tn(gw[rows_at, :], ciw)
        xf = xt[rows_at, :].astype(F32).reshape(count, WIDTH, TOK)
        gf = gt[rows_at, :].astype(F32).reshape(count, WIDTH, TOK)
        rows_xb[heads] = jnp.sum(xf * back, axis=1, keepdims=True)
        rows_gf[heads] = jnp.sum(gf * front, axis=1, keepdims=True)
        rows_gx[heads] = jnp.sum(gf * xf, axis=1, keepdims=True)
        total = inner[rows_at, :].reshape(count, WIDTH, TOK) + rows_te[heads] * back
        gx = rows_dt[heads] * total + rows_skip[heads] * gf
        gx_ref[:, pl.ds(at, block)] = gx.reshape(block, TOK).T.astype(BF16)

    work = [(half + n, 4) for half in (other, mine) for n in range(0, HALF, 4)]

    def fill(n):
        for _ in range(min(n, len(work))):
            within(*work.pop(0))

    fill(1)
    for c in range(1, CHUNKS):
        states(mine, c)
    fill(1)
    for step in range(CHUNKS + 3):
        if step < CHUNKS:
            pairs(step)
        if 0 <= step - 1 < CHUNKS:
            totals(step - 1)
        if 0 <= step - 2 < CHUNKS:
            prefixes(step - 2)
        if 0 <= step - 3 < CHUNKS:
            finals(step - 3)
        if step < 3:
            fill(1)
        elif step == 3:
            fill(10)
            outputs(mine, 0)
        else:
            outputs(mine, step - 3)
        if step == 5:
            u_swap.wait()
            for j in range(0, MODEL, 512):
                ut[j : j + 512, :TOK] = u_ref[:, j : j + 512].T
                ut[j : j + 512, TOK:] = ur[:, j : j + 512].astype(BF16).T
    for c in range(CHUNKS):
        y2_copy(c).wait_recv()
        outputs(other, c)

    sums = pairacc[...]
    sums = jnp.where(row_i >= col_i, sums, 0.0)
    sumw = wide(sums)
    acc = gbacc[...] + dot_tn(sumw, wide(dot(u_ref[...], wc_ref[...])))
    acc = acc[:TOK] + acc[TOK:]
    grad_b = fold(acc)
    acc = gcacc[...]
    acc = acc[:TOK] + acc[TOK:]
    grad_c = fold(acc) + fold(dot(sumw, b4[...]))

    def flat(ref):
        return ref[...].reshape(HEADS, TOK)

    dt = flat_dt[...]
    raw = flat_raw[...]
    end = flat(rows_te)
    rate = -jnp.exp(alog)
    col = flat(rows_col)
    xb = end * flat(rows_xb)
    direct = col + xb
    own_out = dt * xb
    own_in = flat(rows_fs) * flat(rows_gf)
    cross = flat(rows_fs)[:, TOK - 1 :] * jnp.sum(flat(rows_cross), axis=1, keepdims=True)
    change = rowacc[...].T[:HEADS] - dt * col + own_in - own_out
    lanes = lax.broadcasted_iota(jnp.int32, (HEADS, TOK), 1)
    edge = cross + jnp.sum(own_out, axis=1, keepdims=True)
    change = change + jnp.where(lanes == TOK - 1, edge, 0.0)
    grad_log = jnp.dot(change, since, precision=lax.Precision.HIGHEST, preferred_element_type=F32)
    grad_raw = (direct + grad_log * rate) * (1.0 / (1.0 + jnp.exp(-raw)))
    grad_bias = jnp.sum(grad_raw, axis=1, keepdims=True)
    grad_alog = jnp.sum(grad_log * dt, axis=1, keepdims=True) * rate
    grad_skip = jnp.sum(flat(rows_gx), axis=1, keepdims=True)
    extra = jnp.where(lanes == 0, grad_bias, jnp.where(lanes == 1, grad_alog, jnp.where(lanes == 2, grad_skip, 0.0)))
    extra = padded(extra).T[:8]
    grad_d = padded(grad_raw).T
    gs[0:128, :] = jnp.where(core == 0, grad_c, grad_b)
    gs[128:256, :] = grad_d
    gs[256:264, :] = extra
    cols_swap = push(gs, gr, cs, cr, cpeer)
    cols_swap.start()
    bt, ctall, dtall = tall(grad_b), tall(grad_c), tall(grad_d)[:, :HEADS]
    both_t = jnp.concatenate([bt, ctall], axis=1)

    def model_grads(i, carry):
        at = pl.ds(pl.multiple_of(i * 512, 512), 512)
        both_w = jnp.concatenate([wb_ref[at, :], wc_ref[at, :]], axis=1)
        p = dot_nt(both_t, both_w) + dot(dtall, wd_ref[:, at])
        gu_ref[:, at] = (p[:TOK] + p[TOK:]).astype(BF16)
        return carry

    lax.fori_loop(0, 2, model_grads, 0)
    cols_swap.wait()
    both_extra = extra + gr[256:264, :]
    main_w = wide(jnp.concatenate([jnp.where(core == 0, grad_b, grad_c), gr[0:128, :]], axis=0))
    steps_w = wide(jnp.concatenate([grad_d, gr[128:256, :]], axis=0))

    def weights(i, carry):
        cols = ut[pl.ds(pl.multiple_of(i * 640, 640), 640), :]
        h1[i, :, :, 0:40, :] = fold(dot(cols, main_w)).reshape(NZ, 2, 40, 128)
        gwd[...] = fold(dot(cols, steps_w))
        for s in range(16):
            first_part = gwd[pl.ds(pl.multiple_of(s * 40 + 8 * core, 8), 8), :]
            next_part = gwd[pl.ds(pl.multiple_of(s * 40 + 16 + 8 * core, 8), 8), :]
            third_part = jnp.where(core == 0, gwd[s * 40 + 32 : s * 40 + 40, :], both_extra)
            packed = first_part + pltpu.roll(next_part, 40, 1)
            h1[i, s // 2, s % 2, 40:48, :] = packed + pltpu.roll(third_part, 80, 1)
        return carry

    lax.fori_loop(0, NX, weights, 0)
    out = fin
    def part(start, there):
        return pl.ds(pl.multiple_of(start + 8 * lax.rem(there, 2), 8), 8)

    def begin(copies):
        for copy in copies:
            copy.start()
        return copies

    def arrived(copies):
        for copy in copies:
            copy.wait_recv()

    znext = [lax.rem(z + d, NZ) for d in range(1, NZ)]
    xnext = [lax.rem(x + d, NX) for d in range(1, NX)]
    z_one = begin([push(h1.at[:, t, :, pl.ds(32, 16)], c0.at[z], z0s.at[d], z0r.at[d], zpeers[d]) for d, t in enumerate(znext)])
    x_one = begin([push(h1.at[t, :, :, pl.ds(0, 16)], a0.at[x], x0s.at[d], x0r.at[d], xpeers[d]) for d, t in enumerate(xnext)])
    y_one = begin([push(h1.at[:, :, t // 2, part(16, t)], b0.at[y], y0s.at[d], y0r.at[d], ypeers[d]) for d, t in enumerate(ynext)])
    lax.fori_loop(2, 5, model_grads, 0)
    arrived(x_one)
    total = h1[x, :, :, pl.ds(0, 16), :]
    for t in xnext:
        total = total + a0[t]
    a1[...] = total
    y_two = begin([push(a1.at[:, t // 2, part(0, t)], a1r.at[y], y3s.at[d], y3r.at[d], ypeers[d]) for d, t in enumerate(ynext)])
    arrived(y_one)
    total = h1[:, :, h, part(16, yl), :]
    for t in ynext:
        total = total + b0[t]
    b1[...] = total
    z_two = begin([push(b1.at[:, t], b1r.at[z], z1s.at[d], z1r.at[d], zpeers[d]) for d, t in enumerate(znext)])
    arrived(z_one)
    total = h1[:, z, :, pl.ds(32, 16), :]
    for t in znext:
        total = total + c0[t]
    c1[...] = total
    x_two = begin([push(c1.at[t], c1r.at[x], x1s.at[d], x1r.at[d], xpeers[d]) for d, t in enumerate(xnext)])
    arrived(y_two)
    total = a1[:, h, part(0, yl), :]
    for t in ynext:
        total = total + a1r[t]
    a2[...] = total
    z_three = begin([push(a2.at[t], a2r.at[z], z2s.at[d], z2r.at[d], zpeers[d]) for d, t in enumerate(znext)])
    arrived(z_two)
    total = b1[:, z]
    for t in znext:
        total = total + b1r[t]
    b2[...] = total
    x_three = begin([push(b2.at[t], b2r.at[x], x2s.at[d], x2r.at[d], xpeers[d]) for d, t in enumerate(xnext)])
    arrived(x_two)
    total = c1[x]
    for t in xnext:
        total = total + c1r[t]
    c2[...] = total
    y_three = begin([push(c2.at[t // 2, part(0, t)], c2r.at[y], y4s.at[d], y4r.at[d], ypeers[d]) for d, t in enumerate(ynext)])
    arrived(z_three)
    total = a2[z]
    for t in znext:
        total = total + a2r[t]
    out[core, 0, yl] = total
    arrived(x_three)
    total = b2[x]
    for t in xnext:
        total = total + b2r[t]
    out[core, 1, yl] = total
    arrived(y_three)
    total = c2[h, part(0, yl), :]
    for t in ynext:
        total = total + c2r[t]
    out[core, 2, yl] = total
    last = begin([push(out.at[core, :, yl], out.at[core, :, yl], ls.at[d], lr.at[d], peer) for d, peer in enumerate(dpeers)])
    for copy in last:
        copy.wait()

    whole = fin[...].reshape(2, 48, 128)
    gbw_ref[...] = whole[0, :40]
    gcw_ref[...] = whole[1, :40]
    tail = jnp.concatenate([whole[0, 40:], whole[1, 40:]], axis=0)
    gdw_ref[0:16, :] = tail[:, :HEADS]
    gdw_ref[16:32, :] = tail[:, 40:80]
    tail = tail[:, 80:120]
    gdw_ref[32:40, :] = tail[:8]
    ex_ref[...] = tail[8:]
    for c in range(CHUNKS):
        y1[c].wait_send()
        for copy in a_copies(c) + x_copies(c) + b_copies(c):
            copy.wait_send()
        y2_copy(c).wait_send()
    for copy in x_one + y_one + z_one + x_two + y_two + z_two + x_three + y_three + z_three:
        copy.wait_send()


def layer(u, x, g, wb, wc, wd, bias, alog, skip):
    vmem = pl.BlockSpec(memory_space=pltpu.VMEM)
    dma = pltpu.SemaphoreType.DMA
    half = (2, HALF, WIDTH, STATE)

    def f32(*shape):
        return pltpu.VMEM(shape + (128,), F32)

    def b16(*shape):
        return pltpu.VMEM(shape, BF16)

    def sems(counts):
        pairs = []
        for n in counts:
            pairs += [dma if n == () else dma(n)] * 2
        return pairs

    shape = jax.ShapeDtypeStruct
    return pl.pallas_call(
        layer_kernel,
        out_shape=(
            shape((TOK, MODEL), BF16), shape((TOK, MODEL), BF16), shape((40, STATE), F32),
            shape((40, STATE), F32), shape((40, HEADS), F32), shape((8, HEADS), F32),
        ),
        in_specs=[vmem] * 9,
        out_specs=(vmem,) * 6,
        scratch_shapes=[
            b16(MODEL, TOK), b16(MODEL, TOK), b16(MODEL, 256), b16(MODEL, 256), b16(MODEL, 256),
            b16(256, 256), b16(256, 256), b16(256, 256), b16(256, 256),
            f32(TOK), f32(TOK), f32(TOK), f32(MODEL), pltpu.VMEM((256, 256), F32), pltpu.VMEM((256, 256), F32),
        ] + [f32(HEADS, 1)] * 11 + [
            f32(HEADS), f32(HEADS), f32(640),
            f32(2, HEADS, WIDTH), f32(2, 24), f32(2, HEADS, WIDTH),
            f32(*half[:3]), f32(*half[:3]),
            f32(NZ, 2, HALF, PIECE), f32(2, HALF, PIECE), f32(NX, HALF, PIECE), f32(NZ, 2, HALF, PIECE),
            f32(*half[:3]), f32(*half[:3]),
            f32(24), f32(4, 24), f32(24), f32(NZ, 24), f32(NX, 24),
            pltpu.VMEM((TOK, MODEL), F32), pltpu.VMEM((TOK, MODEL), F32), f32(264), f32(264), f32(4, 8, 2, 48),
            f32(4, 8, 2, 16), f32(8, 2, 16), f32(4, 8, 8), f32(8, 8), f32(8, 8),
            f32(4, 4, 8, 8), f32(4, 8, 8), f32(8, 4, 8), f32(4, 8), f32(4, 8),
            f32(8, 4, 2, 16), f32(4, 2, 16), f32(4, 2, 16), f32(2, 16), f32(4, 8),
            f32(2, 3, 2, 8),
        ] + sems(
            [(CHUNKS,), (CHUNKS, NZ - 1), (CHUNKS, NX - 1), (CHUNKS, NZ - 1), (CHUNKS,), (), (NZ - 1,), (NX - 1,)]
        ) + sems([(), (3,), (3,), (7,), (3,), (7,), (3,), (7,), (3,), (3,), (3,), ()]),
        compiler_params=pltpu.CompilerParams(
            collective_id=0, has_side_effects=True, vmem_limit_bytes=60 << 20
        ),
        name="layer",
    )(u, x, g, wb, wc, wd, bias, alog, skip)


def body(layer_input, ssm_input, out_grad, b_weight, c_weight, dt_weight, dt_bias, a_log, d_skip):
    gx, gu, gb, gc, gd, extra = layer(
        layer_input, ssm_input, out_grad, b_weight, c_weight, dt_weight.T,
        dt_bias[None], a_log[None], d_skip[None],
    )
    return gx, gu, gb, gc, gd, extra[0], extra[1], extra[2]


def solution(mesh):
    split_mesh = Mesh(mesh.devices.reshape(4, 8, 2, 2, 2), AXES)
    cut, whole = P(DP_SEQ, None), P()
    return jax.shard_map(
        body,
        mesh=split_mesh,
        in_specs=(cut, cut, cut) + (whole,) * 6,
        out_specs=(cut, cut) + (P(SEQ, None),) * 3 + (whole,) * 3,
        check_vma=False,
    )
```

```python
import jax
import jax.numpy as jnp
from jax import lax
from jax.experimental import pallas as pl
from jax.experimental.pallas import tpu as pltpu
from jax.sharding import Mesh
from jax.sharding import PartitionSpec as P

SEQ = ("x", "z", "yh")
DP_SEQ = ("yl", "core", "x", "z", "yh")
AXES = ("x", "z", "yh", "yl", "core")
SIZES = {"x": 4, "z": 8, "yh": 2, "yl": 2, "core": 2}
MESH = pl.DeviceIdType.MESH
HEADS, WIDTH, STATE = 40, 64, 128
HALF = HEADS // 2
SIZES_OF = (2, 4, 4, 4, 4, 2)
STARTS = tuple(sum(SIZES_OF[:c]) for c in range(len(SIZES_OF)))
CHUNKS = len(SIZES_OF)
NX, NZ = SIZES["x"], SIZES["z"]
PIECE = WIDTH // NZ
FAR_FIRST = (4, 3, 5, 2, 6, 1, 7)


def place():
    return {axis: lax.axis_index(axis) for axis in AXES}


def shifted(here, **steps):
    there = dict(here)
    for axis, step in steps.items():
        there[axis] = lax.rem(here[axis] + step, SIZES[axis])
    return tuple(there[axis] for axis in AXES)


def greet(peers):
    barrier = pltpu.get_barrier_semaphore()
    for peer in peers:
        pl.semaphore_signal(barrier, inc=1, device_id=peer, device_id_type=MESH)
    pl.semaphore_wait(barrier, len(peers))


def push(src, dst, send, recv, peer):
    return pltpu.make_async_remote_copy(
        src_ref=src, dst_ref=dst, send_sem=send, recv_sem=recv, device_id=peer, device_id_type=MESH
    )


TOK = 128
MODEL = 2560
F32, BF16 = jnp.float32, jnp.bfloat16


def dot(a, b):
    return jnp.dot(a, b, preferred_element_type=F32)


def dot_tn(a, b):
    return lax.dot_general(a, b, (((0,), (0,)), ((), ())), preferred_element_type=F32)


def dot_nt(a, b):
    return lax.dot_general(a, b, (((1,), (1,)), ((), ())), preferred_element_type=F32)


def split(v):
    top = v.astype(BF16)
    return top, (v - top.astype(F32)).astype(BF16)


def wide(v):
    return jnp.concatenate(split(v), axis=1)


def tall(v):
    return jnp.concatenate(split(v), axis=0)


def square(v):
    w = wide(v)
    return jnp.concatenate([w, w], axis=0)


def fold(p):
    return p[:, :128] + p[:, 128:]


def padded(v):
    return jnp.concatenate([v, jnp.zeros((TOK - v.shape[0], TOK), F32)], axis=0)


def layer_kernel(
    u_ref, x_ref, g_ref, wb_ref, wc_ref, wd_ref, bias_ref, alog_ref, skip_ref,
    gx_ref, gu_ref, gbw_ref, gcw_ref, gdw_ref, ex_ref,
    xt, gt, ut, xw, gw, b4, c4, bt4, ct4, scores, pairacc, rowacc, inner, gbacc, gcacc,
    rows_dt, rows_ws, rows_fs, rows_te, rows_cum, rows_skip, rows_col, rows_xb, rows_gf, rows_cross, rows_gx,
    flat_dt, flat_raw, gwd, sr, dec, car, par, pq, arec, xs, xr, bs, ps, ys, dpar, coef, pair, zd, rd,
    us, ur, gs, gr, h1, a0, a1, a1r, a2, a2r, b0, b1, b1r, b2, b2r, c0, c1, c1r, c2, c2r, fin,
    *sems,
):
    here = place()
    x, z, h, yl, core = (here[a] for a in AXES)
    y = h * 2 + yl
    low = h == 0
    mine, other = h * HALF, (1 - h) * HALF
    partner = shifted(here, yh=1)
    cpeer = shifted(here, core=1)
    dpeers = [cpeer, shifted(here, yl=1), shifted(here, yl=1, core=1)]
    zpeers = [shifted(here, z=d) for d in range(1, NZ)]
    xpeers = [shifted(here, x=d) for d in range(1, NX)]
    ynext = [lax.rem(y + d, 4) for d in range(1, 4)]
    ypeers = [(x, z, t // 2, lax.rem(t, 2), core) for t in ynext]
    peers = [cpeer, dpeers[2]] + ypeers + zpeers + xpeers
    scan_sems, red_sems = sems[:16], sems[16:]
    y1s, y1r, as_, ar_, xss, xrs, bss, brs, y2s, y2r, d1s, d1r, d2s, d2r, d3s, d3r = scan_sems
    cs, cr, x0s, x0r, y0s, y0r, z0s, z0r, y3s, y3r, z1s, z1r, x1s, x1r, z2s, z2r, x2s, x2r, y4s, y4r, ls, lr, us_sem, ur_sem = red_sems
    barrier = pltpu.get_barrier_semaphore()
    for peer in peers:
        pl.semaphore_signal(barrier, inc=1, device_id=peer, device_id_type=MESH)

    u = u_ref[...]
    columns = jnp.concatenate([bias_ref[...], alog_ref[...], skip_ref[...], jnp.zeros((5, HEADS), F32)], axis=0)
    columns = jnp.concatenate([columns, jnp.zeros((8, TOK - HEADS), F32)], axis=1)
    columns = padded(columns).T[:HEADS]
    alog = columns[:, 1:2]
    raw = dot_nt(wd_ref[...], u) + columns[:, 0:1]
    small = jnp.exp(-jnp.abs(raw))
    above = 1.0 + small
    gap = above - 1.0
    log_part = jnp.where(gap == 0.0, small, jnp.log(above) * (small / jnp.where(gap == 0.0, 1.0, gap)))
    dt = jnp.maximum(raw, 0.0) + log_part
    rate = -jnp.exp(alog)
    row_i = lax.broadcasted_iota(jnp.int32, (TOK, TOK), 0)
    col_i = lax.broadcasted_iota(jnp.int32, (TOK, TOK), 1)
    upto = (row_i <= col_i).astype(F32)
    since = (row_i >= col_i).astype(F32)
    cum = jnp.dot(dt * rate, upto, precision=lax.Precision.HIGHEST, preferred_element_type=F32)
    last = cum[:, TOK - 1 :]
    to_end = jnp.exp(last - cum)
    from_start = jnp.exp(cum)
    flat_dt[...] = dt
    flat_raw[...] = raw

    def rows(v):
        return v.reshape(HEADS, 1, TOK)

    rows_dt[...] = rows(dt)
    rows_ws[...] = rows(to_end * dt)
    rows_fs[...] = rows(from_start)
    rows_te[...] = rows(to_end)
    rows_cum[...] = rows(cum)
    rows_skip[...] = rows(jnp.broadcast_to(columns[:, 2:3], (HEADS, TOK)))
    decay = jnp.broadcast_to(jnp.exp(last), (HEADS, STATE))
    fill = jnp.ones((4, STATE), F32)
    dec[0] = jnp.concatenate([decay[:HALF], fill], axis=0)
    dec[1] = jnp.concatenate([decay[HALF:], fill], axis=0)
    proj_b = dot(u, wb_ref[...])
    proj_c = dot(u, wc_ref[...])
    b4[...] = square(proj_b)
    c4[...] = square(proj_c)

    def states(start, c):
        count, block = SIZES_OF[c], SIZES_OF[c] * WIDTH
        at = pl.multiple_of((start + STARTS[c]) * WIDTH, 2 * WIDTH)
        heads = pl.ds(start + STARTS[c], count)
        rows_at = pl.ds(at, block)
        xc = x_ref[:, pl.ds(at, block)].T
        gc = g_ref[:, pl.ds(at, block)].T
        xt[rows_at, :] = xc
        gt[rows_at, :] = gc
        xsc = xc.astype(F32).reshape(count, WIDTH, TOK) * rows_ws[heads]
        gsc = gc.astype(F32).reshape(count, WIDTH, TOK) * rows_fs[heads]
        xwc = wide(xsc.reshape(block, TOK))
        gwc = wide(gsc.reshape(block, TOK))
        xw[rows_at, :] = xwc
        gw[rows_at, :] = gwc
        sr[0, heads] = fold(dot(xwc, b4[...])).reshape(count, WIDTH, STATE)
        sr[1, heads] = fold(dot(gwc, c4[...])).reshape(count, WIDTH, STATE)

    states(other, 0)
    pl.semaphore_wait(barrier, len(peers))
    first = push(dec.at[1 - h], dpar, d1s, d1r, partner)
    first.start()
    y1 = [
        push(
            sr.at[:, pl.ds(other + STARTS[c], SIZES_OF[c])],
            par.at[:, pl.ds(STARTS[c], SIZES_OF[c])],
            y1s.at[c], y1r.at[c], partner,
        )
        for c in range(CHUNKS)
    ]
    y1[0].start()
    us[...] = u.astype(F32)
    u_swap = push(us, ur, us_sem, ur_sem, cpeer)
    u_swap.start()
    states(other, 1)
    y1[1].start()
    xr[x] = jnp.zeros((HALF, PIECE, STATE), F32)
    first.wait()
    own_decay = dec[h]
    par_decay = dpar[...]
    one = jnp.ones_like(own_decay)
    coef[0] = jnp.where(low, par_decay, one)
    coef[1] = jnp.where(low, one, own_decay)
    coef[2] = jnp.where(low, one, par_decay)
    coef[3] = jnp.where(low, own_decay, one)
    pair[...] = own_decay * par_decay
    zd[z] = own_decay * par_decay
    second = [push(pair, zd.at[z], d2s.at[d], d2r.at[d], peer) for d, peer in enumerate(zpeers)]
    for copy in second:
        copy.start()
    states(mine, 0)
    for c in range(2, CHUNKS):
        states(other, c)
    bt4[...] = square(proj_b.T)
    ct4[...] = square(proj_c.T)
    scores[...] = jnp.where(row_i >= col_i, fold(dot(wide(proj_c), bt4[...])), 0.0)
    pairacc[...] = jnp.zeros((TOK, TOK), F32)
    rowacc[...] = jnp.zeros((TOK, TOK), F32)
    for copy in second:
        copy.wait()
    row = zd[0]
    for k in range(1, NZ):
        row = row * zd[k]
    rd[x] = row
    third = [push(rd.at[x], rd.at[x], d3s.at[d], d3r.at[d], peer) for d, peer in enumerate(xpeers)]
    for copy in third:
        copy.start()

    def a_copies(c):
        heads = pl.ds(STARTS[c], SIZES_OF[c])
        copies = []
        for d, peer in enumerate(zpeers):
            pz = pl.multiple_of(lax.rem(z + d + 1, NZ) * PIECE, PIECE)
            copies.append(
                push(pq.at[:, heads, pl.ds(pz, PIECE)], arec.at[z, :, heads], as_.at[c, d], ar_.at[c, d], peer)
            )
        return copies

    def x_copies(c):
        heads = pl.ds(STARTS[c], SIZES_OF[c])
        copies = []
        for d, peer in enumerate(xpeers):
            px = lax.rem(x + d + 1, NX)
            back = jnp.where(px > x, 0, 1)
            copies.append(push(xs.at[back, heads], xr.at[x, heads], xss.at[c, d], xrs.at[c, d], peer))
        return copies

    def b_copies(c):
        heads = pl.ds(STARTS[c], SIZES_OF[c])
        here_rows = pl.ds(pl.multiple_of(z * PIECE, PIECE), PIECE)
        copies = []
        for d, peer in enumerate(zpeers):
            pz = lax.rem(z + d + 1, NZ)
            copies.append(
                push(bs.at[pz, :, heads], ps.at[:, heads, here_rows], bss.at[c, d], brs.at[c, d], peer)
            )
        return copies

    def y2_copy(c):
        return push(
            ys.at[:, pl.ds(STARTS[c], SIZES_OF[c])],
            car.at[:, pl.ds(mine + STARTS[c], SIZES_OF[c])],
            y2s.at[c], y2r.at[c], partner,
        )

    def pairs(c):
        y1[c].wait_recv()
        if c + 2 < CHUNKS:
            y1[c + 2].start()

        def head(i, carry):
            k = STARTS[c] + i
            at = pl.ds(k, 1)
            pq[0, k] = coef[0, at, :] * sr[0, mine + k] + coef[1, at, :] * par[0, k]
            pq[1, k] = coef[2, at, :] * sr[1, mine + k] + coef[3, at, :] * par[1, k]
            return carry

        lax.fori_loop(0, SIZES_OF[c], head, 0)
        heads = pl.ds(STARTS[c], SIZES_OF[c])
        own = pl.ds(pl.multiple_of(z * PIECE, PIECE), PIECE)
        arec[z, :, heads] = pq[:, heads, own, :]
        copies = a_copies(c)
        for d in FAR_FIRST:
            copies[d - 1].start()

    def totals(c):
        for copy in a_copies(c):
            copy.wait_recv()

        def head(i, carry):
            k = STARTS[c] + i
            at = pl.ds(k, 1)
            forward = arec[0, 0, k]
            backward = arec[NZ - 1, 1, k]
            for j in range(1, NZ):
                forward = zd[j, at, :] * forward + arec[j, 0, k]
                backward = zd[NZ - 1 - j, at, :] * backward + arec[NZ - 1 - j, 1, k]
            xs[0, k] = forward
            xs[1, k] = backward
            return carry

        lax.fori_loop(0, SIZES_OF[c], head, 0)
        for copy in x_copies(c):
            copy.start()

    def prefixes(c):
        if c == 0:
            for copy in third:
                copy.wait()
        for copy in x_copies(c):
            copy.wait_recv()

        def head(i, carry):
            k = STARTS[c] + i
            at = pl.ds(k, 1)
            forward = jnp.zeros((PIECE, STATE), jnp.float32)
            backward = jnp.zeros((PIECE, STATE), jnp.float32)
            for j in range(NX):
                forward = jnp.where(j < x, rd[j, at, :] * forward + xr[j, k], forward)
                m = NX - 1 - j
                backward = jnp.where(m > x, rd[m, at, :] * backward + xr[m, k], backward)
            for j in range(NZ):
                bs[j, 0, k] = forward
                forward = zd[j, at, :] * forward + arec[j, 0, k]
                m = NZ - 1 - j
                bs[m, 1, k] = backward
                backward = zd[m, at, :] * backward + arec[m, 1, k]
            return carry

        lax.fori_loop(0, SIZES_OF[c], head, 0)
        heads = pl.ds(STARTS[c], SIZES_OF[c])
        own = pl.ds(pl.multiple_of(z * PIECE, PIECE), PIECE)
        ps[:, heads, own, :] = bs[z, :, heads]
        copies = b_copies(c)
        for d in FAR_FIRST:
            copies[d - 1].start()

    def finals(c):
        for copy in b_copies(c):
            copy.wait_recv()

        def head(i, carry):
            k = STARTS[c] + i
            at = pl.ds(k, 1)
            before, after = ps[0, k], ps[1, k]
            zero = jnp.zeros_like(before)
            ys[0, k] = coef[3, at, :] * before + jnp.where(low, sr[0, mine + k], zero)
            ys[1, k] = coef[1, at, :] * after + jnp.where(low, zero, sr[1, mine + k])
            car[0, mine + k] = coef[2, at, :] * before + jnp.where(low, zero, par[0, k])
            car[1, mine + k] = coef[0, at, :] * after + jnp.where(low, par[1, k], zero)
            return carry

        lax.fori_loop(0, SIZES_OF[c], head, 0)
        y2_copy(c).start()


    def within(start, count):
        def two(i, carry):
            for j in range(2):
                k = start + 2 * i + j
                at = pl.ds(pl.multiple_of(k * WIDTH, WIDTH), WIDTH)
                gk = gt[at, :]
                dots = dot_tn(gk, xt[at, :])
                across = jnp.broadcast_to(rows_cum[k], (TOK, TOK))
                table = jnp.exp(jnp.minimum(across.T - across, 0.0))
                weight = table * scores[...]
                inner[at, :] = fold(dot(gk, wide(weight)))
                terms = weight * dots
                rows_col[k] = jnp.sum(terms, axis=0, keepdims=True)
                pairacc[...] += table * dots * rows_dt[k]
                sums = jnp.sum(terms * rows_dt[k], axis=1, keepdims=True)
                rowacc[...] = jnp.where(col_i == k, sums, rowacc[...])
            return carry

        lax.fori_loop(0, count // 2, two, 0)

    gbacc[...] = jnp.zeros((2 * TOK, 2 * TOK), F32)
    gcacc[...] = jnp.zeros((2 * TOK, 2 * TOK), F32)

    def outputs(start, c):
        count, block = SIZES_OF[c], SIZES_OF[c] * WIDTH
        at = pl.multiple_of((start + STARTS[c]) * WIDTH, 2 * WIDTH)
        heads = pl.ds(start + STARTS[c], count)
        rows_at = pl.ds(at, block)
        ci = car[0, heads]
        co = car[1, heads]
        rows_cross[heads] = jnp.sum(ci * co, axis=1, keepdims=True)
        ciw = wide(ci.reshape(block, STATE))
        cow = wide(co.reshape(block, STATE))
        back = fold(dot(cow, bt4[...])).reshape(count, WIDTH, TOK)
        front = fold(dot(ciw, ct4[...])).reshape(count, WIDTH, TOK)
        gbacc[...] += dot_tn(xw[rows_at, :], cow)
        gcacc[...] += dot_tn(gw[rows_at, :], ciw)
        xf = xt[rows_at, :].astype(F32).reshape(count, WIDTH, TOK)
        gf = gt[rows_at, :].astype(F32).reshape(count, WIDTH, TOK)
        rows_xb[heads] = jnp.sum(xf * back, axis=1, keepdims=True)
        rows_gf[heads] = jnp.sum(gf * front, axis=1, keepdims=True)
        rows_gx[heads] = jnp.sum(gf * xf, axis=1, keepdims=True)
        total = inner[rows_at, :].reshape(count, WIDTH, TOK) + rows_te[heads] * back
        gx = rows_dt[heads] * total + rows_skip[heads] * gf
        gx_ref[:, pl.ds(at, block)] = gx.reshape(block, TOK).T.astype(BF16)

    work = [(half + n, 4) for half in (other, mine) for n in range(0, HALF, 4)]

    def fill(n):
        for _ in range(min(n, len(work))):
            within(*work.pop(0))

    fill(1)
    for c in range(1, CHUNKS):
        states(mine, c)
    fill(1)
    for step in range(CHUNKS + 3):
        if step < CHUNKS:
            pairs(step)
        if 0 <= step - 1 < CHUNKS:
            totals(step - 1)
        if 0 <= step - 2 < CHUNKS:
            prefixes(step - 2)
        if 0 <= step - 3 < CHUNKS:
            finals(step - 3)
        if step < 3:
            fill(1)
        elif step == 3:
            fill(10)
            outputs(mine, 0)
        else:
            outputs(mine, step - 3)
        if step == 5:
            u_swap.wait()
            for j in range(0, MODEL, 512):
                ut[j : j + 512, :TOK] = u_ref[:, j : j + 512].T
                ut[j : j + 512, TOK:] = ur[:, j : j + 512].astype(BF16).T
    sums = pairacc[...]
    sumw = wide(jnp.where(row_i >= col_i, sums, 0.0))
    gbacc[...] += dot_tn(sumw, wide(dot(u_ref[...], wc_ref[...])))
    scores[...] = fold(dot(sumw, b4[...]))
    rowacc[...] = rowacc[...].T
    for c in range(CHUNKS):
        y2_copy(c).wait_recv()
        outputs(other, c)

    acc = gbacc[...]
    acc = acc[:TOK] + acc[TOK:]
    grad_b = fold(acc)
    acc = gcacc[...]
    acc = acc[:TOK] + acc[TOK:]
    grad_c = fold(acc) + scores[...]

    def flat(ref):
        return ref[...].reshape(HEADS, TOK)

    dt = flat_dt[...]
    raw = flat_raw[...]
    end = flat(rows_te)
    rate = -jnp.exp(alog)
    col = flat(rows_col)
    xb = end * flat(rows_xb)
    direct = col + xb
    own_out = dt * xb
    own_in = flat(rows_fs) * flat(rows_gf)
    cross = flat(rows_fs)[:, TOK - 1 :] * jnp.sum(flat(rows_cross), axis=1, keepdims=True)
    change = rowacc[0:HEADS, :] - dt * col + own_in - own_out
    lanes = lax.broadcasted_iota(jnp.int32, (HEADS, TOK), 1)
    edge = cross + jnp.sum(own_out, axis=1, keepdims=True)
    change = change + jnp.where(lanes == TOK - 1, edge, 0.0)
    grad_log = jnp.dot(change, since, precision=lax.Precision.HIGHEST, preferred_element_type=F32)
    grad_raw = (direct + grad_log * rate) * (1.0 / (1.0 + jnp.exp(-raw)))
    grad_bias = jnp.sum(grad_raw, axis=1, keepdims=True)
    grad_alog = jnp.sum(grad_log * dt, axis=1, keepdims=True) * rate
    grad_skip = jnp.sum(flat(rows_gx), axis=1, keepdims=True)
    extra = jnp.where(lanes == 0, grad_bias, jnp.where(lanes == 1, grad_alog, jnp.where(lanes == 2, grad_skip, 0.0)))
    extra = padded(extra).T[:8]
    grad_d = padded(grad_raw).T
    gs[0:128, :] = jnp.where(core == 0, grad_c, grad_b)
    gs[128:256, :] = grad_d
    gs[256:264, :] = extra
    cols_swap = push(gs, gr, cs, cr, cpeer)
    cols_swap.start()
    bt, ctall, dtall = tall(grad_b), tall(grad_c), tall(grad_d)[:, :HEADS]
    both_t = jnp.concatenate([bt, ctall], axis=1)

    def model_grads(i, carry):
        at = pl.ds(pl.multiple_of(i * 512, 512), 512)
        both_w = jnp.concatenate([wb_ref[at, :], wc_ref[at, :]], axis=1)
        p = dot_nt(both_t, both_w) + dot(dtall, wd_ref[:, at])
        gu_ref[:, at] = (p[:TOK] + p[TOK:]).astype(BF16)
        return carry

    lax.fori_loop(0, 2, model_grads, 0)
    cols_swap.wait()
    both_extra = extra + gr[256:264, :]
    main_w = wide(jnp.concatenate([jnp.where(core == 0, grad_b, grad_c), gr[0:128, :]], axis=0))
    steps_w = wide(jnp.concatenate([grad_d, gr[128:256, :]], axis=0))

    znext = [lax.rem(z + d, NZ) for d in range(1, NZ)]

    def z_firsts(i):
        copies = [
            push(h1.at[i, n, :, pl.ds(32, 16)], c0.at[z, i], z0s.at[i, d], z0r.at[i, d], zpeers[d])
            for d, n in enumerate(znext)
        ]
        return [copies[d - 1] for d in FAR_FIRST]

    def weights(i, carry):
        cols = ut[pl.ds(pl.multiple_of(i * 640, 640), 640), :]
        h1[i, :, :, 0:40, :] = fold(dot(cols, main_w)).reshape(NZ, 2, 40, 128)
        gwd[...] = fold(dot(cols, steps_w))
        for s in range(16):
            first_part = gwd[pl.ds(pl.multiple_of(s * 40 + 8 * core, 8), 8), :]
            next_part = gwd[pl.ds(pl.multiple_of(s * 40 + 16 + 8 * core, 8), 8), :]
            third_part = jnp.where(core == 0, gwd[s * 40 + 32 : s * 40 + 40, :], both_extra)
            packed = first_part + pltpu.roll(next_part, 40, 1)
            h1[i, s // 2, s % 2, 40:48, :] = packed + pltpu.roll(third_part, 80, 1)
        for copy in z_firsts(i):
            copy.start()
        return carry

    lax.fori_loop(0, NX, weights, 0)
    out = fin
    def part(start, there):
        return pl.ds(pl.multiple_of(start + 8 * lax.rem(there, 2), 8), 8)

    def begin(copies):
        for copy in copies:
            copy.start()
        return copies

    def arrived(copies):
        for copy in copies:
            copy.wait_recv()

    xnext = [lax.rem(x + d, NX) for d in range(1, NX)]
    z_one = [copy for i in range(NX) for copy in z_firsts(i)]
    x_one = begin([push(h1.at[t, :, :, pl.ds(0, 16)], a0.at[x], x0s.at[d], x0r.at[d], xpeers[d]) for d, t in enumerate(xnext)])
    y_one = begin([push(h1.at[:, :, t // 2, part(16, t)], b0.at[y], y0s.at[d], y0r.at[d], ypeers[d]) for d, t in enumerate(ynext)])
    lax.fori_loop(2, 5, model_grads, 0)
    arrived(x_one)
    total = h1[x, :, :, pl.ds(0, 16), :]
    for t in xnext:
        total = total + a0[t]
    a1[...] = total
    y_two = begin([push(a1.at[:, t // 2, part(0, t)], a1r.at[y], y3s.at[d], y3r.at[d], ypeers[d]) for d, t in enumerate(ynext)])
    arrived(y_one)
    total = h1[:, :, h, part(16, yl), :]
    for t in ynext:
        total = total + b0[t]
    b1[...] = total
    z_two = begin([push(b1.at[:, t], b1r.at[z], z1s.at[d], z1r.at[d], zpeers[d]) for d, t in enumerate(znext)])
    arrived(z_one)
    total = h1[:, z, :, pl.ds(32, 16), :]
    for t in znext:
        total = total + c0[t]
    c1[...] = total
    x_two = begin([push(c1.at[t], c1r.at[x], x1s.at[d], x1r.at[d], xpeers[d]) for d, t in enumerate(xnext)])
    arrived(y_two)
    total = a1[:, h, part(0, yl), :]
    for t in ynext:
        total = total + a1r[t]
    a2[...] = total
    z_three = begin([push(a2.at[t], a2r.at[z], z2s.at[d], z2r.at[d], zpeers[d]) for d, t in enumerate(znext)])
    arrived(z_two)
    total = b1[:, z]
    for t in znext:
        total = total + b1r[t]
    b2[...] = total
    x_three = begin([push(b2.at[t], b2r.at[x], x2s.at[d], x2r.at[d], xpeers[d]) for d, t in enumerate(xnext)])
    arrived(x_two)
    total = c1[x]
    for t in xnext:
        total = total + c1r[t]
    c2[...] = total
    y_three = begin([push(c2.at[t // 2, part(0, t)], c2r.at[y], y4s.at[d], y4r.at[d], ypeers[d]) for d, t in enumerate(ynext)])
    arrived(z_three)
    total = a2[z]
    for t in znext:
        total = total + a2r[t]
    out[core, 0, yl] = total
    arrived(x_three)
    total = b2[x]
    for t in xnext:
        total = total + b2r[t]
    out[core, 1, yl] = total
    arrived(y_three)
    total = c2[h, part(0, yl), :]
    for t in ynext:
        total = total + c2r[t]
    out[core, 2, yl] = total
    last = begin([push(out.at[core, :, yl], out.at[core, :, yl], ls.at[d], lr.at[d], peer) for d, peer in enumerate(dpeers)])
    for copy in last:
        copy.wait()

    whole = fin[...].reshape(2, 48, 128)
    gbw_ref[...] = whole[0, :40]
    gcw_ref[...] = whole[1, :40]
    tail = jnp.concatenate([whole[0, 40:], whole[1, 40:]], axis=0)
    gdw_ref[0:16, :] = tail[:, :HEADS]
    gdw_ref[16:32, :] = tail[:, 40:80]
    tail = tail[:, 80:120]
    gdw_ref[32:40, :] = tail[:8]
    ex_ref[...] = tail[8:]
    for c in range(CHUNKS):
        y1[c].wait_send()
        for copy in a_copies(c) + x_copies(c) + b_copies(c):
            copy.wait_send()
        y2_copy(c).wait_send()
    for copy in x_one + y_one + z_one + x_two + y_two + z_two + x_three + y_three + z_three:
        copy.wait_send()


def layer(u, x, g, wb, wc, wd, bias, alog, skip):
    vmem = pl.BlockSpec(memory_space=pltpu.VMEM)
    dma = pltpu.SemaphoreType.DMA
    half = (2, HALF, WIDTH, STATE)

    def f32(*shape):
        return pltpu.VMEM(shape + (128,), F32)

    def b16(*shape):
        return pltpu.VMEM(shape, BF16)

    def sems(counts):
        pairs = []
        for n in counts:
            pairs += [dma if n == () else dma(n)] * 2
        return pairs

    shape = jax.ShapeDtypeStruct
    return pl.pallas_call(
        layer_kernel,
        out_shape=(
            shape((TOK, MODEL), BF16), shape((TOK, MODEL), BF16), shape((40, STATE), F32),
            shape((40, STATE), F32), shape((40, HEADS), F32), shape((8, HEADS), F32),
        ),
        in_specs=[vmem] * 9,
        out_specs=(vmem,) * 6,
        scratch_shapes=[
            b16(MODEL, TOK), b16(MODEL, TOK), b16(MODEL, 256), b16(MODEL, 256), b16(MODEL, 256),
            b16(256, 256), b16(256, 256), b16(256, 256), b16(256, 256),
            f32(TOK), f32(TOK), f32(TOK), f32(MODEL), pltpu.VMEM((256, 256), F32), pltpu.VMEM((256, 256), F32),
        ] + [f32(HEADS, 1)] * 11 + [
            f32(HEADS), f32(HEADS), f32(640),
            f32(2, HEADS, WIDTH), f32(2, 24), f32(2, HEADS, WIDTH),
            f32(*half[:3]), f32(*half[:3]),
            f32(NZ, 2, HALF, PIECE), f32(2, HALF, PIECE), f32(NX, HALF, PIECE), f32(NZ, 2, HALF, PIECE),
            f32(*half[:3]), f32(*half[:3]),
            f32(24), f32(4, 24), f32(24), f32(NZ, 24), f32(NX, 24),
            pltpu.VMEM((TOK, MODEL), F32), pltpu.VMEM((TOK, MODEL), F32), f32(264), f32(264), f32(4, 8, 2, 48),
            f32(4, 8, 2, 16), f32(8, 2, 16), f32(4, 8, 8), f32(8, 8), f32(8, 8),
            f32(4, 4, 8, 8), f32(4, 8, 8), f32(8, 4, 8), f32(4, 8), f32(4, 8),
            f32(8, 4, 2, 16), f32(4, 2, 16), f32(4, 2, 16), f32(2, 16), f32(4, 8),
            f32(2, 3, 2, 8),
        ] + sems(
            [(CHUNKS,), (CHUNKS, NZ - 1), (CHUNKS, NX - 1), (CHUNKS, NZ - 1), (CHUNKS,), (), (NZ - 1,), (NX - 1,)]
        ) + sems([(), (3,), (3,), (NX, 7), (3,), (7,), (3,), (7,), (3,), (3,), (3,), ()]),
        compiler_params=pltpu.CompilerParams(
            collective_id=0, has_side_effects=True, vmem_limit_bytes=60 << 20
        ),
        name="layer",
    )(u, x, g, wb, wc, wd, bias, alog, skip)


def body(layer_input, ssm_input, out_grad, b_weight, c_weight, dt_weight, dt_bias, a_log, d_skip):
    gx, gu, gb, gc, gd, extra = layer(
        layer_input, ssm_input, out_grad, b_weight, c_weight, dt_weight.T,
        dt_bias[None], a_log[None], d_skip[None],
    )
    return gx, gu, gb, gc, gd, extra[0], extra[1], extra[2]


def solution(mesh):
    split_mesh = Mesh(mesh.devices.reshape(4, 8, 2, 2, 2), AXES)
    cut, whole = P(DP_SEQ, None), P()
    return jax.shard_map(
        body,
        mesh=split_mesh,
        in_specs=(cut, cut, cut) + (whole,) * 6,
        out_specs=(cut, cut) + (P(SEQ, None),) * 3 + (whole,) * 3,
        check_vma=False,
    )
```

```python
import jax
import jax.numpy as jnp
from jax import lax
from jax.experimental import pallas as pl
from jax.experimental.pallas import tpu as pltpu
from jax.sharding import Mesh
from jax.sharding import PartitionSpec as P

SEQ = ("x", "z", "yh")
DP_SEQ = ("yl", "core", "x", "z", "yh")
AXES = ("x", "z", "yh", "yl", "core")
SIZES = {"x": 4, "z": 8, "yh": 2, "yl": 2, "core": 2}
MESH = pl.DeviceIdType.MESH
HEADS, WIDTH, STATE = 40, 64, 128
HALF = HEADS // 2
SIZES_OF = (2, 4, 4, 4, 4, 2)
STARTS = tuple(sum(SIZES_OF[:c]) for c in range(len(SIZES_OF)))
CHUNKS = len(SIZES_OF)
NX, NZ = SIZES["x"], SIZES["z"]
PIECE = WIDTH // NZ
FAR_FIRST = (4, 3, 5, 2, 6, 1, 7)


def place():
    return {axis: lax.axis_index(axis) for axis in AXES}


def shifted(here, **steps):
    there = dict(here)
    for axis, step in steps.items():
        there[axis] = lax.rem(here[axis] + step, SIZES[axis])
    return tuple(there[axis] for axis in AXES)


def greet(peers):
    barrier = pltpu.get_barrier_semaphore()
    for peer in peers:
        pl.semaphore_signal(barrier, inc=1, device_id=peer, device_id_type=MESH)
    pl.semaphore_wait(barrier, len(peers))


def push(src, dst, send, recv, peer):
    return pltpu.make_async_remote_copy(
        src_ref=src, dst_ref=dst, send_sem=send, recv_sem=recv, device_id=peer, device_id_type=MESH
    )


TOK = 128
MODEL = 2560
F32, BF16 = jnp.float32, jnp.bfloat16


def dot(a, b):
    return jnp.dot(a, b, preferred_element_type=F32)


def dot_tn(a, b):
    return lax.dot_general(a, b, (((0,), (0,)), ((), ())), preferred_element_type=F32)


def dot_nt(a, b):
    return lax.dot_general(a, b, (((1,), (1,)), ((), ())), preferred_element_type=F32)


def split(v):
    top = v.astype(BF16)
    return top, (v - top.astype(F32)).astype(BF16)


def wide(v):
    return jnp.concatenate(split(v), axis=1)


def tall(v):
    return jnp.concatenate(split(v), axis=0)


def square(v):
    w = wide(v)
    return jnp.concatenate([w, w], axis=0)


def fold(p):
    return p[:, :128] + p[:, 128:]


def padded(v):
    return jnp.concatenate([v, jnp.zeros((TOK - v.shape[0], TOK), F32)], axis=0)


def layer_kernel(
    u_ref, x_ref, g_ref, wb_ref, wc_ref, wd_ref, bias_ref, alog_ref, skip_ref,
    gx_ref, gu_ref, gbw_ref, gcw_ref, gdw_ref, ex_ref,
    xt, gt, ut, xw, gw, b4, c4, bt4, ct4, scores, pairacc, rowacc, inner, gbacc, gcacc,
    rows_dt, rows_ws, rows_fs, rows_te, rows_cum, rows_skip, rows_col, rows_xb, rows_gf, rows_cross, rows_gx,
    flat_dt, flat_raw, gwd, sr, dec, car, par, pq, arec, xs, xr, bs, ps, ys, dpar, coef, pair, zd, rd,
    us, ur, gs, gr, h1, a0, a1, a1r, a2, a2r, b0, b1, b1r, b2, b2r, c0, c1, c1r, c2, c2r, fin,
    *sems,
):
    here = place()
    x, z, h, yl, core = (here[a] for a in AXES)
    y = h * 2 + yl
    low = h == 0
    mine, other = h * HALF, (1 - h) * HALF
    partner = shifted(here, yh=1)
    cpeer = shifted(here, core=1)
    dpeers = [cpeer, shifted(here, yl=1), shifted(here, yl=1, core=1)]
    zpeers = [shifted(here, z=d) for d in range(1, NZ)]
    xpeers = [shifted(here, x=d) for d in range(1, NX)]
    ynext = [lax.rem(y + d, 4) for d in range(1, 4)]
    ypeers = [(x, z, t // 2, lax.rem(t, 2), core) for t in ynext]
    peers = [cpeer, dpeers[2]] + ypeers + zpeers + xpeers
    scan_sems, red_sems = sems[:16], sems[16:]
    y1s, y1r, as_, ar_, xss, xrs, bss, brs, y2s, y2r, d1s, d1r, d2s, d2r, d3s, d3r = scan_sems
    cs, cr, x0s, x0r, y0s, y0r, z0s, z0r, y3s, y3r, z1s, z1r, x1s, x1r, z2s, z2r, x2s, x2r, y4s, y4r, ls, lr, us_sem, ur_sem = red_sems
    barrier = pltpu.get_barrier_semaphore()
    for peer in peers:
        pl.semaphore_signal(barrier, inc=1, device_id=peer, device_id_type=MESH)

    u = u_ref[...]
    columns = jnp.concatenate([bias_ref[...], alog_ref[...], skip_ref[...], jnp.zeros((5, HEADS), F32)], axis=0)
    columns = jnp.concatenate([columns, jnp.zeros((8, TOK - HEADS), F32)], axis=1)
    columns = padded(columns).T[:HEADS]
    alog = columns[:, 1:2]
    raw = dot_nt(wd_ref[...], u) + columns[:, 0:1]
    small = jnp.exp(-jnp.abs(raw))
    above = 1.0 + small
    gap = above - 1.0
    log_part = jnp.where(gap == 0.0, small, jnp.log(above) * (small / jnp.where(gap == 0.0, 1.0, gap)))
    dt = jnp.maximum(raw, 0.0) + log_part
    rate = -jnp.exp(alog)
    row_i = lax.broadcasted_iota(jnp.int32, (TOK, TOK), 0)
    col_i = lax.broadcasted_iota(jnp.int32, (TOK, TOK), 1)
    upto = (row_i <= col_i).astype(F32)
    since = (row_i >= col_i).astype(F32)
    cum = jnp.dot(dt * rate, upto, precision=lax.Precision.HIGHEST, preferred_element_type=F32)
    last = cum[:, TOK - 1 :]
    to_end = jnp.exp(last - cum)
    from_start = jnp.exp(cum)
    flat_dt[...] = dt
    flat_raw[...] = raw

    def rows(v):
        return v.reshape(HEADS, 1, TOK)

    rows_dt[...] = rows(dt)
    rows_ws[...] = rows(to_end * dt)
    rows_fs[...] = rows(from_start)
    rows_te[...] = rows(to_end)
    rows_cum[...] = rows(cum)
    rows_skip[...] = rows(jnp.broadcast_to(columns[:, 2:3], (HEADS, TOK)))
    decay = jnp.broadcast_to(jnp.exp(last), (HEADS, STATE))
    fill = jnp.ones((4, STATE), F32)
    dec[0] = jnp.concatenate([decay[:HALF], fill], axis=0)
    dec[1] = jnp.concatenate([decay[HALF:], fill], axis=0)
    proj_b = dot(u, wb_ref[...])
    proj_c = dot(u, wc_ref[...])
    b4[...] = square(proj_b)
    c4[...] = square(proj_c)

    def states(start, c):
        count, block = SIZES_OF[c], SIZES_OF[c] * WIDTH
        at = pl.multiple_of((start + STARTS[c]) * WIDTH, 2 * WIDTH)
        heads = pl.ds(start + STARTS[c], count)
        rows_at = pl.ds(at, block)
        xc = x_ref[:, pl.ds(at, block)].T
        gc = g_ref[:, pl.ds(at, block)].T
        xt[rows_at, :] = xc
        gt[rows_at, :] = gc
        xsc = xc.astype(F32).reshape(count, WIDTH, TOK) * rows_ws[heads]
        gsc = gc.astype(F32).reshape(count, WIDTH, TOK) * rows_fs[heads]
        xwc = wide(xsc.reshape(block, TOK))
        gwc = wide(gsc.reshape(block, TOK))
        xw[rows_at, :] = xwc
        gw[rows_at, :] = gwc
        sr[0, heads] = fold(dot(xwc, b4[...])).reshape(count, WIDTH, STATE)
        sr[1, heads] = fold(dot(gwc, c4[...])).reshape(count, WIDTH, STATE)

    states(other, 0)
    pl.semaphore_wait(barrier, len(peers))
    first = push(dec.at[1 - h], dpar, d1s, d1r, partner)
    first.start()
    y1 = [
        push(
            sr.at[:, pl.ds(other + STARTS[c], SIZES_OF[c])],
            par.at[:, pl.ds(STARTS[c], SIZES_OF[c])],
            y1s.at[c], y1r.at[c], partner,
        )
        for c in range(CHUNKS)
    ]
    y1[0].start()
    us[...] = u.astype(F32)
    u_swap = push(us, ur, us_sem, ur_sem, cpeer)
    u_swap.start()
    states(other, 1)
    y1[1].start()
    xr[x] = jnp.zeros((HALF, PIECE, STATE), F32)
    first.wait()
    own_decay = dec[h]
    par_decay = dpar[...]
    one = jnp.ones_like(own_decay)
    coef[0] = jnp.where(low, par_decay, one)
    coef[1] = jnp.where(low, one, own_decay)
    coef[2] = jnp.where(low, one, par_decay)
    coef[3] = jnp.where(low, own_decay, one)
    pair[...] = own_decay * par_decay
    zd[z] = own_decay * par_decay
    second = [push(pair, zd.at[z], d2s.at[d], d2r.at[d], peer) for d, peer in enumerate(zpeers)]
    for copy in second:
        copy.start()
    states(mine, 0)
    for c in range(2, CHUNKS):
        states(other, c)
    bt4[...] = square(proj_b.T)
    ct4[...] = square(proj_c.T)
    scores[...] = jnp.where(row_i >= col_i, fold(dot(wide(proj_c), bt4[...])), 0.0)
    pairacc[...] = jnp.zeros((TOK, TOK), F32)
    rowacc[...] = jnp.zeros((TOK, TOK), F32)
    for copy in second:
        copy.wait()
    row = zd[0]
    for k in range(1, NZ):
        row = row * zd[k]
    rd[x] = row
    third = [push(rd.at[x], rd.at[x], d3s.at[d], d3r.at[d], peer) for d, peer in enumerate(xpeers)]
    for copy in third:
        copy.start()

    def a_copies(c):
        heads = pl.ds(STARTS[c], SIZES_OF[c])
        copies = []
        for d, peer in enumerate(zpeers):
            pz = pl.multiple_of(lax.rem(z + d + 1, NZ) * PIECE, PIECE)
            copies.append(
                push(pq.at[:, heads, pl.ds(pz, PIECE)], arec.at[z, :, heads], as_.at[c, d], ar_.at[c, d], peer)
            )
        return copies

    def x_copies(c):
        heads = pl.ds(STARTS[c], SIZES_OF[c])
        copies = []
        for d, peer in enumerate(xpeers):
            px = lax.rem(x + d + 1, NX)
            back = jnp.where(px > x, 0, 1)
            copies.append(push(xs.at[back, heads], xr.at[x, heads], xss.at[c, d], xrs.at[c, d], peer))
        return copies

    def b_copies(c):
        heads = pl.ds(STARTS[c], SIZES_OF[c])
        here_rows = pl.ds(pl.multiple_of(z * PIECE, PIECE), PIECE)
        copies = []
        for d, peer in enumerate(zpeers):
            pz = lax.rem(z + d + 1, NZ)
            copies.append(
                push(bs.at[pz, :, heads], ps.at[:, heads, here_rows], bss.at[c, d], brs.at[c, d], peer)
            )
        return copies

    def y2_copy(c):
        return push(
            ys.at[:, pl.ds(STARTS[c], SIZES_OF[c])],
            car.at[:, pl.ds(mine + STARTS[c], SIZES_OF[c])],
            y2s.at[c], y2r.at[c], partner,
        )

    def pairs(c):
        y1[c].wait_recv()
        if c + 2 < CHUNKS:
            y1[c + 2].start()

        def head(i, carry):
            k = STARTS[c] + i
            at = pl.ds(k, 1)
            pq[0, k] = coef[0, at, :] * sr[0, mine + k] + coef[1, at, :] * par[0, k]
            pq[1, k] = coef[2, at, :] * sr[1, mine + k] + coef[3, at, :] * par[1, k]
            return carry

        lax.fori_loop(0, SIZES_OF[c], head, 0)
        heads = pl.ds(STARTS[c], SIZES_OF[c])
        own = pl.ds(pl.multiple_of(z * PIECE, PIECE), PIECE)
        arec[z, :, heads] = pq[:, heads, own, :]
        copies = a_copies(c)
        for d in FAR_FIRST:
            copies[d - 1].start()

    def totals(c):
        for copy in a_copies(c):
            copy.wait_recv()

        def head(i, carry):
            k = STARTS[c] + i
            at = pl.ds(k, 1)
            forward = arec[0, 0, k]
            backward = arec[NZ - 1, 1, k]
            for j in range(1, NZ):
                forward = zd[j, at, :] * forward + arec[j, 0, k]
                backward = zd[NZ - 1 - j, at, :] * backward + arec[NZ - 1 - j, 1, k]
            xs[0, k] = forward
            xs[1, k] = backward
            return carry

        lax.fori_loop(0, SIZES_OF[c], head, 0)
        for copy in x_copies(c):
            copy.start()

    def prefixes(c):
        if c == 0:
            for copy in third:
                copy.wait()
        for copy in x_copies(c):
            copy.wait_recv()

        def head(i, carry):
            k = STARTS[c] + i
            at = pl.ds(k, 1)
            forward = jnp.zeros((PIECE, STATE), jnp.float32)
            backward = jnp.zeros((PIECE, STATE), jnp.float32)
            for j in range(NX):
                forward = jnp.where(j < x, rd[j, at, :] * forward + xr[j, k], forward)
                m = NX - 1 - j
                backward = jnp.where(m > x, rd[m, at, :] * backward + xr[m, k], backward)
            for j in range(NZ):
                bs[j, 0, k] = forward
                forward = zd[j, at, :] * forward + arec[j, 0, k]
                m = NZ - 1 - j
                bs[m, 1, k] = backward
                backward = zd[m, at, :] * backward + arec[m, 1, k]
            return carry

        lax.fori_loop(0, SIZES_OF[c], head, 0)
        heads = pl.ds(STARTS[c], SIZES_OF[c])
        own = pl.ds(pl.multiple_of(z * PIECE, PIECE), PIECE)
        ps[:, heads, own, :] = bs[z, :, heads]
        copies = b_copies(c)
        for d in FAR_FIRST:
            copies[d - 1].start()

    def finals(c):
        for copy in b_copies(c):
            copy.wait_recv()

        def head(i, carry):
            k = STARTS[c] + i
            at = pl.ds(k, 1)
            before, after = ps[0, k], ps[1, k]
            zero = jnp.zeros_like(before)
            ys[0, k] = coef[3, at, :] * before + jnp.where(low, sr[0, mine + k], zero)
            ys[1, k] = coef[1, at, :] * after + jnp.where(low, zero, sr[1, mine + k])
            car[0, mine + k] = coef[2, at, :] * before + jnp.where(low, zero, par[0, k])
            car[1, mine + k] = coef[0, at, :] * after + jnp.where(low, par[1, k], zero)
            return carry

        lax.fori_loop(0, SIZES_OF[c], head, 0)
        y2_copy(c).start()


    def within(start, count):
        def two(i, carry):
            for j in range(2):
                k = start + 2 * i + j
                at = pl.ds(pl.multiple_of(k * WIDTH, WIDTH), WIDTH)
                gk = gt[at, :]
                dots = dot_tn(gk, xt[at, :])
                across = jnp.broadcast_to(rows_cum[k], (TOK, TOK))
                table = jnp.exp(jnp.minimum(across.T - across, 0.0))
                weight = table * scores[...]
                inner[at, :] = fold(dot(gk, wide(weight)))
                terms = weight * dots
                rows_col[k] = jnp.sum(terms, axis=0, keepdims=True)
                pairacc[...] += table * dots * rows_dt[k]
                sums = jnp.sum(terms * rows_dt[k], axis=1, keepdims=True)
                rowacc[...] = jnp.where(col_i == k, sums, rowacc[...])
            return carry

        lax.fori_loop(0, count // 2, two, 0)

    gbacc[...] = jnp.zeros((2 * TOK, 2 * TOK), F32)
    gcacc[...] = jnp.zeros((2 * TOK, 2 * TOK), F32)

    def outputs(start, c):
        count, block = SIZES_OF[c], SIZES_OF[c] * WIDTH
        at = pl.multiple_of((start + STARTS[c]) * WIDTH, 2 * WIDTH)
        heads = pl.ds(start + STARTS[c], count)
        rows_at = pl.ds(at, block)
        ci = car[0, heads]
        co = car[1, heads]
        rows_cross[heads] = jnp.sum(ci * co, axis=1, keepdims=True)
        ciw = wide(ci.reshape(block, STATE))
        cow = wide(co.reshape(block, STATE))
        back = fold(dot(cow, bt4[...])).reshape(count, WIDTH, TOK)
        front = fold(dot(ciw, ct4[...])).reshape(count, WIDTH, TOK)
        gbacc[...] += dot_tn(xw[rows_at, :], cow)
        gcacc[...] += dot_tn(gw[rows_at, :], ciw)
        xf = xt[rows_at, :].astype(F32).reshape(count, WIDTH, TOK)
        gf = gt[rows_at, :].astype(F32).reshape(count, WIDTH, TOK)
        rows_xb[heads] = jnp.sum(xf * back, axis=1, keepdims=True)
        rows_gf[heads] = jnp.sum(gf * front, axis=1, keepdims=True)
        rows_gx[heads] = jnp.sum(gf * xf, axis=1, keepdims=True)
        total = inner[rows_at, :].reshape(count, WIDTH, TOK) + rows_te[heads] * back
        gx = rows_dt[heads] * total + rows_skip[heads] * gf
        gx_ref[:, pl.ds(at, block)] = gx.reshape(block, TOK).T.astype(BF16)

    work = [(other, 4)] + [(mine + n, 4) for n in range(0, HALF, 4)] + [(other + n, 4) for n in range(4, HALF, 4)]

    def fill(n):
        for _ in range(min(n, len(work))):
            within(*work.pop(0))

    fill(1)
    for c in range(1, CHUNKS):
        states(mine, c)
    fill(1)
    for step in range(CHUNKS + 3):
        if step < CHUNKS:
            pairs(step)
        if 0 <= step - 1 < CHUNKS:
            totals(step - 1)
        if 0 <= step - 2 < CHUNKS:
            prefixes(step - 2)
        if 0 <= step - 3 < CHUNKS:
            finals(step - 3)
        fill(1 if step != 2 else 2)
        if step >= 3:
            outputs(mine, step - 3)
        if step == 5:
            u_swap.wait()
            for j in range(0, MODEL, 512):
                ut[j : j + 512, :TOK] = u_ref[:, j : j + 512].T
                ut[j : j + 512, TOK:] = ur[:, j : j + 512].astype(BF16).T
    sums = pairacc[...]
    sumw = wide(jnp.where(row_i >= col_i, sums, 0.0))
    gbacc[...] += dot_tn(sumw, wide(dot(u_ref[...], wc_ref[...])))
    scores[...] = fold(dot(sumw, b4[...]))
    rowacc[...] = rowacc[...].T
    for c in range(CHUNKS):
        y2_copy(c).wait_recv()
        outputs(other, c)

    acc = gbacc[...]
    acc = acc[:TOK] + acc[TOK:]
    grad_b = fold(acc)
    acc = gcacc[...]
    acc = acc[:TOK] + acc[TOK:]
    grad_c = fold(acc) + scores[...]

    def flat(ref):
        return ref[...].reshape(HEADS, TOK)

    dt = flat_dt[...]
    raw = flat_raw[...]
    end = flat(rows_te)
    rate = -jnp.exp(alog)
    col = flat(rows_col)
    xb = end * flat(rows_xb)
    direct = col + xb
    own_out = dt * xb
    own_in = flat(rows_fs) * flat(rows_gf)
    cross = flat(rows_fs)[:, TOK - 1 :] * jnp.sum(flat(rows_cross), axis=1, keepdims=True)
    change = rowacc[0:HEADS, :] - dt * col + own_in - own_out
    lanes = lax.broadcasted_iota(jnp.int32, (HEADS, TOK), 1)
    edge = cross + jnp.sum(own_out, axis=1, keepdims=True)
    change = change + jnp.where(lanes == TOK - 1, edge, 0.0)
    grad_log = jnp.dot(change, since, precision=lax.Precision.HIGHEST, preferred_element_type=F32)
    grad_raw = (direct + grad_log * rate) * (1.0 / (1.0 + jnp.exp(-raw)))
    grad_bias = jnp.sum(grad_raw, axis=1, keepdims=True)
    grad_alog = jnp.sum(grad_log * dt, axis=1, keepdims=True) * rate
    grad_skip = jnp.sum(flat(rows_gx), axis=1, keepdims=True)
    extra = jnp.where(lanes == 0, grad_bias, jnp.where(lanes == 1, grad_alog, jnp.where(lanes == 2, grad_skip, 0.0)))
    extra = padded(extra).T[:8]
    grad_d = padded(grad_raw).T
    gs[0:128, :] = jnp.where(core == 0, grad_c, grad_b)
    gs[128:256, :] = grad_d
    gs[256:264, :] = extra
    cols_swap = push(gs, gr, cs, cr, cpeer)
    cols_swap.start()
    bt, ctall, dtall = tall(grad_b), tall(grad_c), tall(grad_d)[:, :HEADS]
    both_t = jnp.concatenate([bt, ctall], axis=1)

    def model_grads(i, carry):
        at = pl.ds(pl.multiple_of(i * 512, 512), 512)
        both_w = jnp.concatenate([wb_ref[at, :], wc_ref[at, :]], axis=1)
        p = dot_nt(both_t, both_w) + dot(dtall, wd_ref[:, at])
        gu_ref[:, at] = (p[:TOK] + p[TOK:]).astype(BF16)
        return carry

    lax.fori_loop(0, 2, model_grads, 0)
    cols_swap.wait()
    both_extra = extra + gr[256:264, :]
    main_w = wide(jnp.concatenate([jnp.where(core == 0, grad_b, grad_c), gr[0:128, :]], axis=0))
    steps_w = wide(jnp.concatenate([grad_d, gr[128:256, :]], axis=0))

    znext = [lax.rem(z + d, NZ) for d in range(1, NZ)]

    def z_firsts(i):
        copies = [
            push(h1.at[i, n, :, pl.ds(32, 16)], c0.at[z, i], z0s.at[i, d], z0r.at[i, d], zpeers[d])
            for d, n in enumerate(znext)
        ]
        return [copies[d - 1] for d in FAR_FIRST]

    def weights(i, carry):
        cols = ut[pl.ds(pl.multiple_of(i * 640, 640), 640), :]
        h1[i, :, :, 0:40, :] = fold(dot(cols, main_w)).reshape(NZ, 2, 40, 128)
        gwd[...] = fold(dot(cols, steps_w))
        for s in range(16):
            first_part = gwd[pl.ds(pl.multiple_of(s * 40 + 8 * core, 8), 8), :]
            next_part = gwd[pl.ds(pl.multiple_of(s * 40 + 16 + 8 * core, 8), 8), :]
            third_part = jnp.where(core == 0, gwd[s * 40 + 32 : s * 40 + 40, :], both_extra)
            packed = first_part + pltpu.roll(next_part, 40, 1)
            h1[i, s // 2, s % 2, 40:48, :] = packed + pltpu.roll(third_part, 80, 1)
        for copy in z_firsts(i):
            copy.start()
        return carry

    lax.fori_loop(0, NX, weights, 0)
    out = fin
    def part(start, there):
        return pl.ds(pl.multiple_of(start + 8 * lax.rem(there, 2), 8), 8)

    def begin(copies):
        for copy in copies:
            copy.start()
        return copies

    def arrived(copies):
        for copy in copies:
            copy.wait_recv()

    xnext = [lax.rem(x + d, NX) for d in range(1, NX)]
    z_one = [copy for i in range(NX) for copy in z_firsts(i)]
    x_one = begin([push(h1.at[t, :, :, pl.ds(0, 16)], a0.at[x], x0s.at[d], x0r.at[d], xpeers[d]) for d, t in enumerate(xnext)])
    y_one = begin([push(h1.at[:, :, t // 2, part(16, t)], b0.at[y], y0s.at[d], y0r.at[d], ypeers[d]) for d, t in enumerate(ynext)])
    lax.fori_loop(2, 5, model_grads, 0)
    arrived(x_one)
    total = h1[x, :, :, pl.ds(0, 16), :]
    for t in xnext:
        total = total + a0[t]
    a1[...] = total
    y_two = begin([push(a1.at[:, t // 2, part(0, t)], a1r.at[y], y3s.at[d], y3r.at[d], ypeers[d]) for d, t in enumerate(ynext)])
    arrived(y_one)
    total = h1[:, :, h, part(16, yl), :]
    for t in ynext:
        total = total + b0[t]
    b1[...] = total
    z_two = begin([push(b1.at[:, t], b1r.at[z], z1s.at[d], z1r.at[d], zpeers[d]) for d, t in enumerate(znext)])
    arrived(z_one)
    total = h1[:, z, :, pl.ds(32, 16), :]
    for t in znext:
        total = total + c0[t]
    c1[...] = total
    x_two = begin([push(c1.at[t], c1r.at[x], x1s.at[d], x1r.at[d], xpeers[d]) for d, t in enumerate(xnext)])
    arrived(y_two)
    total = a1[:, h, part(0, yl), :]
    for t in ynext:
        total = total + a1r[t]
    a2[...] = total
    z_three = begin([push(a2.at[t], a2r.at[z], z2s.at[d], z2r.at[d], zpeers[d]) for d, t in enumerate(znext)])
    arrived(z_two)
    total = b1[:, z]
    for t in znext:
        total = total + b1r[t]
    b2[...] = total
    x_three = begin([push(b2.at[t], b2r.at[x], x2s.at[d], x2r.at[d], xpeers[d]) for d, t in enumerate(xnext)])
    arrived(x_two)
    total = c1[x]
    for t in xnext:
        total = total + c1r[t]
    c2[...] = total
    y_three = begin([push(c2.at[t // 2, part(0, t)], c2r.at[y], y4s.at[d], y4r.at[d], ypeers[d]) for d, t in enumerate(ynext)])
    arrived(z_three)
    total = a2[z]
    for t in znext:
        total = total + a2r[t]
    out[core, 0, yl] = total
    arrived(x_three)
    total = b2[x]
    for t in xnext:
        total = total + b2r[t]
    out[core, 1, yl] = total
    arrived(y_three)
    total = c2[h, part(0, yl), :]
    for t in ynext:
        total = total + c2r[t]
    out[core, 2, yl] = total
    last = begin([push(out.at[core, :, yl], out.at[core, :, yl], ls.at[d], lr.at[d], peer) for d, peer in enumerate(dpeers)])
    for copy in last:
        copy.wait()

    whole = fin[...].reshape(2, 48, 128)
    gbw_ref[...] = whole[0, :40]
    gcw_ref[...] = whole[1, :40]
    tail = jnp.concatenate([whole[0, 40:], whole[1, 40:]], axis=0)
    gdw_ref[0:16, :] = tail[:, :HEADS]
    gdw_ref[16:32, :] = tail[:, 40:80]
    tail = tail[:, 80:120]
    gdw_ref[32:40, :] = tail[:8]
    ex_ref[...] = tail[8:]
    for c in range(CHUNKS):
        y1[c].wait_send()
        for copy in a_copies(c) + x_copies(c) + b_copies(c):
            copy.wait_send()
        y2_copy(c).wait_send()
    for copy in x_one + y_one + z_one + x_two + y_two + z_two + x_three + y_three + z_three:
        copy.wait_send()


def layer(u, x, g, wb, wc, wd, bias, alog, skip):
    vmem = pl.BlockSpec(memory_space=pltpu.VMEM)
    dma = pltpu.SemaphoreType.DMA
    half = (2, HALF, WIDTH, STATE)

    def f32(*shape):
        return pltpu.VMEM(shape + (128,), F32)

    def b16(*shape):
        return pltpu.VMEM(shape, BF16)

    def sems(counts):
        pairs = []
        for n in counts:
            pairs += [dma if n == () else dma(n)] * 2
        return pairs

    shape = jax.ShapeDtypeStruct
    return pl.pallas_call(
        layer_kernel,
        out_shape=(
            shape((TOK, MODEL), BF16), shape((TOK, MODEL), BF16), shape((40, STATE), F32),
            shape((40, STATE), F32), shape((40, HEADS), F32), shape((8, HEADS), F32),
        ),
        in_specs=[vmem] * 9,
        out_specs=(vmem,) * 6,
        scratch_shapes=[
            b16(MODEL, TOK), b16(MODEL, TOK), b16(MODEL, 256), b16(MODEL, 256), b16(MODEL, 256),
            b16(256, 256), b16(256, 256), b16(256, 256), b16(256, 256),
            f32(TOK), f32(TOK), f32(TOK), f32(MODEL), pltpu.VMEM((256, 256), F32), pltpu.VMEM((256, 256), F32),
        ] + [f32(HEADS, 1)] * 11 + [
            f32(HEADS), f32(HEADS), f32(640),
            f32(2, HEADS, WIDTH), f32(2, 24), f32(2, HEADS, WIDTH),
            f32(*half[:3]), f32(*half[:3]),
            f32(NZ, 2, HALF, PIECE), f32(2, HALF, PIECE), f32(NX, HALF, PIECE), f32(NZ, 2, HALF, PIECE),
            f32(*half[:3]), f32(*half[:3]),
            f32(24), f32(4, 24), f32(24), f32(NZ, 24), f32(NX, 24),
            pltpu.VMEM((TOK, MODEL), F32), pltpu.VMEM((TOK, MODEL), F32), f32(264), f32(264), f32(4, 8, 2, 48),
            f32(4, 8, 2, 16), f32(8, 2, 16), f32(4, 8, 8), f32(8, 8), f32(8, 8),
            f32(4, 4, 8, 8), f32(4, 8, 8), f32(8, 4, 8), f32(4, 8), f32(4, 8),
            f32(8, 4, 2, 16), f32(4, 2, 16), f32(4, 2, 16), f32(2, 16), f32(4, 8),
            f32(2, 3, 2, 8),
        ] + sems(
            [(CHUNKS,), (CHUNKS, NZ - 1), (CHUNKS, NX - 1), (CHUNKS, NZ - 1), (CHUNKS,), (), (NZ - 1,), (NX - 1,)]
        ) + sems([(), (3,), (3,), (NX, 7), (3,), (7,), (3,), (7,), (3,), (3,), (3,), ()]),
        compiler_params=pltpu.CompilerParams(
            collective_id=0, has_side_effects=True, vmem_limit_bytes=60 << 20
        ),
        name="layer",
    )(u, x, g, wb, wc, wd, bias, alog, skip)


def body(layer_input, ssm_input, out_grad, b_weight, c_weight, dt_weight, dt_bias, a_log, d_skip):
    gx, gu, gb, gc, gd, extra = layer(
        layer_input, ssm_input, out_grad, b_weight, c_weight, dt_weight.T,
        dt_bias[None], a_log[None], d_skip[None],
    )
    return gx, gu, gb, gc, gd, extra[0], extra[1], extra[2]


def solution(mesh):
    split_mesh = Mesh(mesh.devices.reshape(4, 8, 2, 2, 2), AXES)
    cut, whole = P(DP_SEQ, None), P()
    return jax.shard_map(
        body,
        mesh=split_mesh,
        in_specs=(cut, cut, cut) + (whole,) * 6,
        out_specs=(cut, cut) + (P(SEQ, None),) * 3 + (whole,) * 3,
        check_vma=False,
    )
```

```python
import jax
import jax.numpy as jnp
from jax import lax
from jax.experimental import pallas as pl
from jax.experimental.pallas import tpu as pltpu
from jax.sharding import Mesh
from jax.sharding import PartitionSpec as P

SEQ = ("x", "z", "yh")
DP_SEQ = ("yl", "core", "x", "z", "yh")
AXES = ("x", "z", "yh", "yl", "core")
SIZES = {"x": 4, "z": 8, "yh": 2, "yl": 2, "core": 2}
MESH = pl.DeviceIdType.MESH
HEADS, WIDTH, STATE = 40, 64, 128
HALF = HEADS // 2
SIZES_OF = (2, 4, 4, 4, 4, 2)
STARTS = tuple(sum(SIZES_OF[:c]) for c in range(len(SIZES_OF)))
CHUNKS = len(SIZES_OF)
NX, NZ = SIZES["x"], SIZES["z"]
PIECE = WIDTH // NZ
FAR_FIRST = (4, 3, 5, 2, 6, 1, 7)


def place():
    return {axis: lax.axis_index(axis) for axis in AXES}


def shifted(here, **steps):
    there = dict(here)
    for axis, step in steps.items():
        there[axis] = lax.rem(here[axis] + step, SIZES[axis])
    return tuple(there[axis] for axis in AXES)


def greet(peers):
    barrier = pltpu.get_barrier_semaphore()
    for peer in peers:
        pl.semaphore_signal(barrier, inc=1, device_id=peer, device_id_type=MESH)
    pl.semaphore_wait(barrier, len(peers))


def push(src, dst, send, recv, peer):
    return pltpu.make_async_remote_copy(
        src_ref=src, dst_ref=dst, send_sem=send, recv_sem=recv, device_id=peer, device_id_type=MESH
    )


TOK = 128
MODEL = 2560
F32, BF16 = jnp.float32, jnp.bfloat16


def dot(a, b):
    return jnp.dot(a, b, preferred_element_type=F32)


def dot_tn(a, b):
    return lax.dot_general(a, b, (((0,), (0,)), ((), ())), preferred_element_type=F32)


def dot_nt(a, b):
    return lax.dot_general(a, b, (((1,), (1,)), ((), ())), preferred_element_type=F32)


def split(v):
    top = v.astype(BF16)
    return top, (v - top.astype(F32)).astype(BF16)


def wide(v):
    return jnp.concatenate(split(v), axis=1)


def tall(v):
    return jnp.concatenate(split(v), axis=0)


def square(v):
    w = wide(v)
    return jnp.concatenate([w, w], axis=0)


def fold(p):
    return p[:, :128] + p[:, 128:]


def padded(v):
    return jnp.concatenate([v, jnp.zeros((TOK - v.shape[0], TOK), F32)], axis=0)


def layer_kernel(
    u_ref, x_ref, g_ref, wb_ref, wc_ref, wd_ref, bias_ref, alog_ref, skip_ref,
    gx_ref, gu_ref, gbw_ref, gcw_ref, gdw_ref, ex_ref,
    xt, gt, ut, xw, gw, b4, c4, bt4, ct4, scores, pairacc, rowacc, inner, gbacc, gcacc,
    rows_dt, rows_ws, rows_fs, rows_te, rows_cum, rows_skip, rows_col, rows_xb, rows_gf, rows_cross, rows_gx,
    flat_dt, flat_raw, gwd, sr, dec, car, par, pq, arec, xs, xr, bs, ps, ys, dpar, coef, pair, zd, rd,
    us, ur, gs, gr, h1, a0, a1, a1r, a2, a2r, b0, b1, b1r, b2, b2r, c0, c1, c1r, c2, c2r, fin,
    *sems,
):
    here = place()
    x, z, h, yl, core = (here[a] for a in AXES)
    y = h * 2 + yl
    low = h == 0
    mine, other = h * HALF, (1 - h) * HALF
    partner = shifted(here, yh=1)
    cpeer = shifted(here, core=1)
    dpeers = [cpeer, shifted(here, yl=1), shifted(here, yl=1, core=1)]
    zpeers = [shifted(here, z=d) for d in range(1, NZ)]
    xpeers = [shifted(here, x=d) for d in range(1, NX)]
    ynext = [lax.rem(y + d, 4) for d in range(1, 4)]
    ypeers = [(x, z, t // 2, lax.rem(t, 2), core) for t in ynext]
    peers = [cpeer, dpeers[2]] + ypeers + zpeers + xpeers
    scan_sems, red_sems = sems[:16], sems[16:]
    y1s, y1r, as_, ar_, xss, xrs, bss, brs, y2s, y2r, d1s, d1r, d2s, d2r, d3s, d3r = scan_sems
    cs, cr, x0s, x0r, y0s, y0r, z0s, z0r, y3s, y3r, z1s, z1r, x1s, x1r, z2s, z2r, x2s, x2r, y4s, y4r, ls, lr, us_sem, ur_sem = red_sems
    barrier = pltpu.get_barrier_semaphore()
    for peer in peers:
        pl.semaphore_signal(barrier, inc=1, device_id=peer, device_id_type=MESH)

    u = u_ref[...]
    columns = jnp.concatenate([bias_ref[...], alog_ref[...], skip_ref[...], jnp.zeros((5, HEADS), F32)], axis=0)
    columns = jnp.concatenate([columns, jnp.zeros((8, TOK - HEADS), F32)], axis=1)
    columns = padded(columns).T[:HEADS]
    alog = columns[:, 1:2]
    raw = dot_nt(wd_ref[...], u) + columns[:, 0:1]
    small = jnp.exp(-jnp.abs(raw))
    above = 1.0 + small
    gap = above - 1.0
    log_part = jnp.where(gap == 0.0, small, jnp.log(above) * (small / jnp.where(gap == 0.0, 1.0, gap)))
    dt = jnp.maximum(raw, 0.0) + log_part
    rate = -jnp.exp(alog)
    row_i = lax.broadcasted_iota(jnp.int32, (TOK, TOK), 0)
    col_i = lax.broadcasted_iota(jnp.int32, (TOK, TOK), 1)
    upto = (row_i <= col_i).astype(F32)
    since = (row_i >= col_i).astype(F32)
    cum = jnp.dot(dt * rate, upto, precision=lax.Precision.HIGHEST, preferred_element_type=F32)
    last = cum[:, TOK - 1 :]
    to_end = jnp.exp(last - cum)
    from_start = jnp.exp(cum)
    flat_dt[...] = dt
    flat_raw[...] = raw

    def rows(v):
        return v.reshape(HEADS, 1, TOK)

    rows_dt[...] = rows(dt)
    rows_ws[...] = rows(to_end * dt)
    rows_fs[...] = rows(from_start)
    rows_te[...] = rows(to_end)
    rows_cum[...] = rows(cum)
    rows_skip[...] = rows(jnp.broadcast_to(columns[:, 2:3], (HEADS, TOK)))
    decay = jnp.broadcast_to(jnp.exp(last), (HEADS, STATE))
    fill = jnp.ones((4, STATE), F32)
    dec[0] = jnp.concatenate([decay[:HALF], fill], axis=0)
    dec[1] = jnp.concatenate([decay[HALF:], fill], axis=0)
    proj_b = dot(u, wb_ref[...])
    proj_c = dot(u, wc_ref[...])
    b4[...] = square(proj_b)
    c4[...] = square(proj_c)

    def states(start, c):
        count, block = SIZES_OF[c], SIZES_OF[c] * WIDTH
        at = pl.multiple_of((start + STARTS[c]) * WIDTH, 2 * WIDTH)
        heads = pl.ds(start + STARTS[c], count)
        rows_at = pl.ds(at, block)
        xc = x_ref[:, pl.ds(at, block)].T
        gc = g_ref[:, pl.ds(at, block)].T
        xt[rows_at, :] = xc
        gt[rows_at, :] = gc
        xsc = xc.astype(F32).reshape(count, WIDTH, TOK) * rows_ws[heads]
        gsc = gc.astype(F32).reshape(count, WIDTH, TOK) * rows_fs[heads]
        xwc = wide(xsc.reshape(block, TOK))
        gwc = wide(gsc.reshape(block, TOK))
        xw[rows_at, :] = xwc
        gw[rows_at, :] = gwc
        sr[0, heads] = fold(dot(xwc, b4[...])).reshape(count, WIDTH, STATE)
        sr[1, heads] = fold(dot(gwc, c4[...])).reshape(count, WIDTH, STATE)

    states(other, 0)
    pl.semaphore_wait(barrier, len(peers))
    first = push(dec.at[1 - h], dpar, d1s, d1r, partner)
    first.start()
    y1 = [
        push(
            sr.at[:, pl.ds(other + STARTS[c], SIZES_OF[c])],
            par.at[:, pl.ds(STARTS[c], SIZES_OF[c])],
            y1s.at[c], y1r.at[c], partner,
        )
        for c in range(CHUNKS)
    ]
    y1[0].start()
    us[...] = u.astype(F32)
    u_swap = push(us, ur, us_sem, ur_sem, cpeer)
    u_swap.start()
    states(other, 1)
    y1[1].start()
    xr[x] = jnp.zeros((HALF, PIECE, STATE), F32)
    first.wait()
    own_decay = dec[h]
    par_decay = dpar[...]
    one = jnp.ones_like(own_decay)
    coef[0] = jnp.where(low, par_decay, one)
    coef[1] = jnp.where(low, one, own_decay)
    coef[2] = jnp.where(low, one, par_decay)
    coef[3] = jnp.where(low, own_decay, one)
    pair[...] = own_decay * par_decay
    zd[z] = own_decay * par_decay
    second = [push(pair, zd.at[z], d2s.at[d], d2r.at[d], peer) for d, peer in enumerate(zpeers)]
    for copy in second:
        copy.start()
    states(mine, 0)
    for c in range(2, CHUNKS):
        states(other, c)
    bt4[...] = square(proj_b.T)
    ct4[...] = square(proj_c.T)
    scores[...] = jnp.where(row_i >= col_i, fold(dot(wide(proj_c), bt4[...])), 0.0)
    pairacc[...] = jnp.zeros((TOK, TOK), F32)
    rowacc[...] = jnp.zeros((TOK, TOK), F32)
    for copy in second:
        copy.wait()
    row = zd[0]
    for k in range(1, NZ):
        row = row * zd[k]
    rd[x] = row
    third = [push(rd.at[x], rd.at[x], d3s.at[d], d3r.at[d], peer) for d, peer in enumerate(xpeers)]
    for copy in third:
        copy.start()

    def a_copies(c):
        heads = pl.ds(STARTS[c], SIZES_OF[c])
        copies = []
        for d, peer in enumerate(zpeers):
            pz = pl.multiple_of(lax.rem(z + d + 1, NZ) * PIECE, PIECE)
            copies.append(
                push(pq.at[:, heads, pl.ds(pz, PIECE)], arec.at[z, :, heads], as_.at[c, d], ar_.at[c, d], peer)
            )
        return copies

    def x_copies(c):
        heads = pl.ds(STARTS[c], SIZES_OF[c])
        copies = []
        for d, peer in enumerate(xpeers):
            px = lax.rem(x + d + 1, NX)
            back = jnp.where(px > x, 0, 1)
            copies.append(push(xs.at[back, heads], xr.at[x, heads], xss.at[c, d], xrs.at[c, d], peer))
        return copies

    def b_copies(c):
        heads = pl.ds(STARTS[c], SIZES_OF[c])
        here_rows = pl.ds(pl.multiple_of(z * PIECE, PIECE), PIECE)
        copies = []
        for d, peer in enumerate(zpeers):
            pz = lax.rem(z + d + 1, NZ)
            copies.append(
                push(bs.at[pz, :, heads], ps.at[:, heads, here_rows], bss.at[c, d], brs.at[c, d], peer)
            )
        return copies

    def y2_copy(c):
        return push(
            ys.at[:, pl.ds(STARTS[c], SIZES_OF[c])],
            car.at[:, pl.ds(mine + STARTS[c], SIZES_OF[c])],
            y2s.at[c], y2r.at[c], partner,
        )

    def pairs(c):
        y1[c].wait_recv()
        if c + 2 < CHUNKS:
            y1[c + 2].start()

        def head(i, carry):
            k = STARTS[c] + i
            at = pl.ds(k, 1)
            pq[0, k] = coef[0, at, :] * sr[0, mine + k] + coef[1, at, :] * par[0, k]
            pq[1, k] = coef[2, at, :] * sr[1, mine + k] + coef[3, at, :] * par[1, k]
            return carry

        lax.fori_loop(0, SIZES_OF[c], head, 0)
        heads = pl.ds(STARTS[c], SIZES_OF[c])
        own = pl.ds(pl.multiple_of(z * PIECE, PIECE), PIECE)
        arec[z, :, heads] = pq[:, heads, own, :]
        copies = a_copies(c)
        for d in FAR_FIRST:
            copies[d - 1].start()

    def totals(c):
        for copy in a_copies(c):
            copy.wait_recv()

        def head(i, carry):
            k = STARTS[c] + i
            at = pl.ds(k, 1)
            forward = arec[0, 0, k]
            backward = arec[NZ - 1, 1, k]
            for j in range(1, NZ):
                forward = zd[j, at, :] * forward + arec[j, 0, k]
                backward = zd[NZ - 1 - j, at, :] * backward + arec[NZ - 1 - j, 1, k]
            xs[0, k] = forward
            xs[1, k] = backward
            return carry

        lax.fori_loop(0, SIZES_OF[c], head, 0)
        for copy in x_copies(c):
            copy.start()

    def prefixes(c):
        if c == 0:
            for copy in third:
                copy.wait()
        for copy in x_copies(c):
            copy.wait_recv()

        def head(i, carry):
            k = STARTS[c] + i
            at = pl.ds(k, 1)
            forward = jnp.zeros((PIECE, STATE), jnp.float32)
            backward = jnp.zeros((PIECE, STATE), jnp.float32)
            for j in range(NX):
                forward = jnp.where(j < x, rd[j, at, :] * forward + xr[j, k], forward)
                m = NX - 1 - j
                backward = jnp.where(m > x, rd[m, at, :] * backward + xr[m, k], backward)
            for j in range(NZ):
                bs[j, 0, k] = forward
                forward = zd[j, at, :] * forward + arec[j, 0, k]
                m = NZ - 1 - j
                bs[m, 1, k] = backward
                backward = zd[m, at, :] * backward + arec[m, 1, k]
            return carry

        lax.fori_loop(0, SIZES_OF[c], head, 0)
        heads = pl.ds(STARTS[c], SIZES_OF[c])
        own = pl.ds(pl.multiple_of(z * PIECE, PIECE), PIECE)
        ps[:, heads, own, :] = bs[z, :, heads]
        copies = b_copies(c)
        for d in FAR_FIRST:
            copies[d - 1].start()

    def finals(c):
        for copy in b_copies(c):
            copy.wait_recv()

        def head(i, carry):
            k = STARTS[c] + i
            at = pl.ds(k, 1)
            before, after = ps[0, k], ps[1, k]
            zero = jnp.zeros_like(before)
            ys[0, k] = coef[3, at, :] * before + jnp.where(low, sr[0, mine + k], zero)
            ys[1, k] = coef[1, at, :] * after + jnp.where(low, zero, sr[1, mine + k])
            car[0, mine + k] = coef[2, at, :] * before + jnp.where(low, zero, par[0, k])
            car[1, mine + k] = coef[0, at, :] * after + jnp.where(low, par[1, k], zero)
            return carry

        lax.fori_loop(0, SIZES_OF[c], head, 0)
        y2_copy(c).start()


    def within(start, count):
        def two(i, carry):
            for j in range(2):
                k = start + 2 * i + j
                at = pl.ds(pl.multiple_of(k * WIDTH, WIDTH), WIDTH)
                gk = gt[at, :]
                dots = dot_tn(gk, xt[at, :])
                across = jnp.broadcast_to(rows_cum[k], (TOK, TOK))
                table = jnp.exp(jnp.minimum(across.T - across, 0.0))
                weight = table * scores[...]
                inner[at, :] = fold(dot(gk, wide(weight)))
                terms = weight * dots
                rows_col[k] = jnp.sum(terms, axis=0, keepdims=True)
                pairacc[...] += table * dots * rows_dt[k]
                sums = jnp.sum(terms * rows_dt[k], axis=1, keepdims=True)
                rowacc[...] = jnp.where(col_i == k, sums, rowacc[...])
            return carry

        lax.fori_loop(0, count // 2, two, 0)

    gbacc[...] = jnp.zeros((2 * TOK, 2 * TOK), F32)
    gcacc[...] = jnp.zeros((2 * TOK, 2 * TOK), F32)

    def outputs(start, c):
        count, block = SIZES_OF[c], SIZES_OF[c] * WIDTH
        at = pl.multiple_of((start + STARTS[c]) * WIDTH, 2 * WIDTH)
        heads = pl.ds(start + STARTS[c], count)
        rows_at = pl.ds(at, block)
        ci = car[0, heads]
        co = car[1, heads]
        rows_cross[heads] = jnp.sum(ci * co, axis=1, keepdims=True)
        ciw = wide(ci.reshape(block, STATE))
        cow = wide(co.reshape(block, STATE))
        back = fold(dot(cow, bt4[...])).reshape(count, WIDTH, TOK)
        front = fold(dot(ciw, ct4[...])).reshape(count, WIDTH, TOK)
        gbacc[...] += dot_tn(xw[rows_at, :], cow)
        gcacc[...] += dot_tn(gw[rows_at, :], ciw)
        xf = xt[rows_at, :].astype(F32).reshape(count, WIDTH, TOK)
        gf = gt[rows_at, :].astype(F32).reshape(count, WIDTH, TOK)
        rows_xb[heads] = jnp.sum(xf * back, axis=1, keepdims=True)
        rows_gf[heads] = jnp.sum(gf * front, axis=1, keepdims=True)
        rows_gx[heads] = jnp.sum(gf * xf, axis=1, keepdims=True)
        total = inner[rows_at, :].reshape(count, WIDTH, TOK) + rows_te[heads] * back
        gx = rows_dt[heads] * total + rows_skip[heads] * gf
        gx_ref[:, pl.ds(at, block)] = gx.reshape(block, TOK).T.astype(BF16)

    work = [(other, 4)] + [(mine + n, 4) for n in range(0, HALF, 4)] + [(other + n, 4) for n in range(4, HALF, 4)]

    def fill(n):
        for _ in range(min(n, len(work))):
            within(*work.pop(0))

    fill(1)
    for c in range(1, CHUNKS):
        states(mine, c)
    fill(1)
    for step in range(CHUNKS + 3):
        if step < CHUNKS:
            pairs(step)
        if 0 <= step - 1 < CHUNKS:
            totals(step - 1)
        if 0 <= step - 2 < CHUNKS:
            prefixes(step - 2)
        if 0 <= step - 3 < CHUNKS:
            finals(step - 3)
        fill(1 if step != 2 else 2)
        if step >= 3:
            outputs(mine, step - 3)
        if step == 5:
            u_swap.wait()
            for j in range(0, MODEL, 512):
                ut[j : j + 512, :TOK] = u_ref[:, j : j + 512].T
                ut[j : j + 512, TOK:] = ur[:, j : j + 512].astype(BF16).T
    sums = pairacc[...]
    sumw = wide(jnp.where(row_i >= col_i, sums, 0.0))
    gbacc[...] += dot_tn(sumw, wide(dot(u_ref[...], wc_ref[...])))
    scores[...] = fold(dot(sumw, b4[...]))
    rowacc[...] = rowacc[...].T
    for c in range(CHUNKS):
        y2_copy(c).wait_recv()
        outputs(other, c)

    acc = gbacc[...]
    acc = acc[:TOK] + acc[TOK:]
    grad_b = fold(acc)
    acc = gcacc[...]
    acc = acc[:TOK] + acc[TOK:]
    grad_c = fold(acc) + scores[...]

    def flat(ref):
        return ref[...].reshape(HEADS, TOK)

    dt = flat_dt[...]
    raw = flat_raw[...]
    end = flat(rows_te)
    rate = -jnp.exp(alog)
    col = flat(rows_col)
    xb = end * flat(rows_xb)
    direct = col + xb
    own_out = dt * xb
    own_in = flat(rows_fs) * flat(rows_gf)
    cross = flat(rows_fs)[:, TOK - 1 :] * jnp.sum(flat(rows_cross), axis=1, keepdims=True)
    change = rowacc[0:HEADS, :] - dt * col + own_in - own_out
    lanes = lax.broadcasted_iota(jnp.int32, (HEADS, TOK), 1)
    edge = cross + jnp.sum(own_out, axis=1, keepdims=True)
    change = change + jnp.where(lanes == TOK - 1, edge, 0.0)
    grad_log = jnp.dot(change, since, precision=lax.Precision.HIGHEST, preferred_element_type=F32)
    grad_raw = (direct + grad_log * rate) * (1.0 / (1.0 + jnp.exp(-raw)))
    grad_bias = jnp.sum(grad_raw, axis=1, keepdims=True)
    grad_alog = jnp.sum(grad_log * dt, axis=1, keepdims=True) * rate
    grad_skip = jnp.sum(flat(rows_gx), axis=1, keepdims=True)
    extra = jnp.where(lanes == 0, grad_bias, jnp.where(lanes == 1, grad_alog, jnp.where(lanes == 2, grad_skip, 0.0)))
    extra = padded(extra).T[:8]
    grad_d = padded(grad_raw).T
    gs[0:128, :] = jnp.where(core == 0, grad_c, grad_b)
    gs[128:256, :] = grad_d
    gs[256:264, :] = extra
    cols_swap = push(gs, gr, cs, cr, cpeer)
    cols_swap.start()
    bt, ctall, dtall = tall(grad_b), tall(grad_c), tall(grad_d)[:, :HEADS]
    both_t = jnp.concatenate([bt, ctall], axis=1)

    def model_grads(i, carry):
        at = pl.ds(pl.multiple_of(i * 512, 512), 512)
        both_w = jnp.concatenate([wb_ref[at, :], wc_ref[at, :]], axis=1)
        p = dot_nt(both_t, both_w) + dot(dtall, wd_ref[:, at])
        gu_ref[:, at] = (p[:TOK] + p[TOK:]).astype(BF16)
        return carry

    lax.fori_loop(0, 2, model_grads, 0)
    cols_swap.wait()
    both_extra = extra + gr[256:264, :]
    main_w = wide(jnp.concatenate([jnp.where(core == 0, grad_b, grad_c), gr[0:128, :]], axis=0))
    steps_w = wide(jnp.concatenate([grad_d, gr[128:256, :]], axis=0))

    znext = [lax.rem(z + d, NZ) for d in range(1, NZ)]

    def z_firsts(i):
        copies = [
            push(h1.at[i, n, :, pl.ds(32, 16)], c0.at[z, i], z0s.at[i, d], z0r.at[i, d], zpeers[d])
            for d, n in enumerate(znext)
        ]
        return [copies[d - 1] for d in FAR_FIRST]

    def y_firsts(i):
        return [
            push(
                h1.at[i, :, n // 2, pl.ds(pl.multiple_of(16 + 8 * lax.rem(n, 2), 8), 8)], b0.at[y, i],
                y0s.at[i, d], y0r.at[i, d], ypeers[d],
            )
            for d, n in enumerate(ynext)
        ]

    def weights(i, carry):
        cols = ut[pl.ds(pl.multiple_of(i * 640, 640), 640), :]
        h1[i, :, :, 0:40, :] = fold(dot(cols, main_w)).reshape(NZ, 2, 40, 128)
        gwd[...] = fold(dot(cols, steps_w))
        for s in range(16):
            first_part = gwd[pl.ds(pl.multiple_of(s * 40 + 8 * core, 8), 8), :]
            next_part = gwd[pl.ds(pl.multiple_of(s * 40 + 16 + 8 * core, 8), 8), :]
            third_part = jnp.where(core == 0, gwd[s * 40 + 32 : s * 40 + 40, :], both_extra)
            packed = first_part + pltpu.roll(next_part, 40, 1)
            h1[i, s // 2, s % 2, 40:48, :] = packed + pltpu.roll(third_part, 80, 1)
        for copy in z_firsts(i) + y_firsts(i):
            copy.start()
        return carry

    lax.fori_loop(0, NX, weights, 0)
    out = fin
    def part(start, there):
        return pl.ds(pl.multiple_of(start + 8 * lax.rem(there, 2), 8), 8)

    def begin(copies):
        for copy in copies:
            copy.start()
        return copies

    def arrived(copies):
        for copy in copies:
            copy.wait_recv()

    xnext = [lax.rem(x + d, NX) for d in range(1, NX)]
    z_one = [copy for i in range(NX) for copy in z_firsts(i)]
    x_one = begin([push(h1.at[t, :, :, pl.ds(0, 16)], a0.at[x], x0s.at[d], x0r.at[d], xpeers[d]) for d, t in enumerate(xnext)])
    y_one = [copy for i in range(NX) for copy in y_firsts(i)]
    lax.fori_loop(2, 5, model_grads, 0)
    arrived(x_one)
    total = h1[x, :, :, pl.ds(0, 16), :]
    for t in xnext:
        total = total + a0[t]
    a1[...] = total
    y_two = begin([push(a1.at[:, t // 2, part(0, t)], a1r.at[y], y3s.at[d], y3r.at[d], ypeers[d]) for d, t in enumerate(ynext)])
    arrived(y_one)
    total = h1[:, :, h, part(16, yl), :]
    for t in ynext:
        total = total + b0[t]
    b1[...] = total
    z_two = begin([push(b1.at[:, t], b1r.at[z], z1s.at[d], z1r.at[d], zpeers[d]) for d, t in enumerate(znext)])
    arrived(z_one)
    total = h1[:, z, :, pl.ds(32, 16), :]
    for t in znext:
        total = total + c0[t]
    c1[...] = total
    x_two = begin([push(c1.at[t], c1r.at[x], x1s.at[d], x1r.at[d], xpeers[d]) for d, t in enumerate(xnext)])
    arrived(y_two)
    total = a1[:, h, part(0, yl), :]
    for t in ynext:
        total = total + a1r[t]
    a2[...] = total
    z_three = begin([push(a2.at[t], a2r.at[z], z2s.at[d], z2r.at[d], zpeers[d]) for d, t in enumerate(znext)])
    arrived(z_two)
    total = b1[:, z]
    for t in znext:
        total = total + b1r[t]
    b2[...] = total
    x_three = begin([push(b2.at[t], b2r.at[x], x2s.at[d], x2r.at[d], xpeers[d]) for d, t in enumerate(xnext)])
    arrived(x_two)
    total = c1[x]
    for t in xnext:
        total = total + c1r[t]
    c2[...] = total
    y_three = begin([push(c2.at[t // 2, part(0, t)], c2r.at[y], y4s.at[d], y4r.at[d], ypeers[d]) for d, t in enumerate(ynext)])
    arrived(z_three)
    total = a2[z]
    for t in znext:
        total = total + a2r[t]
    out[core, 0, yl] = total
    arrived(x_three)
    total = b2[x]
    for t in xnext:
        total = total + b2r[t]
    out[core, 1, yl] = total
    arrived(y_three)
    total = c2[h, part(0, yl), :]
    for t in ynext:
        total = total + c2r[t]
    out[core, 2, yl] = total
    last = begin([push(out.at[core, :, yl], out.at[core, :, yl], ls.at[d], lr.at[d], peer) for d, peer in enumerate(dpeers)])
    for copy in last:
        copy.wait()

    whole = fin[...].reshape(2, 48, 128)
    gbw_ref[...] = whole[0, :40]
    gcw_ref[...] = whole[1, :40]
    tail = jnp.concatenate([whole[0, 40:], whole[1, 40:]], axis=0)
    gdw_ref[0:16, :] = tail[:, :HEADS]
    gdw_ref[16:32, :] = tail[:, 40:80]
    tail = tail[:, 80:120]
    gdw_ref[32:40, :] = tail[:8]
    ex_ref[...] = tail[8:]
    for c in range(CHUNKS):
        y1[c].wait_send()
        for copy in a_copies(c) + x_copies(c) + b_copies(c):
            copy.wait_send()
        y2_copy(c).wait_send()
    for copy in x_one + y_one + z_one + x_two + y_two + z_two + x_three + y_three + z_three:
        copy.wait_send()


def layer(u, x, g, wb, wc, wd, bias, alog, skip):
    vmem = pl.BlockSpec(memory_space=pltpu.VMEM)
    dma = pltpu.SemaphoreType.DMA
    half = (2, HALF, WIDTH, STATE)

    def f32(*shape):
        return pltpu.VMEM(shape + (128,), F32)

    def b16(*shape):
        return pltpu.VMEM(shape, BF16)

    def sems(counts):
        pairs = []
        for n in counts:
            pairs += [dma if n == () else dma(n)] * 2
        return pairs

    shape = jax.ShapeDtypeStruct
    return pl.pallas_call(
        layer_kernel,
        out_shape=(
            shape((TOK, MODEL), BF16), shape((TOK, MODEL), BF16), shape((40, STATE), F32),
            shape((40, STATE), F32), shape((40, HEADS), F32), shape((8, HEADS), F32),
        ),
        in_specs=[vmem] * 9,
        out_specs=(vmem,) * 6,
        scratch_shapes=[
            b16(MODEL, TOK), b16(MODEL, TOK), b16(MODEL, 256), b16(MODEL, 256), b16(MODEL, 256),
            b16(256, 256), b16(256, 256), b16(256, 256), b16(256, 256),
            f32(TOK), f32(TOK), f32(TOK), f32(MODEL), pltpu.VMEM((256, 256), F32), pltpu.VMEM((256, 256), F32),
        ] + [f32(HEADS, 1)] * 11 + [
            f32(HEADS), f32(HEADS), f32(640),
            f32(2, HEADS, WIDTH), f32(2, 24), f32(2, HEADS, WIDTH),
            f32(*half[:3]), f32(*half[:3]),
            f32(NZ, 2, HALF, PIECE), f32(2, HALF, PIECE), f32(NX, HALF, PIECE), f32(NZ, 2, HALF, PIECE),
            f32(*half[:3]), f32(*half[:3]),
            f32(24), f32(4, 24), f32(24), f32(NZ, 24), f32(NX, 24),
            pltpu.VMEM((TOK, MODEL), F32), pltpu.VMEM((TOK, MODEL), F32), f32(264), f32(264), f32(4, 8, 2, 48),
            f32(4, 8, 2, 16), f32(8, 2, 16), f32(4, 8, 8), f32(8, 8), f32(8, 8),
            f32(4, 4, 8, 8), f32(4, 8, 8), f32(8, 4, 8), f32(4, 8), f32(4, 8),
            f32(8, 4, 2, 16), f32(4, 2, 16), f32(4, 2, 16), f32(2, 16), f32(4, 8),
            f32(2, 3, 2, 8),
        ] + sems(
            [(CHUNKS,), (CHUNKS, NZ - 1), (CHUNKS, NX - 1), (CHUNKS, NZ - 1), (CHUNKS,), (), (NZ - 1,), (NX - 1,)]
        ) + sems([(), (3,), (NX, 3), (NX, 7), (3,), (7,), (3,), (7,), (3,), (3,), (3,), ()]),
        compiler_params=pltpu.CompilerParams(
            collective_id=0, has_side_effects=True, vmem_limit_bytes=60 << 20
        ),
        name="layer",
    )(u, x, g, wb, wc, wd, bias, alog, skip)


def body(layer_input, ssm_input, out_grad, b_weight, c_weight, dt_weight, dt_bias, a_log, d_skip):
    gx, gu, gb, gc, gd, extra = layer(
        layer_input, ssm_input, out_grad, b_weight, c_weight, dt_weight.T,
        dt_bias[None], a_log[None], d_skip[None],
    )
    return gx, gu, gb, gc, gd, extra[0], extra[1], extra[2]


def solution(mesh):
    split_mesh = Mesh(mesh.devices.reshape(4, 8, 2, 2, 2), AXES)
    cut, whole = P(DP_SEQ, None), P()
    return jax.shard_map(
        body,
        mesh=split_mesh,
        in_specs=(cut, cut, cut) + (whole,) * 6,
        out_specs=(cut, cut) + (P(SEQ, None),) * 3 + (whole,) * 3,
        check_vma=False,
    )
```
